32 devices in a mesh: dp: 8 (over z, x), tensor: 4 (over y, core).
Axes of the slice: x: 2, y: 2, z: 4, core: 2. Of those that a mesh axis runs over, the one named last changes fastest.
Arguments:
- hidden_in: bfloat16 [16384, 768], P('dp'), may hold values from -6 to 6
- doc_ids: int32 [16384], P('dp'), may hold values from 0 to 7, as said below
- ln1_gain: float32 [768], replicated, may hold values from 0.5 to 1.5
- ln1_bias: float32 [768], replicated, may hold values from -1.25 to 1.25
- w_qkv: bfloat16 [768, 3, 12, 64], P(None, None, 'tensor'), may hold values from -0.3125 to 0.3125
- b_qv: float32 [2, 12, 64], P(None, 'tensor'), may hold values from -1.75 to 1.75
- w_out: bfloat16 [12, 64, 768], P('tensor'), may hold values from -0.875 to 0.875
- b_out: float32 [768], replicated, may hold values from -1.25 to 1.25
- ln2_gain: float32 [768], replicated, may hold values from 0.5 to 1.5
- ln2_bias: float32 [768], replicated, may hold values from -1.25 to 1.25
- w_fc: bfloat16 [768, 3072], P(None, 'tensor'), may hold values from -0.21875 to 0.21875
- b_fc: float32 [24, 128], P('tensor'), may hold values from -1.75 to 1.75
- w_proj: bfloat16 [3072, 768], P('tensor'), may hold values from -0.109375 to 0.109375
- b_proj: float32 [768], replicated, may hold values from -1.25 to 1.25
- grad_out: bfloat16 [16384, 768], P('dp'), may hold values from -6 to 6
Outputs:
- block_out: bfloat16 [16384, 768], P('dp')
- grad_in: float32 [16384, 768], P('dp')
- grad_ln1_gain: float32 [768], P('dp')
- grad_ln1_bias: float32 [768], P('dp')
- grad_w_qkv: float32 [768, 3, 12, 64], P('dp', None, 'tensor')
- grad_b_qv: float32 [2, 12, 64], P(None, 'tensor', 'dp')
- grad_w_out: float32 [12, 64, 768], P('tensor', None, 'dp')
- grad_b_out: float32 [768], P('dp')
- grad_ln2_gain: float32 [768], P('dp')
- grad_ln2_bias: float32 [768], P('dp')
- grad_w_fc: float32 [768, 3072], P('dp', 'tensor')
- grad_b_fc: float32 [24, 128], P('tensor', 'dp')
- grad_w_proj: float32 [3072, 768], P('tensor', 'dp')
- grad_b_proj: float32 [768], P('dp')
The draws below stay inside these ranges and needn't reach their ends.
Inputs may be any that keep to these rules, and one draw needn't show every extreme that they name: `doc_ids`: each aligned block of 2048 tokens (one index of dp) holds either 2048 // 1024 sequences of 1024 tokens or 8 sequences of 256 tokens, numbered from 0 in order; exactly half of the blocks hold the long ones.
All inputs are finite; a program needn't handle non-finite values.
Results may differ from the reference program's by a relative error of at most 0.015.
The reference program's roundings to bfloat16 on the way count: a program that leaves them out, or rounds other values in their place, can miss the bound.
Values may be sent and summed in bfloat16 or wider, within the bound.
No kernel may reach another device: no remote copies, remote signals or barrier semaphores. Data moves between devices by JAX's collectives and lax.ppermute only.
A program may use at most 192 MiB of HBM per device.

```python
import math
import jax
import jax.numpy as jnp
from jax import lax

HEADS = 12
HEAD_DIM = 64
FF = 3072
D = 768
ROWS = 2048
LONG_LEN = 1024
SHORT_LEN = 256
TOKENS = 16384
N_DP = 8


def draw_doc_ids(key, part):
    blocks = TOKENS // ROWS
    order = jax.random.permutation(key, blocks)
    long_block = order < blocks // 2
    positions = jnp.arange(ROWS, dtype=jnp.int32)
    long_ids = positions // LONG_LEN
    short_ids = positions // SHORT_LEN
    result = jnp.where(long_block[:, None], long_ids[None, :], short_ids[None, :])
    return result.reshape(-1).astype(jnp.int32)


def strengthened(entries, rng, source, target, shards_of, factor):
    owner, partner = [(jnp.arange(entries.shape[dim]) // (entries.shape[dim] // shards_of)).reshape([-1 if axis == dim else 1 for axis in range(entries.ndim)]) for dim in (source, target)]
    chosen = jax.random.permutation(rng, shards_of)[partner]
    strong = (owner == chosen) | (owner == (partner + shards_of // 2) % shards_of)
    return jnp.where(strong, factor * entries, entries)


def shard_levels(stream_key, extent, shards, least, high):
    level = 1.0
    for position, shards_of in shards:
        draws = jax.random.uniform(jax.random.fold_in(jax.random.fold_in(stream_key, 6), position), (shards_of,), jnp.float32, least / len(shards), high / len(shards))
        level = level * jnp.repeat(jnp.exp(draws), extent[position] // shards_of).reshape((-1,) + (1,) * (len(extent) - 1 - position))
    return level


def noise(rng, extent, spread, limit, shards=(), held_as=jnp.bfloat16):
    gain = shard_levels(rng, extent, shards, -0.22, 0.18) if shards else 1.0
    drawn = jax.random.normal(rng, extent, jnp.float32) * spread * gain
    return jnp.minimum(jnp.maximum(drawn, -limit), limit).astype(held_as)


def gaussian_with(rng, dims, spread, reach, shards, heavy, held_as=jnp.bfloat16):
    entries = spread * jax.random.normal(rng, dims, jnp.float32)
    if shards:
        entries = entries * shard_levels(rng, dims, shards, -0.22, 0.18)
    return jnp.clip(strengthened(entries, jax.random.fold_in(rng, 3), *heavy), -reach, reach).astype(held_as)


def setup_inputs(seed: int = 0) -> dict:
    keys = jax.random.split(jax.random.key(seed), 16)
    return {
        "hidden_in": noise(keys[0], (TOKENS, D), 1.0, 6.0, ((0, 8),)),
        "doc_ids": draw_doc_ids(jax.random.fold_in(keys[15], 71), 0),
        "ln1_gain": jnp.clip(1.0 + 0.1 * jax.random.normal(keys[2], (D,), jnp.float32), 0.5, 1.5),
        "ln1_bias": noise(keys[3], (D,), 0.2, 1.25, (), jnp.float32),
        "w_qkv": noise(keys[4], (D, 3, HEADS, HEAD_DIM), (D // 2) ** -0.5, 0.3125, ((2, 4),)),
        "b_qv": noise(keys[5], (2, HEADS, HEAD_DIM), 0.3, 1.75, ((1, 4),), jnp.float32),
        "w_out": noise(keys[6], (HEADS, HEAD_DIM, D), (D // 16) ** -0.5, 0.875, ((0, 4),)),
        "b_out": noise(keys[7], (D,), 0.2, 1.25, (), jnp.float32),
        "ln2_gain": jnp.clip(1.0 + 0.1 * jax.random.normal(keys[8], (D,), jnp.float32), 0.5, 1.5),
        "ln2_bias": noise(keys[9], (D,), 0.2, 1.25, (), jnp.float32),
        "w_fc": noise(keys[10], (D, FF), D ** -0.5, 0.21875, ((1, 4),)),
        "b_fc": noise(keys[11], (FF // 128, 128), 0.3, 1.75, ((0, 4),), jnp.float32),
        "w_proj": noise(keys[12], (FF, D), FF ** -0.5, 0.109375, ((0, 4),)),
        "b_proj": noise(keys[13], (D,), 0.2, 1.25, (), jnp.float32),
        "grad_out": gaussian_with(keys[14], (TOKENS, D), 1.0, 6.0, ((0, 8),), (0, 1, 8, 2.0)),
    }


@jax.custom_vjp
def low(v):
    return lax.optimization_barrier(v.astype(jnp.bfloat16)).astype(jnp.float32)

@jax.custom_vjp
def low_back(v):
    return v

def low_keep(v):
    return (low(v), None)

def low_pass(kept, grad):
    return (grad,)

def back_keep(v):
    return (v, None)

def back_low(kept, grad):
    return (low(grad),)
low.defvjp(low_keep, low_pass)
low_back.defvjp(back_keep, back_low)
EPSILON = 1e-05
MASKED = -1e+30

def matmul(left, right):
    return jnp.dot(left, right, precision=lax.Precision.HIGHEST)

def normalize(values):
    row_mean = lax.optimization_barrier(jnp.mean(values, axis=-1, keepdims=True))
    centered = values - row_mean
    return centered * lax.rsqrt(lax.optimization_barrier(jnp.mean(centered * centered, axis=-1, keepdims=True)) + EPSILON)

def attend(inputs):
    queries, key_rows, value_rows, seq_ids = inputs
    scale_factor = 1.0 / math.sqrt(HEAD_DIM)
    scores = jnp.einsum('qhd,khd->hqk', queries, key_rows, precision=lax.Precision.HIGHEST) * scale_factor
    scores = low_back(scores)
    positions = jnp.arange(queries.shape[0])
    allowed = (positions[:, None] >= positions[None, :]) & (seq_ids[:, None] == seq_ids[None, :])
    scores = jnp.where(allowed[None], scores, MASKED)
    row_max = lax.optimization_barrier(jnp.max(scores, axis=-1, keepdims=True))
    exp_scores = jnp.exp(scores - row_max)
    weights = low(exp_scores / lax.optimization_barrier(jnp.sum(exp_scores, axis=-1, keepdims=True)))
    return jnp.einsum('hqk,khd->qhd', weights, value_rows, precision=lax.Precision.HIGHEST)

def forward(x_float, ln1_gain, ln1_bias, w_qkv, b_qv, w_out, b_out, ln2_gain, ln2_bias, w_fc, b_fc, w_proj, b_proj, doc_ids):
    tokens = x_float.shape[0]
    first_in = low(normalize(x_float) * ln1_gain + ln1_bias)
    projected = matmul(first_in, w_qkv.reshape(D, 3 * D)).reshape(tokens, 3, HEADS, HEAD_DIM)
    queries = low(low_back(projected[:, 0] + b_qv[0]))
    key_rows = low(low_back(projected[:, 1]))
    value_rows = low(low_back(projected[:, 2] + b_qv[1]))
    block_shape = (N_DP, ROWS, HEADS, HEAD_DIM)
    attended = lax.map(jax.checkpoint(attend), (queries.reshape(block_shape), key_rows.reshape(block_shape), value_rows.reshape(block_shape), doc_ids.reshape(N_DP, ROWS)))
    attended = low(low_back(attended.reshape(tokens, D)))
    branch = low_back(matmul(attended, w_out.reshape(D, D)) + b_out)
    residual = x_float + branch
    second_in = low(normalize(residual) * ln2_gain + ln2_bias)
    pre_act = low_back(matmul(second_in, w_fc) + b_fc.reshape(FF))
    act_low = low(jax.nn.gelu(pre_act, approximate=True))
    return residual + matmul(act_low, w_proj) + b_proj

def reference(hidden_in, doc_ids, ln1_gain, ln1_bias, w_qkv, b_qv, w_out, b_out, ln2_gain, ln2_bias, w_fc, b_fc, w_proj, b_proj, grad_out):
    inputs_float = (hidden_in.astype(jnp.float32), ln1_gain, ln1_bias, w_qkv.astype(jnp.float32), b_qv, w_out.astype(jnp.float32), b_out, ln2_gain, ln2_bias, w_fc.astype(jnp.float32), b_fc, w_proj.astype(jnp.float32), b_proj)

    def closed(*inputs):
        return forward(*inputs, doc_ids)
    block_out, pullback = jax.vjp(closed, *inputs_float)
    gradients = pullback(grad_out.astype(jnp.float32))
    return (block_out.astype(jnp.bfloat16), gradients[0], gradients[1], gradients[2], gradients[3], gradients[4], gradients[5], gradients[6], gradients[7], gradients[8], gradients[9], gradients[10], gradients[11], gradients[12])
```

```python
import math

import jax
import jax.numpy as jnp
from jax import lax
from jax.experimental import pallas as pl
from jax.experimental.pallas import tpu as pltpu
from jax.sharding import PartitionSpec as P

EPSILON = 1e-05
MASKED = -1e30
QUERY_ROWS = 256
SHORT_LEN = 256
BF16 = jnp.bfloat16
F32 = jnp.float32
VMEM_BYTES = 60 * 1024 * 1024


def dot_nn(left, right):
    return lax.dot_general(left, right, (((1,), (0,)), ((), ())), preferred_element_type=F32)


def dot_nt(left, right):
    return lax.dot_general(left, right, (((1,), (1,)), ((), ())), preferred_element_type=F32)


def dot_tn(left, right):
    return lax.dot_general(left, right, (((0,), (0,)), ((), ())), preferred_element_type=F32)


def normalize(values):
    row_mean = jnp.mean(values, axis=-1, keepdims=True)
    centered = values - row_mean
    inv_std = lax.rsqrt(jnp.mean(centered * centered, axis=-1, keepdims=True) + EPSILON)
    return (centered * inv_std, inv_std)


def norm_back(grad_normed, normed, inv_std, gain_vec):
    scaled = grad_normed * gain_vec
    return inv_std * (
        scaled
        - jnp.mean(scaled, axis=-1, keepdims=True)
        - normed * jnp.mean(scaled * normed, axis=-1, keepdims=True)
    )


def head_lanes(values, head, head_dim):
    per_group = 128 // head_dim
    first = (head // per_group) * 128
    group = values[:, first : min(first + 128, values.shape[1])]
    if group.shape[1] == head_dim:
        return group
    lane = lax.broadcasted_iota(jnp.int32, group.shape, 1)
    inside = (lane // head_dim) == (head % per_group)
    return jnp.where(inside, group, jnp.zeros_like(group))


def group_lanes(head, head_dim, width):
    per_group = 128 // head_dim
    first = (head // per_group) * 128
    return slice(first, min(first + 128, width))


def allowed_diagonal():
    key_pos = lax.broadcasted_iota(jnp.int32, (QUERY_ROWS, QUERY_ROWS), 0)
    row_pos = lax.broadcasted_iota(jnp.int32, (QUERY_ROWS, QUERY_ROWS), 1)
    return key_pos <= row_pos


def attend_block(queries, keys_ref, values_t_ref, start, old_rows, heads, head_dim):
    width = heads * head_dim
    attended_t = []
    logs = []
    allowed = allowed_diagonal()
    for head in range(heads):
        query = head_lanes(queries, head, head_dim)
        lanes = group_lanes(head, head_dim, width)
        rows = slice(head * head_dim, (head + 1) * head_dim)
        here = pl.ds(start, QUERY_ROWS)
        near = jnp.where(allowed, dot_nt(keys_ref[here, lanes], query), MASKED)
        row_max = jnp.max(near, axis=0, keepdims=True)
        if old_rows:
            far = dot_nt(keys_ref[0:old_rows, lanes], query)
            row_max = jnp.maximum(row_max, jnp.max(far, axis=0, keepdims=True))
        near = jnp.exp(near - row_max)
        total = jnp.sum(near, axis=0, keepdims=True)
        if old_rows:
            far = jnp.exp(far - row_max)
            total = total + jnp.sum(far, axis=0, keepdims=True)
        inverse = 1.0 / total
        result = dot_nn(values_t_ref[rows, here], (near * inverse).astype(BF16))
        if old_rows:
            result = result + dot_nn(values_t_ref[rows, 0:old_rows], (far * inverse).astype(BF16))
        attended_t.append(result)
        logs.append(row_max + jnp.log(total))
    attended = jnp.concatenate(attended_t, axis=0).T
    return attended, logs


def attend_body(
    heads, head_dim, block, first_in, w_ref, bias_ref, qkv_ref, att_ref, log_ref, keys_ref,
    values_t_ref, is_long,
):
    width = heads * head_dim
    blocks = keys_ref.shape[0] // QUERY_ROWS
    projected = dot_nn(first_in, w_ref[...])
    queries = (projected[:, :width] + bias_ref[0:1, :]).astype(BF16)
    key_rows = projected[:, width : 2 * width].astype(BF16)
    value_rows = projected[:, 2 * width :] + bias_ref[1:2, :]
    qkv_ref[...] = jnp.concatenate([queries, key_rows, value_rows.astype(BF16)], axis=1)
    start = pl.multiple_of(block * QUERY_ROWS, QUERY_ROWS)
    keys_ref[pl.ds(start, QUERY_ROWS), :] = key_rows
    values_t_ref[:, pl.ds(start, QUERY_ROWS)] = value_rows.T.astype(BF16)
    scaled = queries * jnp.asarray(1.0 / math.sqrt(head_dim), BF16)

    def finish(attended, logs):
        att_ref[...] = attended.astype(BF16)
        log_ref[...] = jnp.concatenate(
            logs + [jnp.zeros((8 - heads, QUERY_ROWS), F32)], axis=0
        )

    @pl.when(jnp.logical_or(is_long == 0, block == 0))
    def _():
        finish(*attend_block(scaled, keys_ref, values_t_ref, start, 0, heads, head_dim))

    for position in range(1, blocks):

        @pl.when(jnp.logical_and(is_long == 1, block == position))
        def _(position=position):
            finish(
                *attend_block(
                    scaled,
                    keys_ref,
                    values_t_ref,
                    position * QUERY_ROWS,
                    position * QUERY_ROWS,
                    heads,
                    head_dim,
                )
            )


def forward_own_kernel(heads, head_dim, info_ref, x_ref, gain_ref, shift_ref, w_ref, bias_ref,
                       first_ref, qkv_ref, att_ref, log_ref, keys_ref, values_t_ref):
    normed, _ = normalize(x_ref[...].astype(F32))
    first_in = (normed * gain_ref[...] + shift_ref[...]).astype(BF16)
    first_ref[...] = first_in
    attend_body(heads, head_dim, pl.program_id(0), first_in, w_ref, bias_ref, qkv_ref, att_ref,
                log_ref, keys_ref, values_t_ref, info_ref[1])


def forward_other_kernel(heads, head_dim, info_ref, first_ref, w_ref, bias_ref, att_own_ref,
                         w_out_own_ref, w_out_ref, qkv_ref, att_ref, log_ref, branch_ref,
                         keys_ref, values_t_ref):
    attend_body(heads, head_dim, pl.program_id(0), first_ref[...], w_ref, bias_ref, qkv_ref,
                att_ref, log_ref, keys_ref, values_t_ref, info_ref[1])
    branch = dot_nn(att_own_ref[...], w_out_own_ref[...]) + dot_nn(att_ref[...], w_out_ref[...])
    branch_ref[...] = branch.astype(BF16)


def mlp_kernel(info_ref, x_ref, branch_a_ref, branch_b_ref, b_out_ref, gain_ref, shift_ref, go_ref,
               fc_own_ref, fc_other_ref, proj_own_ref, proj_other_ref, b_fc_ref,
               residual_ref, mlp_ref, grad_ref, d_fc_own_ref, d_fc_other_ref, d_proj_own_ref,
               d_proj_other_ref, d_b_fc_ref, d_b_proj_ref,
               in_t_ref, go_t_ref, pre_own_ref, pre_other_ref, act_own_ref, act_other_ref):
    step = pl.program_id(0)
    rows = x_ref.shape[0]
    residual = x_ref[...].astype(F32) + (
        branch_a_ref[...].astype(F32) + branch_b_ref[...].astype(F32) + b_out_ref[...]
    )
    residual_ref[...] = residual
    normed, _ = normalize(residual)
    second_in = (normed * gain_ref[...] + shift_ref[...]).astype(BF16)
    grad_out = go_ref[...]
    here = pl.ds(pl.multiple_of(step * rows, rows), rows)
    in_t_ref[:, here] = second_in.T
    go_t_ref[:, here] = grad_out.T

    @pl.when(step == 0)
    def _():
        d_b_fc_ref[...] = jnp.zeros_like(d_b_fc_ref)
        d_b_proj_ref[...] = jnp.zeros_like(d_b_proj_ref)

    d_b_proj_ref[...] += jnp.sum(grad_out.astype(F32), axis=0, keepdims=True)
    mlp = None
    grad_second = None
    parts = (
        (fc_own_ref, proj_own_ref, pre_own_ref, act_own_ref),
        (fc_other_ref, proj_other_ref, pre_other_ref, act_other_ref),
    )
    slope = math.sqrt(2.0 / math.pi)
    for part, (fc_ref, proj_ref, pre_ref, act_ref) in enumerate(parts):
        pre_act = dot_nn(second_in, fc_ref[...]) + b_fc_ref[part : part + 1, :]
        square = pre_act * pre_act
        bent = jnp.tanh(slope * (pre_act + 0.044715 * (pre_act * square)))
        half = 0.5 * (1.0 + bent)
        act_low = (pre_act * half).astype(BF16)
        act_ref[here, :] = act_low
        part_out = dot_nn(act_low, proj_ref[...])
        grad_act = dot_nt(grad_out, proj_ref[...])
        derivative = half + (0.5 * pre_act) * (1.0 - bent * bent) * (
            slope + (3.0 * 0.044715 * slope) * square
        )
        grad_pre = (grad_act * derivative).astype(BF16)
        pre_ref[here, :] = grad_pre
        d_b_fc_ref[part : part + 1, :] += jnp.sum(grad_pre.astype(F32), axis=0, keepdims=True)
        part_grad = dot_nt(grad_pre, fc_ref[...])
        mlp = part_out if mlp is None else mlp + part_out
        grad_second = part_grad if grad_second is None else grad_second + part_grad
    mlp_ref[...] = mlp.astype(BF16)
    grad_ref[...] = grad_second.astype(BF16)

    @pl.when(step == pl.num_programs(0) - 1)
    def _():
        d_fc_other_ref[...] = dot_nn(in_t_ref[...], pre_other_ref[...]).astype(BF16)
        d_proj_other_ref[...] = dot_nn(go_t_ref[...], act_other_ref[...]).astype(BF16)
        d_fc_own_ref[...] = dot_nn(in_t_ref[...], pre_own_ref[...])
        d_proj_own_ref[...] = dot_nn(go_t_ref[...], act_own_ref[...])


def attend_back_block(queries, grads, logs, keys_ref, keys_t_ref, values_ref, grad_keys_ref,
                      grad_values_ref, start, old_rows, heads, head_dim, scale):
    width = heads * head_dim
    allowed = allowed_diagonal()
    grad_queries_t = []
    new_keys = []
    new_values = []
    for head in range(heads):
        query = head_lanes(queries, head, head_dim)
        scaled = query * jnp.asarray(scale, BF16)
        grad = head_lanes(grads, head, head_dim)
        lanes = group_lanes(head, head_dim, width)
        rows = slice(head * head_dim, (head + 1) * head_dim)
        log_row = logs[head : head + 1, :]
        here = pl.ds(start, QUERY_ROWS)
        near = dot_nt(keys_ref[here, lanes], scaled)
        near = jnp.where(allowed, jnp.exp(near - log_row), 0.0)
        grad_near = dot_nt(values_ref[here, lanes], grad)
        delta = jnp.sum(near * grad_near, axis=0, keepdims=True)
        if old_rows:
            old = slice(0, old_rows)
            far = jnp.exp(dot_nt(keys_ref[old, lanes], scaled) - log_row)
            grad_far = dot_nt(values_ref[old, lanes], grad)
            delta = delta + jnp.sum(far * grad_far, axis=0, keepdims=True)
        scores_near = (near * (grad_near - delta)).astype(BF16)
        result = dot_nn(keys_t_ref[rows, here], scores_near)
        new_keys.append(dot_nn(scores_near, query))
        new_values.append(dot_nn(near.astype(BF16), grad))
        if old_rows:
            scores_far = (far * (grad_far - delta)).astype(BF16)
            result = result + dot_nn(keys_t_ref[rows, old], scores_far)
            grad_keys_ref[old, lanes] += dot_nn(scores_far, query)
            grad_values_ref[old, lanes] += dot_nn(far.astype(BF16), grad)
        grad_queries_t.append(result)
    for head in range(heads):
        lanes = group_lanes(head, head_dim, width)
        here = pl.ds(start, QUERY_ROWS)
        grad_keys_ref[here, lanes] += new_keys[head]
        grad_values_ref[here, lanes] += new_values[head]
    return jnp.concatenate(grad_queries_t, axis=0).T * scale


def backward_other_kernel(heads, head_dim, info_ref, grad_a_ref, grad_b_ref, residual_ref, go_ref,
                          gain_ref, first_ref, qkv_ref, att_ref, log_ref, w_ref, w_out_ref,
                          grad_residual_ref, grad_branch_ref, grad_first_ref, d_w_ref, d_bias_ref,
                          d_norm_ref, acc_ref, keys_t_ref, keys_ref, values_ref, grad_keys_ref,
                          grad_values_ref, grad_queries_ref):
    step = pl.program_id(0)
    grad_second = grad_a_ref[...].astype(F32) + grad_b_ref[...].astype(F32)
    normed, inv_std = normalize(residual_ref[...])
    grad_residual = go_ref[...].astype(F32) + norm_back(grad_second, normed, inv_std, gain_ref[...])
    grad_residual_ref[...] = grad_residual
    grad_branch = grad_residual.astype(BF16)
    grad_branch_ref[...] = grad_branch

    @pl.when(step == 0)
    def _():
        d_norm_ref[...] = jnp.zeros_like(d_norm_ref)

    d_norm_ref[0:1, :] += jnp.sum(grad_second * normed, axis=0, keepdims=True)
    d_norm_ref[1:2, :] += jnp.sum(grad_second, axis=0, keepdims=True)
    d_norm_ref[2:3, :] += jnp.sum(grad_branch.astype(F32), axis=0, keepdims=True)
    grad_first = attend_back(heads, head_dim, grad_branch, first_ref, qkv_ref, att_ref, log_ref,
                             w_ref, w_out_ref, d_w_ref, d_bias_ref, acc_ref, keys_t_ref, keys_ref,
                             values_ref, grad_keys_ref, grad_values_ref, grad_queries_ref,
                             info_ref[1])
    grad_first_ref[...] = grad_first


def backward_own_kernel(heads, head_dim, info_ref, grad_branch_ref, grad_first_in_ref, first_ref,
                        qkv_ref, att_ref, log_ref, w_ref, w_out_ref,
                        grad_first_ref, d_w_ref, d_bias_ref, acc_ref, keys_t_ref, keys_ref,
                        values_ref, grad_keys_ref, grad_values_ref, grad_queries_ref):
    grad_first = attend_back(heads, head_dim, grad_branch_ref[...], first_ref, qkv_ref, att_ref,
                             log_ref, w_ref, w_out_ref, d_w_ref, d_bias_ref, acc_ref, keys_t_ref,
                             keys_ref, values_ref, grad_keys_ref, grad_values_ref,
                             grad_queries_ref, info_ref[1])
    grad_first_ref[...] = (grad_first + grad_first_in_ref[...]).astype(BF16)


def attend_back(heads, head_dim, grad_branch, first_ref, qkv_ref, att_ref, log_ref, w_ref,
                w_out_ref, d_w_ref, d_bias_ref, acc_ref, keys_t_ref, keys_ref, values_ref,
                grad_keys_ref, grad_values_ref, grad_queries_ref, is_long):
    step = pl.program_id(0)
    steps = pl.num_programs(0)
    blocks = qkv_ref.shape[0] // QUERY_ROWS
    block = blocks - 1 - step
    width = heads * head_dim
    scale = 1.0 / math.sqrt(head_dim)

    @pl.when(step == 0)
    def _():
        key_rows = qkv_ref[:, width : 2 * width]
        keys_ref[...] = key_rows
        values_ref[...] = qkv_ref[:, 2 * width :]
        keys_t_ref[...] = key_rows.T
        grad_keys_ref[...] = jnp.zeros_like(grad_keys_ref)
        grad_values_ref[...] = jnp.zeros_like(grad_values_ref)
        d_bias_ref[...] = jnp.zeros_like(d_bias_ref)
        acc_ref[...] = jnp.zeros_like(acc_ref)

    start = pl.multiple_of(block * QUERY_ROWS, QUERY_ROWS)
    here = pl.ds(start, QUERY_ROWS)
    queries = qkv_ref[here, 0:width]
    logs = log_ref[...]
    grads = dot_nt(grad_branch, w_out_ref[...]).astype(BF16)

    def run(start_row, old_rows):
        grad_queries_ref[...] = attend_back_block(
            queries, grads, logs, keys_ref, keys_t_ref, values_ref, grad_keys_ref,
            grad_values_ref, start_row, old_rows, heads, head_dim, scale)

    @pl.when(jnp.logical_or(is_long == 0, block == 0))
    def _():
        run(start, 0)

    for position in range(1, blocks):

        @pl.when(jnp.logical_and(is_long == 1, block == position))
        def _(position=position):
            run(position * QUERY_ROWS, position * QUERY_ROWS)

    mixed = jnp.concatenate(
        [grad_queries_ref[...], grad_keys_ref[here, :] * scale, grad_values_ref[here, :]], axis=1
    ).astype(BF16)
    d_bias_ref[...] += jnp.sum(mixed.astype(F32), axis=0, keepdims=True)
    acc_ref[:, 0 : 3 * width] += dot_tn(first_ref[...], mixed)
    acc_ref[:, 3 * width :] += dot_tn(grad_branch, att_ref[...])

    @pl.when(step == steps - 1)
    def _():
        d_w_ref[...] = acc_ref[...].astype(d_w_ref.dtype)

    return dot_nt(mixed, w_ref[...])


def last_norm_kernel(info_ref, x_ref, grad_a_ref, grad_b_ref, grad_residual_ref, gain_ref,
                     grad_in_ref, d_norm_ref):
    @pl.when(pl.program_id(0) == 0)
    def _():
        d_norm_ref[...] = jnp.zeros_like(d_norm_ref)

    grad_first = grad_a_ref[...].astype(F32) + grad_b_ref[...].astype(F32)
    normed, inv_std = normalize(x_ref[...].astype(F32))
    grad_in = grad_residual_ref[...] + norm_back(grad_first, normed, inv_std, gain_ref[...])
    grad_in_ref[...] = grad_in.astype(BF16)
    d_norm_ref[0:1, :] += jnp.sum(grad_first * normed, axis=0, keepdims=True)
    d_norm_ref[1:2, :] += jnp.sum(grad_first, axis=0, keepdims=True)


def row_spec(rows, width, shift=False):
    if shift:
        return pl.BlockSpec((rows, width), lambda step, info: (info[0] + step, 0))
    return pl.BlockSpec((rows, width), lambda step, info: (step, 0))


def back_spec(rows, width, blocks, shift=False):
    if shift:
        return pl.BlockSpec((rows, width), lambda step, info: (info[0] + blocks - 1 - step, 0))
    return pl.BlockSpec((rows, width), lambda step, info: (blocks - 1 - step, 0))


def whole(shape):
    return pl.BlockSpec(shape, lambda step, info: (0,) * len(shape))


def call(kernel, steps, in_specs, out_specs, out_shape, scratch, name):
    return pl.pallas_call(
        kernel,
        grid_spec=pltpu.PrefetchScalarGridSpec(
            num_scalar_prefetch=1,
            grid=(steps,),
            in_specs=in_specs,
            out_specs=out_specs,
            scratch_shapes=scratch,
        ),
        out_shape=out_shape,
        compiler_params=pltpu.CompilerParams(
            dimension_semantics=("arbitrary",), vmem_limit_bytes=VMEM_BYTES
        ),
        name=name,
    )


def struct(shape, dtype):
    return jax.ShapeDtypeStruct(shape, dtype)


def exchange(value, axis_name, size, bit):
    return lax.ppermute(value, axis_name, [(i, i ^ bit) for i in range(size)])


def after(value, earlier):
    return lax.optimization_barrier((value, earlier))[0]


def make_body(dp_size, tensor_size):
    def body(hidden_in, doc_ids, ln1_gain, ln1_bias, w_qkv, b_qv, w_out, b_out, ln2_gain, ln2_bias,
             w_fc, b_fc, w_proj, b_proj, grad_out):
        row_count, width = hidden_in.shape
        heads, head_dim = w_qkv.shape[2:]
        local = heads * head_dim
        hidden = w_fc.shape[1]
        rows = row_count // 2
        blocks = rows // QUERY_ROWS
        half = rows // 2
        place = lax.axis_index("tensor")
        upper = place // 2
        core = place % 2
        is_long = (doc_ids[SHORT_LEN] == doc_ids[0]).astype(jnp.int32)
        info = jnp.stack([upper * blocks, is_long]).astype(jnp.int32)

        def core_swap(value):
            return exchange(value, "tensor", tensor_size, 1)

        def pair_swap(value):
            return exchange(value, "tensor", tensor_size, 2)

        qkv_own = w_qkv.reshape(width, 3 * local)
        out_own = w_out.reshape(local, width)
        bias_own = b_qv.reshape(2, local)
        qkv_other = pair_swap(qkv_own)
        out_other = pair_swap(after(out_own, qkv_other))
        small_other = pair_swap(
            jnp.concatenate([b_qv.reshape(1, 2 * local), b_fc.reshape(1, hidden)], axis=1)
        )
        fc_other = pair_swap(after(w_fc, out_other))
        proj_other = pair_swap(after(w_proj, fc_other))
        bias_other = small_other[:, : 2 * local].reshape(2, local)
        b_fc_both = jnp.concatenate([b_fc.reshape(1, hidden), small_other[:, 2 * local :]], axis=0)

        def as_row(vector):
            return vector.reshape(1, width)

        first_spec = row_spec(QUERY_ROWS, width)
        qkv_spec = row_spec(QUERY_ROWS, 3 * local)
        att_spec = row_spec(QUERY_ROWS, local)
        log_spec = pl.BlockSpec((8, QUERY_ROWS), lambda step, info: (0, step))
        attend_scratch = [pltpu.VMEM((rows, local), BF16), pltpu.VMEM((local, rows), BF16)]

        def forward_own(*refs):
            forward_own_kernel(heads, head_dim, *refs)

        def forward_other(*refs):
            forward_other_kernel(heads, head_dim, *refs)

        first_in, mix_own, att_own, log_own = call(
            forward_own,
            blocks,
            [row_spec(QUERY_ROWS, width, True), whole((1, width)), whole((1, width)),
             whole((width, 3 * local)), whole((2, local))],
            [first_spec, qkv_spec, att_spec, log_spec],
            [struct((rows, width), BF16), struct((rows, 3 * local), BF16),
             struct((rows, local), BF16), struct((8, rows), F32)],
            attend_scratch,
            "forward_own",
        )(info, hidden_in, as_row(ln1_gain), as_row(ln1_bias), qkv_own, bias_own)
        mix_other, att_other, log_other, branch = call(
            forward_other,
            blocks,
            [first_spec, whole((width, 3 * local)), whole((2, local)), att_spec,
             whole((local, width)), whole((local, width))],
            [qkv_spec, att_spec, log_spec, first_spec],
            [struct((rows, 3 * local), BF16), struct((rows, local), BF16),
             struct((8, rows), F32), struct((rows, width), BF16)],
            attend_scratch,
            "forward_other",
        )(info, first_in, qkv_other, bias_other, att_own, out_own, out_other)
        branch_swapped = core_swap(branch)

        (residual, mlp, grad_second, d_fc_own, d_fc_other, d_proj_own, d_proj_other, d_b_fc,
         d_b_proj) = call(
            mlp_kernel,
            blocks,
            [row_spec(QUERY_ROWS, width, True), first_spec, first_spec, whole((1, width)),
             whole((1, width)), whole((1, width)), row_spec(QUERY_ROWS, width, True),
             whole((width, hidden)), whole((width, hidden)), whole((hidden, width)),
             whole((hidden, width)), whole((2, hidden))],
            [first_spec, first_spec, first_spec] + [whole((width, hidden))] * 4
            + [whole((2, hidden)), whole((1, width))],
            [struct((rows, width), F32), struct((rows, width), BF16), struct((rows, width), BF16),
             struct((width, hidden), F32), struct((width, hidden), BF16),
             struct((width, hidden), F32), struct((width, hidden), BF16),
             struct((2, hidden), F32), struct((1, width), F32)],
            [pltpu.VMEM((width, rows), BF16)] * 2 + [pltpu.VMEM((rows, hidden), BF16)] * 4,
            "mlp",
        )(info, hidden_in, branch, branch_swapped, as_row(b_out), as_row(ln2_gain),
          as_row(ln2_bias), grad_out, w_fc, fc_other, w_proj, proj_other, b_fc_both)
        grad_swapped = core_swap(grad_second)
        mlp_swapped = core_swap(mlp)

        back_rows = back_spec(QUERY_ROWS, width, blocks)
        back_att = back_spec(QUERY_ROWS, local, blocks)
        back_log = pl.BlockSpec((8, QUERY_ROWS), lambda step, info: (0, blocks - 1 - step))
        back_scratch = [
            pltpu.VMEM((width, 4 * local), F32),
            pltpu.VMEM((local, rows), BF16),
            pltpu.VMEM((rows, local), BF16),
            pltpu.VMEM((rows, local), BF16),
            pltpu.VMEM((rows, local), F32),
            pltpu.VMEM((rows, local), F32),
            pltpu.VMEM((QUERY_ROWS, local), F32),
        ]

        def backward_other(*refs):
            backward_other_kernel(heads, head_dim, *refs)

        def backward_own(*refs):
            backward_own_kernel(heads, head_dim, *refs)

        (grad_residual, grad_branch, grad_first_other, d_att_other, d_bias_other,
         d_norm_two) = call(
            backward_other,
            blocks,
            [back_rows, back_rows, back_rows, back_spec(QUERY_ROWS, width, blocks, True),
             whole((1, width)), back_rows, whole((rows, 3 * local)), back_att, back_log,
             whole((width, 3 * local)), whole((local, width))],
            [back_rows, back_rows, back_rows, whole((width, 4 * local)), whole((1, 3 * local)),
             whole((8, width))],
            [struct((rows, width), F32), struct((rows, width), BF16), struct((rows, width), F32),
             struct((width, 4 * local), BF16), struct((1, 3 * local), F32),
             struct((8, width), F32)],
            back_scratch,
            "backward_other",
        )(info, grad_second, grad_swapped, residual, grad_out, as_row(ln2_gain), first_in,
          mix_other, att_other, log_other, qkv_other, out_other)
        grad_first, d_att_own, d_bias_own = call(
            backward_own,
            blocks,
            [back_rows, back_rows, back_rows, whole((rows, 3 * local)), back_att, back_log,
             whole((width, 3 * local)), whole((local, width))],
            [back_rows, whole((width, 4 * local)), whole((1, 3 * local))],
            [struct((rows, width), BF16), struct((width, 4 * local), F32),
             struct((1, 3 * local), F32)],
            back_scratch,
            "backward_own",
        )(info, grad_branch, grad_first_other, first_in, mix_own, att_own, log_own, qkv_own,
          out_own)
        first_swapped = core_swap(grad_first)
        grad_in_low, d_norm_one = call(
            last_norm_kernel,
            blocks,
            [row_spec(QUERY_ROWS, width, True), first_spec, first_spec, first_spec,
             whole((1, width))],
            [first_spec, whole((8, width))],
            [struct((rows, width), BF16), struct((8, width), F32)],
            [],
            "last_norm",
        )(info, hidden_in, grad_first, first_swapped, grad_residual, as_row(ln1_gain))

        def spread(value):
            far = pair_swap(lax.dynamic_slice_in_dim(value, core * half, half, axis=0))
            farther = core_swap(far)
            low_half = jnp.where(core == 0, far, farther)
            high_half = jnp.where(core == 0, farther, far)
            there = jnp.concatenate([low_half, high_half], axis=0)
            return jnp.concatenate(
                [jnp.where(upper == 0, value, there), jnp.where(upper == 0, there, value)], axis=0
            )

        block_own = (
            residual + (mlp.astype(F32) + mlp_swapped.astype(F32)) + b_proj
        ).astype(BF16)
        block_out = spread(block_own)
        grad_in = spread(grad_in_low).astype(F32)

        bits = dp_size.bit_length() - 1
        position = lax.axis_index("dp")

        def reduce_share(own, other):
            share = width // dp_size
            columns = own.shape[1]
            received = pair_swap(other)
            parts = [own.reshape((dp_size, share, columns)),
                     received.reshape((dp_size, share, columns))]
            for bit in range(bits):
                mine = (position >> bit) & 1
                count = dp_size >> (bit + 1)

                def pick(which):
                    total = None
                    for part in parts:
                        view = part.reshape(count, 2, share, columns)
                        piece = lax.dynamic_index_in_dim(view, which, 1, keepdims=False)
                        piece = piece.astype(F32)
                        total = piece if total is None else total + piece
                    return total

                sent = pick(1 - mine).astype(BF16)
                parts = [pick(mine), exchange(sent, "dp", dp_size, 1 << bit)]
            return (parts[0].astype(F32) + parts[1].astype(F32)).reshape(share, columns)

        fc_share = reduce_share(d_fc_own, d_fc_other)
        proj_share = reduce_share(d_proj_own, d_proj_other)
        att_share = reduce_share(d_att_own, d_att_other)

        def wide(d_bias):
            row = jnp.concatenate([d_bias[:, :local], d_bias[:, 2 * local :]], axis=1)
            return jnp.pad(row, ((0, 0), (0, width - 2 * local)))

        common = [d_b_proj, d_norm_two[0:3], d_norm_one[0:2]]
        small = jnp.concatenate(common + [d_b_fc[0:1], wide(d_bias_own)], axis=0)
        small_sent = jnp.concatenate(common + [d_b_fc[1:2], wide(d_bias_other)], axis=0)
        small = small + pair_swap(small_sent)
        for bit in range(bits):
            small = small + exchange(small, "dp", dp_size, 1 << bit)
        share = width // dp_size
        shares = lax.dynamic_index_in_dim(
            small[0:6].reshape(6, dp_size, share), position, 1, keepdims=False
        )
        d_b_proj_share, d_gain_two, d_shift_two, d_b_out, d_gain_one, d_shift_one = (
            shares[i] for i in range(6)
        )
        fc_rows, fc_columns = b_fc.shape
        d_b_fc_share = lax.dynamic_slice_in_dim(
            small[6].reshape(fc_rows, fc_columns), position * (fc_columns // dp_size),
            fc_columns // dp_size, axis=1,
        )
        d_b_qv_share = lax.dynamic_slice_in_dim(
            small[7, : 2 * local].reshape(2, heads, head_dim), position * (head_dim // dp_size),
            head_dim // dp_size, axis=2,
        )
        d_w_qkv = att_share[:, : 3 * local].reshape(share, 3, heads, head_dim)
        d_w_out = att_share[:, 3 * local :].T.reshape(heads, head_dim, share)
        return (block_out, grad_in, d_gain_one, d_shift_one, d_w_qkv, d_b_qv_share, d_w_out,
                d_b_out, d_gain_two, d_shift_two, fc_share, d_b_fc_share, proj_share.T,
                d_b_proj_share)

    return body


def solution(mesh):
    in_specs = (
        P("dp", None),
        P("dp"),
        P(),
        P(),
        P(None, None, "tensor", None),
        P(None, "tensor", None),
        P("tensor", None, None),
        P(),
        P(),
        P(),
        P(None, "tensor"),
        P("tensor", None),
        P("tensor", None),
        P(),
        P("dp", None),
    )
    out_specs = (
        P("dp", None),
        P("dp", None),
        P("dp"),
        P("dp"),
        P("dp", None, "tensor", None),
        P(None, "tensor", "dp"),
        P("tensor", None, "dp"),
        P("dp"),
        P("dp"),
        P("dp"),
        P("dp", "tensor"),
        P("tensor", "dp"),
        P("tensor", "dp"),
        P("dp"),
    )
    body = make_body(mesh.shape["dp"], mesh.shape["tensor"])
    return jax.shard_map(body, mesh=mesh, in_specs=in_specs, out_specs=out_specs, check_vma=False)
```

```python
import math

import jax
import jax.numpy as jnp
from jax import lax
from jax.experimental import pallas as pl
from jax.experimental.pallas import tpu as pltpu
from jax.sharding import PartitionSpec as P


EPSILON = 1e-05
MASKED = -1e30
QUERY_ROWS = 256
SHORT_LEN = 256
BF16 = jnp.bfloat16
F32 = jnp.float32
VMEM_BYTES = 60 * 1024 * 1024


def dot_nn(left, right):
    return lax.dot_general(left, right, (((1,), (0,)), ((), ())), preferred_element_type=F32)


def dot_nt(left, right):
    return lax.dot_general(left, right, (((1,), (1,)), ((), ())), preferred_element_type=F32)


def dot_tn(left, right):
    return lax.dot_general(left, right, (((0,), (0,)), ((), ())), preferred_element_type=F32)


def normalize(values):
    row_mean = jnp.mean(values, axis=-1, keepdims=True)
    centered = values - row_mean
    inv_std = lax.rsqrt(jnp.mean(centered * centered, axis=-1, keepdims=True) + EPSILON)
    return (centered * inv_std, inv_std)


def norm_back(grad_normed, normed, inv_std, gain_vec):
    scaled = grad_normed * gain_vec
    return inv_std * (
        scaled
        - jnp.mean(scaled, axis=-1, keepdims=True)
        - normed * jnp.mean(scaled * normed, axis=-1, keepdims=True)
    )


def head_lanes(values, head, head_dim):
    per_group = 128 // head_dim
    first = (head // per_group) * 128
    group = values[:, first : min(first + 128, values.shape[1])]
    if group.shape[1] == head_dim:
        return group
    lane = lax.broadcasted_iota(jnp.int32, group.shape, 1)
    inside = (lane // head_dim) == (head % per_group)
    return jnp.where(inside, group, jnp.zeros_like(group))


def group_lanes(head, head_dim, width):
    per_group = 128 // head_dim
    first = (head // per_group) * 128
    return slice(first, min(first + 128, width))


def allowed_diagonal():
    key_pos = lax.broadcasted_iota(jnp.int32, (QUERY_ROWS, QUERY_ROWS), 0)
    row_pos = lax.broadcasted_iota(jnp.int32, (QUERY_ROWS, QUERY_ROWS), 1)
    return key_pos <= row_pos


def attend_block(queries, keys_ref, values_t_ref, start, old_rows, heads, head_dim):
    width = heads * head_dim
    attended_t = []
    logs = []
    allowed = allowed_diagonal()
    for head in range(heads):
        query = head_lanes(queries, head, head_dim)
        lanes = group_lanes(head, head_dim, width)
        rows = slice(head * head_dim, (head + 1) * head_dim)
        here = pl.ds(start, QUERY_ROWS)
        near = jnp.where(allowed, dot_nt(keys_ref[here, lanes], query), MASKED)
        row_max = jnp.max(near, axis=0, keepdims=True)
        if old_rows:
            far = dot_nt(keys_ref[0:old_rows, lanes], query)
            row_max = jnp.maximum(row_max, jnp.max(far, axis=0, keepdims=True))
        near = jnp.exp(near - row_max)
        total = jnp.sum(near, axis=0, keepdims=True)
        if old_rows:
            far = jnp.exp(far - row_max)
            total = total + jnp.sum(far, axis=0, keepdims=True)
        inverse = 1.0 / total
        result = dot_nn(values_t_ref[rows, here], (near * inverse).astype(BF16))
        if old_rows:
            result = result + dot_nn(values_t_ref[rows, 0:old_rows], (far * inverse).astype(BF16))
        attended_t.append(result)
        logs.append(row_max + jnp.log(total))
    attended = jnp.concatenate(attended_t, axis=0).T
    return attended, logs


def attend_body(
    heads, head_dim, block, first_in, w_ref, bias_ref, qkv_ref, att_ref, log_ref, keys_ref,
    values_t_ref, is_long,
):
    width = heads * head_dim
    blocks = keys_ref.shape[0] // QUERY_ROWS
    projected = dot_nt(first_in, w_ref[...])
    queries = (projected[:, :width] + bias_ref[0:1, :]).astype(BF16)
    key_rows = projected[:, width : 2 * width].astype(BF16)
    value_rows = projected[:, 2 * width :] + bias_ref[1:2, :]
    qkv_ref[...] = jnp.concatenate([queries, key_rows, value_rows.astype(BF16)], axis=1)
    start = pl.multiple_of(block * QUERY_ROWS, QUERY_ROWS)
    keys_ref[pl.ds(start, QUERY_ROWS), :] = key_rows
    values_t_ref[:, pl.ds(start, QUERY_ROWS)] = value_rows.T.astype(BF16)
    scaled = queries * jnp.asarray(1.0 / math.sqrt(head_dim), BF16)

    def finish(attended, logs):
        att_ref[...] = attended.astype(BF16)
        log_ref[...] = jnp.concatenate(
            logs + [jnp.zeros((8 - heads, QUERY_ROWS), F32)], axis=0
        )

    @pl.when(jnp.logical_or(is_long == 0, block == 0))
    def _():
        finish(*attend_block(scaled, keys_ref, values_t_ref, start, 0, heads, head_dim))

    for position in range(1, blocks):

        @pl.when(jnp.logical_and(is_long == 1, block == position))
        def _(position=position):
            finish(
                *attend_block(
                    scaled,
                    keys_ref,
                    values_t_ref,
                    position * QUERY_ROWS,
                    position * QUERY_ROWS,
                    heads,
                    head_dim,
                )
            )


def forward_own_kernel(heads, head_dim, info_ref, x_ref, gain_ref, shift_ref, w_ref, bias_ref,
                       first_ref, qkv_ref, att_ref, log_ref, keys_ref, values_t_ref):
    normed, _ = normalize(x_ref[...].astype(F32))
    first_in = (normed * gain_ref[...] + shift_ref[...]).astype(BF16)
    first_ref[...] = first_in
    attend_body(heads, head_dim, pl.program_id(0), first_in, w_ref, bias_ref, qkv_ref, att_ref,
                log_ref, keys_ref, values_t_ref, info_ref[1])


def forward_other_kernel(heads, head_dim, info_ref, first_ref, w_ref, bias_ref, att_own_ref,
                         w_out_own_ref, w_out_ref, qkv_ref, att_ref, log_ref, branch_ref,
                         keys_ref, values_t_ref):
    attend_body(heads, head_dim, pl.program_id(0), first_ref[...], w_ref, bias_ref, qkv_ref,
                att_ref, log_ref, keys_ref, values_t_ref, info_ref[1])
    branch = dot_nn(att_own_ref[...], w_out_own_ref[...]) + dot_nn(att_ref[...], w_out_ref[...])
    branch_ref[...] = branch.astype(BF16)


def mlp_kernel(info_ref, x_ref, branch_a_ref, branch_b_ref, b_out_ref, gain_ref, shift_ref, go_ref,
               fc_own_ref, fc_other_ref, proj_own_ref, proj_other_ref, b_fc_ref,
               residual_ref, mlp_ref, grad_ref, d_fc_ref, d_proj_ref, d_b_fc_ref, d_b_proj_ref,
               in_t_ref, go_t_ref, pre_own_ref, pre_other_ref, act_own_ref, act_other_ref):
    step = pl.program_id(0)
    rows = x_ref.shape[0]
    residual = x_ref[...].astype(F32) + (
        branch_a_ref[...].astype(F32) + branch_b_ref[...].astype(F32) + b_out_ref[...]
    )
    residual_ref[...] = residual
    normed, _ = normalize(residual)
    second_in = (normed * gain_ref[...] + shift_ref[...]).astype(BF16)
    grad_out = go_ref[...]
    here = pl.ds(pl.multiple_of(step * rows, rows), rows)
    in_t_ref[:, here] = second_in.T
    go_t_ref[:, here] = grad_out.T

    @pl.when(step == 0)
    def _():
        d_b_fc_ref[...] = jnp.zeros_like(d_b_fc_ref)
        d_b_proj_ref[...] = jnp.zeros_like(d_b_proj_ref)

    d_b_proj_ref[...] += jnp.sum(grad_out.astype(F32), axis=0, keepdims=True)
    mlp = None
    grad_second = None
    parts = (
        (fc_own_ref, proj_own_ref, pre_own_ref, act_own_ref),
        (fc_other_ref, proj_other_ref, pre_other_ref, act_other_ref),
    )
    slope = math.sqrt(2.0 / math.pi)
    for part, (fc_ref, proj_ref, pre_ref, act_ref) in enumerate(parts):
        pre_act = dot_nn(second_in, fc_ref[...]) + b_fc_ref[part : part + 1, :]
        square = pre_act * pre_act
        bent = jnp.tanh(slope * (pre_act + 0.044715 * (pre_act * square)))
        half = 0.5 * (1.0 + bent)
        act_low = (pre_act * half).astype(BF16)
        act_ref[here, :] = act_low
        part_out = dot_nn(act_low, proj_ref[...])
        grad_act = dot_nt(grad_out, proj_ref[...])
        derivative = half + (0.5 * pre_act) * (1.0 - bent * bent) * (
            slope + (3.0 * 0.044715 * slope) * square
        )
        grad_pre = (grad_act * derivative).astype(BF16)
        pre_ref[here, :] = grad_pre
        d_b_fc_ref[part : part + 1, :] += jnp.sum(grad_pre.astype(F32), axis=0, keepdims=True)
        part_grad = dot_nt(grad_pre, fc_ref[...])
        mlp = part_out if mlp is None else mlp + part_out
        grad_second = part_grad if grad_second is None else grad_second + part_grad
    mlp_ref[...] = mlp.astype(BF16)
    grad_ref[...] = grad_second.astype(BF16)

    @pl.when(step == pl.num_programs(0) - 1)
    def _():
        d_fc_ref[0] = dot_nn(in_t_ref[...], pre_own_ref[...]).astype(BF16)
        d_fc_ref[1] = dot_nn(in_t_ref[...], pre_other_ref[...]).astype(BF16)
        d_proj_ref[0] = dot_nn(go_t_ref[...], act_own_ref[...]).astype(BF16)
        d_proj_ref[1] = dot_nn(go_t_ref[...], act_other_ref[...]).astype(BF16)


def attend_back_block(queries, grads, logs, keys_ref, keys_t_ref, values_ref, grad_keys_ref,
                      grad_values_ref, start, old_rows, heads, head_dim, scale):
    width = heads * head_dim
    allowed = allowed_diagonal()
    grad_queries_t = []
    new_keys = []
    new_values = []
    for head in range(heads):
        query = head_lanes(queries, head, head_dim)
        scaled = query * jnp.asarray(scale, BF16)
        grad = head_lanes(grads, head, head_dim)
        lanes = group_lanes(head, head_dim, width)
        rows = slice(head * head_dim, (head + 1) * head_dim)
        log_row = logs[head : head + 1, :]
        here = pl.ds(start, QUERY_ROWS)
        near = dot_nt(keys_ref[here, lanes], scaled)
        near = jnp.where(allowed, jnp.exp(near - log_row), 0.0)
        grad_near = dot_nt(values_ref[here, lanes], grad)
        delta = jnp.sum(near * grad_near, axis=0, keepdims=True)
        if old_rows:
            old = slice(0, old_rows)
            far = jnp.exp(dot_nt(keys_ref[old, lanes], scaled) - log_row)
            grad_far = dot_nt(values_ref[old, lanes], grad)
            delta = delta + jnp.sum(far * grad_far, axis=0, keepdims=True)
        scores_near = (near * (grad_near - delta)).astype(BF16)
        result = dot_nn(keys_t_ref[rows, here], scores_near)
        new_keys.append(dot_nn(scores_near, query))
        new_values.append(dot_nn(near.astype(BF16), grad))
        if old_rows:
            scores_far = (far * (grad_far - delta)).astype(BF16)
            result = result + dot_nn(keys_t_ref[rows, old], scores_far)
            grad_keys_ref[old, lanes] += dot_nn(scores_far, query)
            grad_values_ref[old, lanes] += dot_nn(far.astype(BF16), grad)
        grad_queries_t.append(result)
    for head in range(heads):
        lanes = group_lanes(head, head_dim, width)
        here = pl.ds(start, QUERY_ROWS)
        grad_keys_ref[here, lanes] += new_keys[head]
        grad_values_ref[here, lanes] += new_values[head]
    return jnp.concatenate(grad_queries_t, axis=0).T * scale


def backward_other_kernel(heads, head_dim, info_ref, grad_a_ref, grad_b_ref, residual_ref, go_ref,
                          gain_ref, first_ref, qkv_ref, att_ref, log_ref, w_ref, w_out_ref,
                          grad_residual_ref, grad_branch_ref, grad_first_ref, d_w_ref, d_bias_ref,
                          d_norm_ref, acc_ref, keys_t_ref, keys_ref, values_ref, grad_keys_ref,
                          grad_values_ref, grad_queries_ref):
    step = pl.program_id(0)
    grad_second = grad_a_ref[...].astype(F32) + grad_b_ref[...].astype(F32)
    normed, inv_std = normalize(residual_ref[...])
    grad_residual = go_ref[...].astype(F32) + norm_back(grad_second, normed, inv_std, gain_ref[...])
    grad_residual_ref[...] = grad_residual
    grad_branch = grad_residual.astype(BF16)
    grad_branch_ref[...] = grad_branch

    @pl.when(step == 0)
    def _():
        d_norm_ref[...] = jnp.zeros_like(d_norm_ref)

    d_norm_ref[0:1, :] += jnp.sum(grad_second * normed, axis=0, keepdims=True)
    d_norm_ref[1:2, :] += jnp.sum(grad_second, axis=0, keepdims=True)
    d_norm_ref[2:3, :] += jnp.sum(grad_branch.astype(F32), axis=0, keepdims=True)
    grad_first = attend_back(heads, head_dim, grad_branch, first_ref, qkv_ref, att_ref, log_ref,
                             w_ref, w_out_ref, d_w_ref, d_bias_ref, acc_ref, keys_t_ref, keys_ref,
                             values_ref, grad_keys_ref, grad_values_ref, grad_queries_ref,
                             info_ref[1])
    grad_first_ref[...] = grad_first


def backward_own_kernel(heads, head_dim, info_ref, grad_branch_ref, grad_first_in_ref, first_ref,
                        qkv_ref, att_ref, log_ref, w_ref, w_out_ref,
                        grad_first_ref, d_w_ref, d_bias_ref, acc_ref, keys_t_ref, keys_ref,
                        values_ref, grad_keys_ref, grad_values_ref, grad_queries_ref):
    grad_first = attend_back(heads, head_dim, grad_branch_ref[...], first_ref, qkv_ref, att_ref,
                             log_ref, w_ref, w_out_ref, d_w_ref, d_bias_ref, acc_ref, keys_t_ref,
                             keys_ref, values_ref, grad_keys_ref, grad_values_ref,
                             grad_queries_ref, info_ref[1])
    grad_first_ref[...] = (grad_first + grad_first_in_ref[...]).astype(BF16)


def attend_back(heads, head_dim, grad_branch, first_ref, qkv_ref, att_ref, log_ref, w_ref,
                w_out_ref, d_w_ref, d_bias_ref, acc_ref, keys_t_ref, keys_ref, values_ref,
                grad_keys_ref, grad_values_ref, grad_queries_ref, is_long):
    step = pl.program_id(0)
    steps = pl.num_programs(0)
    blocks = qkv_ref.shape[0] // QUERY_ROWS
    block = blocks - 1 - step
    width = heads * head_dim
    scale = 1.0 / math.sqrt(head_dim)

    @pl.when(step == 0)
    def _():
        key_rows = qkv_ref[:, width : 2 * width]
        keys_ref[...] = key_rows
        values_ref[...] = qkv_ref[:, 2 * width :]
        keys_t_ref[...] = key_rows.T
        grad_keys_ref[...] = jnp.zeros_like(grad_keys_ref)
        grad_values_ref[...] = jnp.zeros_like(grad_values_ref)
        d_bias_ref[...] = jnp.zeros_like(d_bias_ref)
        acc_ref[...] = jnp.zeros_like(acc_ref)

    start = pl.multiple_of(block * QUERY_ROWS, QUERY_ROWS)
    here = pl.ds(start, QUERY_ROWS)
    queries = qkv_ref[here, 0:width]
    logs = log_ref[...]
    grads = dot_nt(grad_branch, w_out_ref[...]).astype(BF16)

    def run(start_row, old_rows):
        grad_queries_ref[...] = attend_back_block(
            queries, grads, logs, keys_ref, keys_t_ref, values_ref, grad_keys_ref,
            grad_values_ref, start_row, old_rows, heads, head_dim, scale)

    @pl.when(jnp.logical_or(is_long == 0, block == 0))
    def _():
        run(start, 0)

    for position in range(1, blocks):

        @pl.when(jnp.logical_and(is_long == 1, block == position))
        def _(position=position):
            run(position * QUERY_ROWS, position * QUERY_ROWS)

    mixed = jnp.concatenate(
        [grad_queries_ref[...], grad_keys_ref[here, :] * scale, grad_values_ref[here, :]], axis=1
    ).astype(BF16)
    d_bias_ref[...] += jnp.sum(mixed.astype(F32), axis=0, keepdims=True)
    acc_ref[:, 0 : 3 * width] += dot_tn(first_ref[...], mixed)
    acc_ref[:, 3 * width :] += dot_tn(grad_branch, att_ref[...])

    @pl.when(step == steps - 1)
    def _():
        d_w_ref[...] = acc_ref[...].astype(d_w_ref.dtype)

    return dot_nn(mixed, w_ref[...])


def last_norm_kernel(info_ref, x_ref, grad_a_ref, grad_b_ref, grad_residual_ref, gain_ref,
                     grad_in_ref, grad_low_ref, d_norm_ref):
    @pl.when(pl.program_id(0) == 0)
    def _():
        d_norm_ref[...] = jnp.zeros_like(d_norm_ref)

    grad_first = grad_a_ref[...].astype(F32) + grad_b_ref[...].astype(F32)
    normed, inv_std = normalize(x_ref[...].astype(F32))
    grad_in = grad_residual_ref[...] + norm_back(grad_first, normed, inv_std, gain_ref[...])
    grad_low = grad_in.astype(BF16)
    grad_low_ref[...] = grad_low
    grad_in_ref[...] = grad_low.astype(F32)
    d_norm_ref[0:1, :] += jnp.sum(grad_first * normed, axis=0, keepdims=True)
    d_norm_ref[1:2, :] += jnp.sum(grad_first, axis=0, keepdims=True)


def block_kernel(info_ref, residual_ref, mlp_a_ref, mlp_b_ref, bias_ref, out_ref):
    total = residual_ref[...] + (mlp_a_ref[...].astype(F32) + mlp_b_ref[...].astype(F32))
    out_ref[...] = (total + bias_ref[...]).astype(BF16)


def fill_kernel(info_ref, near_ref, far_ref, whole_ref, out_ref):
    from_near = (pl.program_id(0) * near_ref.shape[0]) // info_ref[4] == info_ref[2]

    @pl.when(from_near)
    def _():
        out_ref[...] = near_ref[...].astype(out_ref.dtype)

    @pl.when(jnp.logical_not(from_near))
    def _():
        out_ref[...] = far_ref[...].astype(out_ref.dtype)


def row_spec(rows, width, shift=False):
    if shift:
        return pl.BlockSpec((rows, width), lambda step, info: (info[0] + step, 0))
    return pl.BlockSpec((rows, width), lambda step, info: (step, 0))


def back_spec(rows, width, blocks, shift=False):
    if shift:
        return pl.BlockSpec((rows, width), lambda step, info: (info[0] + blocks - 1 - step, 0))
    return pl.BlockSpec((rows, width), lambda step, info: (blocks - 1 - step, 0))


def whole(shape):
    return pl.BlockSpec(shape, lambda step, info: (0,) * len(shape))


def call(kernel, steps, in_specs, out_specs, out_shape, scratch, cost_us, aliases=None):
    return pl.pallas_call(
        kernel,
        grid_spec=pltpu.PrefetchScalarGridSpec(
            num_scalar_prefetch=1,
            grid=(steps,),
            in_specs=in_specs,
            out_specs=out_specs,
            scratch_shapes=scratch,
        ),
        out_shape=out_shape,
        input_output_aliases=aliases or {},
        compiler_params=pltpu.CompilerParams(
            dimension_semantics=("arbitrary",), vmem_limit_bytes=VMEM_BYTES
        ),
        cost_estimate=pl.CostEstimate(
            flops=int(cost_us * 1e9), transcendentals=0, bytes_accessed=int(cost_us * 3e6)
        ),
    )


def struct(shape, dtype):
    return jax.ShapeDtypeStruct(shape, dtype)


def exchange(value, axis_name, size, bit):
    return lax.ppermute(value, axis_name, [(i, i ^ bit) for i in range(size)])


def after(value, earlier):
    return lax.optimization_barrier((value, earlier))[0]


def make_body(dp_size, tensor_size):
    def body(hidden_in, doc_ids, ln1_gain, ln1_bias, w_qkv, b_qv, w_out, b_out, ln2_gain, ln2_bias,
             w_fc, b_fc, w_proj, b_proj, grad_out):
        row_count, width = hidden_in.shape
        heads, head_dim = w_qkv.shape[2:]
        local = heads * head_dim
        hidden = w_fc.shape[1]
        rows = row_count // 2
        blocks = rows // QUERY_ROWS
        half = rows // 2
        place = lax.axis_index("tensor")
        upper = place // 2
        core = place % 2
        is_long = (doc_ids[SHORT_LEN] == doc_ids[0]).astype(jnp.int32)
        info = jnp.stack(
            [upper * blocks, is_long, core, (1 - upper) * blocks, half]
        ).astype(jnp.int32)

        def core_swap(value):
            return exchange(value, "tensor", tensor_size, 1)

        def pair_swap(value):
            return exchange(value, "tensor", tensor_size, 2)

        qkv_own = w_qkv.transpose(1, 2, 3, 0).reshape(3 * local, width)
        out_own = w_out.reshape(local, width)
        bias_own = b_qv.reshape(2, local)
        bits = dp_size.bit_length() - 1
        position = lax.axis_index("dp")
        share = width // dp_size
        piece = hidden // dp_size
        small_other = pair_swap(
            jnp.concatenate([b_qv.reshape(1, 2 * local), b_fc.reshape(1, hidden)], axis=1)
        )
        earlier = []
        gathered = pair_swap(lax.dynamic_slice_in_dim(w_proj, position * piece, piece, axis=0))
        qkv_other = pair_swap(qkv_own)
        out_other = pair_swap(out_own)
        fc_other = pair_swap(w_fc)
        gathered, hidden_in = lax.optimization_barrier((gathered, hidden_in))
        gathered = gathered.reshape(1, piece, width)
        for bit in reversed(range(bits)):
            mine = (position >> bit) & 1
            come = exchange(gathered, "dp", dp_size, 1 << bit)
            if bit:
                earlier.append(come)
            count = gathered.shape[0]
            gathered = jnp.where(
                mine == 0, jnp.stack([gathered, come], 1), jnp.stack([come, gathered], 1)
            ).reshape(2 * count, piece, width)
        proj_other = gathered.reshape(hidden, width)
        bias_other = small_other[:, : 2 * local].reshape(2, local)
        b_fc_both = jnp.concatenate([b_fc.reshape(1, hidden), small_other[:, 2 * local :]], axis=0)

        first_spec = row_spec(QUERY_ROWS, width)
        qkv_spec = row_spec(QUERY_ROWS, 3 * local)
        att_spec = row_spec(QUERY_ROWS, local)
        log_spec = pl.BlockSpec((8, QUERY_ROWS), lambda step, info: (0, step))
        attend_scratch = [pltpu.VMEM((rows, local), BF16), pltpu.VMEM((local, rows), BF16)]

        def forward_own(*refs):
            forward_own_kernel(heads, head_dim, *refs)

        def forward_other(*refs):
            forward_other_kernel(heads, head_dim, *refs)

        first_in, mix_own, att_own, log_own = call(
            forward_own,
            blocks,
            [row_spec(QUERY_ROWS, width, True), whole((width,)), whole((width,)),
             whole((3 * local, width)), whole((2, local))],
            [first_spec, qkv_spec, att_spec, log_spec],
            [struct((rows, width), BF16), struct((rows, 3 * local), BF16),
             struct((rows, local), BF16), struct((8, rows), F32)],
            attend_scratch,
            11,
        )(info, hidden_in, ln1_gain, ln1_bias, qkv_own, bias_own)
        first_in = after(first_in, tuple(earlier))
        mix_other, att_other, log_other, branch = call(
            forward_other,
            blocks,
            [first_spec, whole((3 * local, width)), whole((2, local)), att_spec,
             whole((local, width)), whole((local, width))],
            [qkv_spec, att_spec, log_spec, first_spec],
            [struct((rows, 3 * local), BF16), struct((rows, local), BF16),
             struct((8, rows), F32), struct((rows, width), BF16)],
            attend_scratch,
            12,
        )(info, first_in, qkv_other, bias_other, att_own, out_own, out_other)
        branch_swapped = core_swap(branch)

        residual, mlp, grad_second, d_fc, d_proj, d_b_fc, d_b_proj = call(
            mlp_kernel,
            blocks,
            [row_spec(QUERY_ROWS, width, True), first_spec, first_spec, whole((width,)),
             whole((width,)), whole((width,)), row_spec(QUERY_ROWS, width, True),
             whole((width, hidden)), whole((width, hidden)), whole((hidden, width)),
             whole((hidden, width)), whole((2, hidden))],
            [first_spec, first_spec, first_spec] + [whole((2, width, hidden))] * 2
            + [whole((2, hidden)), whole((1, width))],
            [struct((rows, width), F32), struct((rows, width), BF16), struct((rows, width), BF16),
             struct((2, width, hidden), BF16), struct((2, width, hidden), BF16),
             struct((2, hidden), F32), struct((1, width), F32)],
            [pltpu.VMEM((width, rows), BF16)] * 2 + [pltpu.VMEM((rows, hidden), BF16)] * 4,
            28,
        )(info, hidden_in, branch, branch_swapped, b_out, ln2_gain,
          ln2_bias, grad_out, w_fc, fc_other, w_proj, proj_other, b_fc_both)
        grad_swapped = core_swap(grad_second)
        mlp_swapped = core_swap(mlp)

        block_out = call(
            block_kernel,
            blocks,
            [first_spec, first_spec, first_spec, whole((width,))],
            row_spec(QUERY_ROWS, width, True),
            struct((row_count, width), BF16),
            [],
            3,
        )(info, residual, mlp, mlp_swapped, b_proj)
        block_near = pair_swap(
            lax.dynamic_slice_in_dim(block_out, upper * rows + core * half, half, axis=0)
        )

        back_rows = back_spec(QUERY_ROWS, width, blocks)
        back_att = back_spec(QUERY_ROWS, local, blocks)
        back_log = pl.BlockSpec((8, QUERY_ROWS), lambda step, info: (0, blocks - 1 - step))
        back_scratch = [
            pltpu.VMEM((width, 4 * local), F32),
            pltpu.VMEM((local, rows), BF16),
            pltpu.VMEM((rows, local), BF16),
            pltpu.VMEM((rows, local), BF16),
            pltpu.VMEM((rows, local), F32),
            pltpu.VMEM((rows, local), F32),
            pltpu.VMEM((QUERY_ROWS, local), F32),
        ]

        def backward_other(*refs):
            backward_other_kernel(heads, head_dim, *refs)

        def backward_own(*refs):
            backward_own_kernel(heads, head_dim, *refs)

        (grad_residual, grad_branch, grad_first_other, d_att_other, d_bias_other,
         d_norm_two) = call(
            backward_other,
            blocks,
            [back_rows, back_rows, back_rows, back_spec(QUERY_ROWS, width, blocks, True),
             whole((width,)), back_rows, whole((rows, 3 * local)), back_att, back_log,
             whole((3 * local, width)), whole((local, width))],
            [back_rows, back_rows, back_rows, whole((width, 4 * local)), whole((1, 3 * local)),
             whole((8, width))],
            [struct((rows, width), F32), struct((rows, width), BF16), struct((rows, width), F32),
             struct((width, 4 * local), BF16), struct((1, 3 * local), F32),
             struct((8, width), F32)],
            back_scratch,
            21,
        )(info, grad_second, grad_swapped, residual, grad_out, ln2_gain, first_in,
          mix_other, att_other, log_other, qkv_other, out_other)
        grad_first, d_att_own, d_bias_own = call(
            backward_own,
            blocks,
            [back_rows, back_rows, back_rows, whole((rows, 3 * local)), back_att, back_log,
             whole((3 * local, width)), whole((local, width))],
            [back_rows, whole((width, 4 * local)), whole((1, 3 * local))],
            [struct((rows, width), BF16), struct((width, 4 * local), BF16),
             struct((1, 3 * local), F32)],
            back_scratch,
            17,
        )(info, grad_branch, grad_first_other, first_in, mix_own, att_own, log_own, qkv_own,
          out_own)
        first_swapped = core_swap(grad_first)
        grad_in, grad_low, d_norm_one = call(
            last_norm_kernel,
            blocks,
            [row_spec(QUERY_ROWS, width, True), first_spec, first_spec, first_spec,
             whole((width,))],
            [row_spec(QUERY_ROWS, width, True), first_spec, whole((8, width))],
            [struct((row_count, width), F32), struct((rows, width), BF16),
             struct((8, width), F32)],
            [],
            7,
        )(info, hidden_in, grad_first, first_swapped, grad_residual, ln1_gain)

        def fill(target, near, far):
            quarter = half // QUERY_ROWS
            return call(
                fill_kernel,
                blocks,
                [pl.BlockSpec((QUERY_ROWS, width), lambda step, info: (
                    jnp.clip(step - quarter * info[2], 0, quarter - 1), 0)),
                 pl.BlockSpec((QUERY_ROWS, width), lambda step, info: (
                    jnp.clip(step - quarter * (1 - info[2]), 0, quarter - 1), 0)),
                 pl.BlockSpec(memory_space=pl.ANY)],
                pl.BlockSpec((QUERY_ROWS, width), lambda step, info: (info[3] + step, 0)),
                struct(target.shape, target.dtype),
                [],
                2,
                {3: 0},
            )(info, near, far, target)

        grad_near = pair_swap(lax.dynamic_slice_in_dim(grad_low, core * half, half, axis=0))
        grad_in = fill(grad_in, grad_near, core_swap(grad_near))
        block_far = core_swap(block_near)
        block_out = fill(block_out, block_near, block_far)

        def pick(value, axis, which):
            return lax.dynamic_index_in_dim(value, which, axis, keepdims=False)

        def split(value):
            lead = value.shape[:-2]
            return value.reshape(lead + (2,) * bits + (share, value.shape[-1]))

        def start_stage(value, bit, left):
            axis = value.ndim - 2 - len(left) + [b for b in reversed(range(bits)) if b in left].index(bit)
            mine = (position >> bit) & 1
            sent = exchange(pick(value, axis, 1 - mine).astype(BF16), "dp", dp_size, 1 << bit)
            return pick(value, axis, mine), sent

        def add(kept, received):
            return kept.astype(F32) + received.astype(F32)

        def stages(value, left):
            for bit in list(left):
                kept, received = start_stage(value, bit, left)
                left = [b for b in left if b != bit]
                value = add(kept, received)
            return value

        order_fc = list(range(bits))
        order_proj = [1 % bits, 0] + list(range(2, bits)) if bits > 1 else order_fc
        kept_fc, sent_fc = start_stage(split(d_fc), order_fc[0], order_fc)
        kept_proj, sent_proj = start_stage(split(d_proj), order_proj[0], order_proj)
        kept_far, sent_far = start_stage(split(d_att_other), order_fc[0], order_fc)
        sent_fc, sent_proj = after((sent_fc, sent_proj), grad_branch)
        half_fc = add(kept_fc, sent_fc)
        half_proj = add(kept_proj, sent_proj)
        come_fc = pair_swap(half_fc[1].astype(BF16))
        come_proj = pair_swap(half_proj[1].astype(BF16))
        kept_near, sent_near = start_stage(split(d_att_own), order_fc[0], order_fc)
        sent_far = after(sent_far, grad_first)
        come_far = pair_swap(add(kept_far, sent_far).astype(BF16))
        come_fc, come_proj, come_far, sent_near = after(
            (come_fc, come_proj, come_far, sent_near), grad_low
        )
        fc_share = stages(add(half_fc[0], come_fc), order_fc[1:])
        proj_share = stages(add(half_proj[0], come_proj), order_proj[1:])
        att_share = stages(add(add(kept_near, sent_near), come_far), order_fc[1:])

        def wide(d_bias):
            row = jnp.concatenate([d_bias[:, :local], d_bias[:, 2 * local :]], axis=1)
            return jnp.pad(row, ((0, 0), (0, width - 2 * local)))

        common = [d_b_proj, d_norm_two[0:3], d_norm_one[0:2]]
        small = jnp.concatenate(common + [d_b_fc[0:1], wide(d_bias_own)], axis=0)
        small_sent = jnp.concatenate(common + [d_b_fc[1:2], wide(d_bias_other)], axis=0)
        small_come = pair_swap(small_sent)
        small = small + small_come
        for bit in range(bits):
            small = small + exchange(small, "dp", dp_size, 1 << bit)
        shares = lax.dynamic_index_in_dim(
            small[0:6].reshape(6, dp_size, share), position, 1, keepdims=False
        )
        d_b_proj_share, d_gain_two, d_shift_two, d_b_out, d_gain_one, d_shift_one = (
            shares[i] for i in range(6)
        )
        fc_rows, fc_columns = b_fc.shape
        d_b_fc_share = lax.dynamic_slice_in_dim(
            small[6].reshape(fc_rows, fc_columns), position * (fc_columns // dp_size),
            fc_columns // dp_size, axis=1,
        )
        d_b_qv_share = lax.dynamic_slice_in_dim(
            small[7, : 2 * local].reshape(2, heads, head_dim), position * (head_dim // dp_size),
            head_dim // dp_size, axis=2,
        )
        att_turned = att_share.T
        d_w_qkv = att_turned[: 3 * local].reshape(3, heads, head_dim, share).transpose(3, 0, 1, 2)
        d_w_out = att_turned[3 * local :].reshape(heads, head_dim, share)
        return (block_out, grad_in, d_gain_one, d_shift_one, d_w_qkv, d_b_qv_share, d_w_out,
                d_b_out, d_gain_two, d_shift_two, fc_share, d_b_fc_share, proj_share.T,
                d_b_proj_share)

    return body


def solution(mesh):
    in_specs = (
        P("dp", None),
        P("dp"),
        P(),
        P(),
        P(None, None, "tensor", None),
        P(None, "tensor", None),
        P("tensor", None, None),
        P(),
        P(),
        P(),
        P(None, "tensor"),
        P("tensor", None),
        P("tensor", None),
        P(),
        P("dp", None),
    )
    out_specs = (
        P("dp", None),
        P("dp", None),
        P("dp"),
        P("dp"),
        P("dp", None, "tensor", None),
        P(None, "tensor", "dp"),
        P("tensor", None, "dp"),
        P("dp"),
        P("dp"),
        P("dp"),
        P("dp", "tensor"),
        P("tensor", "dp"),
        P("tensor", "dp"),
        P("dp"),
    )
    inner = make_body(mesh.shape["dp"], mesh.shape["tensor"])

    return jax.shard_map(inner, mesh=mesh, in_specs=in_specs, out_specs=out_specs, check_vma=False)
```

```python
import math

import jax
import jax.numpy as jnp
from jax import lax
from jax.experimental import pallas as pl
from jax.experimental.pallas import tpu as pltpu
from jax.sharding import PartitionSpec as P


EPSILON = 1e-05
MASKED = -1e30
QUERY_ROWS = 256
SHORT_LEN = 256
BF16 = jnp.bfloat16
F32 = jnp.float32
VMEM_BYTES = 60 * 1024 * 1024


def dot_nn(left, right):
    return lax.dot_general(left, right, (((1,), (0,)), ((), ())), preferred_element_type=F32)


def dot_nt(left, right):
    return lax.dot_general(left, right, (((1,), (1,)), ((), ())), preferred_element_type=F32)


def dot_tn(left, right):
    return lax.dot_general(left, right, (((0,), (0,)), ((), ())), preferred_element_type=F32)


def normalize(values):
    row_mean = jnp.mean(values, axis=-1, keepdims=True)
    centered = values - row_mean
    inv_std = lax.rsqrt(jnp.mean(centered * centered, axis=-1, keepdims=True) + EPSILON)
    return (centered * inv_std, inv_std)


def norm_back(grad_normed, normed, inv_std, gain_vec):
    scaled = grad_normed * gain_vec
    return inv_std * (
        scaled
        - jnp.mean(scaled, axis=-1, keepdims=True)
        - normed * jnp.mean(scaled * normed, axis=-1, keepdims=True)
    )


def head_lanes(values, head, head_dim):
    per_group = 128 // head_dim
    first = (head // per_group) * 128
    group = values[:, first : min(first + 128, values.shape[1])]
    if group.shape[1] == head_dim:
        return group
    lane = lax.broadcasted_iota(jnp.int32, group.shape, 1)
    inside = (lane // head_dim) == (head % per_group)
    return jnp.where(inside, group, jnp.zeros_like(group))


def group_lanes(head, head_dim, width):
    per_group = 128 // head_dim
    first = (head // per_group) * 128
    return slice(first, min(first + 128, width))


def allowed_diagonal():
    key_pos = lax.broadcasted_iota(jnp.int32, (QUERY_ROWS, QUERY_ROWS), 0)
    row_pos = lax.broadcasted_iota(jnp.int32, (QUERY_ROWS, QUERY_ROWS), 1)
    return key_pos <= row_pos


def attend_block(queries, keys_ref, values_t_ref, start, old_rows, heads, head_dim):
    width = heads * head_dim
    attended_t = []
    logs = []
    allowed = allowed_diagonal()
    for head in range(heads):
        query = head_lanes(queries, head, head_dim)
        lanes = group_lanes(head, head_dim, width)
        rows = slice(head * head_dim, (head + 1) * head_dim)
        here = pl.ds(start, QUERY_ROWS)
        near = jnp.where(allowed, dot_nt(keys_ref[here, lanes], query), MASKED)
        row_max = jnp.max(near, axis=0, keepdims=True)
        if old_rows:
            far = dot_nt(keys_ref[0:old_rows, lanes], query)
            row_max = jnp.maximum(row_max, jnp.max(far, axis=0, keepdims=True))
        near = jnp.exp(near - row_max)
        total = jnp.sum(near, axis=0, keepdims=True)
        if old_rows:
            far = jnp.exp(far - row_max)
            total = total + jnp.sum(far, axis=0, keepdims=True)
        inverse = 1.0 / total
        result = dot_nn(values_t_ref[rows, here], (near * inverse).astype(BF16))
        if old_rows:
            result = result + dot_nn(values_t_ref[rows, 0:old_rows], (far * inverse).astype(BF16))
        attended_t.append(result)
        logs.append(row_max + jnp.log(total))
    attended = jnp.concatenate(attended_t, axis=0).T
    return attended, logs


def attend_body(
    heads, head_dim, block, first_in, w_ref, bias_ref, qkv_ref, att_ref, log_ref, keys_ref,
    values_t_ref, is_long,
):
    width = heads * head_dim
    blocks = keys_ref.shape[0] // QUERY_ROWS
    projected = dot_nt(first_in, w_ref[...])
    queries = (projected[:, :width] + bias_ref[0:1, :]).astype(BF16)
    key_rows = projected[:, width : 2 * width].astype(BF16)
    value_rows = projected[:, 2 * width :] + bias_ref[1:2, :]
    qkv_ref[...] = jnp.concatenate([queries, key_rows, value_rows.astype(BF16)], axis=1)
    start = pl.multiple_of(block * QUERY_ROWS, QUERY_ROWS)
    keys_ref[pl.ds(start, QUERY_ROWS), :] = key_rows
    values_t_ref[:, pl.ds(start, QUERY_ROWS)] = value_rows.T.astype(BF16)
    scaled = queries * jnp.asarray(1.0 / math.sqrt(head_dim), BF16)

    def finish(attended, logs):
        att_ref[...] = attended.astype(BF16)
        log_ref[...] = jnp.concatenate(
            logs + [jnp.zeros((8 - heads, QUERY_ROWS), F32)], axis=0
        )

    @pl.when(jnp.logical_or(is_long == 0, block == 0))
    def _():
        finish(*attend_block(scaled, keys_ref, values_t_ref, start, 0, heads, head_dim))

    for position in range(1, blocks):

        @pl.when(jnp.logical_and(is_long == 1, block == position))
        def _(position=position):
            finish(
                *attend_block(
                    scaled,
                    keys_ref,
                    values_t_ref,
                    position * QUERY_ROWS,
                    position * QUERY_ROWS,
                    heads,
                    head_dim,
                )
            )


def forward_own_kernel(heads, head_dim, info_ref, x_ref, gain_ref, shift_ref, w_ref, bias_ref,
                       first_ref, qkv_ref, att_ref, log_ref, keys_ref, values_t_ref):
    normed, _ = normalize(x_ref[...].astype(F32))
    first_in = (normed * gain_ref[...] + shift_ref[...]).astype(BF16)
    first_ref[...] = first_in
    attend_body(heads, head_dim, pl.program_id(0), first_in, w_ref, bias_ref, qkv_ref, att_ref,
                log_ref, keys_ref, values_t_ref, info_ref[1])


def forward_other_kernel(heads, head_dim, info_ref, first_ref, w_ref, bias_ref, att_own_ref,
                         w_out_own_ref, w_out_ref, qkv_ref, att_ref, log_ref, branch_ref,
                         keys_ref, values_t_ref):
    attend_body(heads, head_dim, pl.program_id(0), first_ref[...], w_ref, bias_ref, qkv_ref,
                att_ref, log_ref, keys_ref, values_t_ref, info_ref[1])
    branch = dot_nn(att_own_ref[...], w_out_own_ref[...]) + dot_nn(att_ref[...], w_out_ref[...])
    branch_ref[...] = branch.astype(BF16)


def write_split(source_ref, kept_ref, sent_ref, mine, part=None):
    run = kept_ref.shape[-2]
    count = kept_ref.shape[-3]
    for value in range(2):

        @pl.when(mine == value)
        def _(value=value):
            for index in range(2 * count):
                target = kept_ref if index % 2 == value else sent_ref
                piece = source_ref[index * run : (index + 1) * run, :].astype(BF16)
                if part is None:
                    target[index // 2] = piece
                else:
                    target[part, index // 2] = piece


def mlp_kernel(info_ref, x_ref, branch_a_ref, branch_b_ref, b_out_ref, gain_ref, shift_ref, go_ref,
               fc_own_ref, fc_top_ref, fc_low_ref, proj_own_ref, proj_other_ref, b_fc_ref,
               residual_ref, mlp_ref, grad_ref, fc_kept_ref, fc_sent_ref, proj_kept_ref,
               proj_sent_ref, d_b_fc_ref, d_b_proj_ref,
               sum_ref, in_t_ref, go_t_ref, pre_own_ref, pre_other_ref, act_own_ref, act_other_ref):
    step = pl.program_id(0)
    rows = x_ref.shape[0]
    residual = x_ref[...].astype(F32) + (
        branch_a_ref[...].astype(F32) + branch_b_ref[...].astype(F32) + b_out_ref[...]
    )
    residual_ref[...] = residual
    normed, _ = normalize(residual)
    second_in = (normed * gain_ref[...] + shift_ref[...]).astype(BF16)
    grad_out = go_ref[...]
    here = pl.ds(pl.multiple_of(step * rows, rows), rows)
    in_t_ref[:, here] = second_in.T
    go_t_ref[:, here] = grad_out.T

    @pl.when(step == 0)
    def _():
        d_b_fc_ref[...] = jnp.zeros_like(d_b_fc_ref)
        d_b_proj_ref[...] = jnp.zeros_like(d_b_proj_ref)

    d_b_proj_ref[...] += jnp.sum(grad_out.astype(F32), axis=0, keepdims=True)
    mlp = None
    grad_second = None
    parts = (
        ((fc_own_ref,), proj_own_ref, pre_own_ref, act_own_ref),
        ((fc_top_ref, fc_low_ref), proj_other_ref, pre_other_ref, act_other_ref),
    )
    slope = math.sqrt(2.0 / math.pi)
    for part, (fc_refs, proj_ref, pre_ref, act_ref) in enumerate(parts):
        pre_act = b_fc_ref[part : part + 1, :]
        first = 0
        for fc_ref in fc_refs:
            last = first + fc_ref.shape[0]
            pre_act = pre_act + dot_nn(second_in[:, first:last], fc_ref[...])
            first = last
        square = pre_act * pre_act
        bent = jnp.tanh(slope * (pre_act + 0.044715 * (pre_act * square)))
        half = 0.5 * (1.0 + bent)
        act_low = (pre_act * half).astype(BF16)
        act_ref[here, :] = act_low
        part_out = dot_nn(act_low, proj_ref[...])
        grad_act = dot_nt(grad_out, proj_ref[...])
        derivative = half + (0.5 * pre_act) * (1.0 - bent * bent) * (
            slope + (3.0 * 0.044715 * slope) * square
        )
        grad_pre = (grad_act * derivative).astype(BF16)
        pre_ref[here, :] = grad_pre
        d_b_fc_ref[part : part + 1, :] += jnp.sum(grad_pre.astype(F32), axis=0, keepdims=True)
        part_grad = jnp.concatenate([dot_nt(grad_pre, fc_ref[...]) for fc_ref in fc_refs], axis=1)
        mlp = part_out if mlp is None else mlp + part_out
        grad_second = part_grad if grad_second is None else grad_second + part_grad
    mlp_ref[...] = mlp.astype(BF16)
    grad_ref[...] = grad_second.astype(BF16)

    @pl.when(step == pl.num_programs(0) - 1)
    def _():
        for part, (act_ref, pre_ref) in enumerate(
            ((act_own_ref, pre_own_ref), (act_other_ref, pre_other_ref))
        ):
            sum_ref[...] = dot_nn(in_t_ref[...], pre_ref[...])
            write_split(sum_ref, fc_kept_ref, fc_sent_ref, info_ref[5], part)
            sum_ref[...] = dot_nn(go_t_ref[...], act_ref[...])
            write_split(sum_ref, proj_kept_ref, proj_sent_ref, info_ref[6], part)


def attend_back_block(queries, grads, logs, keys_ref, keys_t_ref, values_ref, grad_keys_ref,
                      grad_values_ref, start, old_rows, heads, head_dim, scale):
    width = heads * head_dim
    allowed = allowed_diagonal()
    grad_queries_t = []
    new_keys = []
    new_values = []
    for head in range(heads):
        query = head_lanes(queries, head, head_dim)
        scaled = query * jnp.asarray(scale, BF16)
        grad = head_lanes(grads, head, head_dim)
        lanes = group_lanes(head, head_dim, width)
        rows = slice(head * head_dim, (head + 1) * head_dim)
        log_row = logs[head : head + 1, :]
        here = pl.ds(start, QUERY_ROWS)
        near = dot_nt(keys_ref[here, lanes], scaled)
        near = jnp.where(allowed, jnp.exp(near - log_row), 0.0)
        grad_near = dot_nt(values_ref[here, lanes], grad)
        delta = jnp.sum(near * grad_near, axis=0, keepdims=True)
        if old_rows:
            old = slice(0, old_rows)
            far = jnp.exp(dot_nt(keys_ref[old, lanes], scaled) - log_row)
            grad_far = dot_nt(values_ref[old, lanes], grad)
            delta = delta + jnp.sum(far * grad_far, axis=0, keepdims=True)
        scores_near = (near * (grad_near - delta)).astype(BF16)
        result = dot_nn(keys_t_ref[rows, here], scores_near)
        new_keys.append(dot_nn(scores_near, query))
        new_values.append(dot_nn(near.astype(BF16), grad))
        if old_rows:
            scores_far = (far * (grad_far - delta)).astype(BF16)
            result = result + dot_nn(keys_t_ref[rows, old], scores_far)
            grad_keys_ref[old, lanes] += dot_nn(scores_far, query)
            grad_values_ref[old, lanes] += dot_nn(far.astype(BF16), grad)
        grad_queries_t.append(result)
    for head in range(heads):
        lanes = group_lanes(head, head_dim, width)
        here = pl.ds(start, QUERY_ROWS)
        grad_keys_ref[here, lanes] += new_keys[head]
        grad_values_ref[here, lanes] += new_values[head]
    return jnp.concatenate(grad_queries_t, axis=0).T * scale


def backward_other_kernel(heads, head_dim, info_ref, grad_a_ref, grad_b_ref, residual_ref, go_ref,
                          gain_ref, mlp_a_ref, mlp_b_ref, b_proj_ref, first_ref, qkv_ref, att_ref, log_ref, w_ref, w_out_ref,
                          grad_residual_ref, grad_branch_ref, grad_first_ref, kept_ref, sent_ref,
                          d_bias_ref, d_norm_ref, block_ref, acc_ref, keys_t_ref, keys_ref, values_ref, grad_keys_ref,
                          grad_values_ref, grad_queries_ref):
    step = pl.program_id(0)
    grad_second = grad_a_ref[...].astype(F32) + grad_b_ref[...].astype(F32)
    normed, inv_std = normalize(residual_ref[...])
    grad_residual = go_ref[...].astype(F32) + norm_back(grad_second, normed, inv_std, gain_ref[...])
    grad_residual_ref[...] = grad_residual
    block_ref[...] = block_value(residual_ref, mlp_a_ref, mlp_b_ref, b_proj_ref)
    grad_branch = grad_residual.astype(BF16)
    grad_branch_ref[...] = grad_branch

    @pl.when(step == 0)
    def _():
        d_norm_ref[...] = jnp.zeros_like(d_norm_ref)

    d_norm_ref[0:1, :] += jnp.sum(grad_second * normed, axis=0, keepdims=True)
    d_norm_ref[1:2, :] += jnp.sum(grad_second, axis=0, keepdims=True)
    d_norm_ref[2:3, :] += jnp.sum(grad_branch.astype(F32), axis=0, keepdims=True)
    grad_first = attend_back(heads, head_dim, grad_branch, first_ref, qkv_ref, att_ref, log_ref,
                             w_ref, w_out_ref, kept_ref, sent_ref, d_bias_ref, acc_ref, keys_t_ref,
                             keys_ref, values_ref, grad_keys_ref, grad_values_ref,
                             grad_queries_ref, info_ref)
    grad_first_ref[...] = grad_first


def backward_own_kernel(heads, head_dim, info_ref, grad_branch_ref, grad_first_in_ref, first_ref,
                        qkv_ref, att_ref, log_ref, w_ref, w_out_ref,
                        grad_first_ref, kept_ref, sent_ref, d_bias_ref, acc_ref, keys_t_ref,
                        keys_ref, values_ref, grad_keys_ref, grad_values_ref, grad_queries_ref):
    grad_first = attend_back(heads, head_dim, grad_branch_ref[...], first_ref, qkv_ref, att_ref,
                             log_ref, w_ref, w_out_ref, kept_ref, sent_ref, d_bias_ref, acc_ref,
                             keys_t_ref, keys_ref, values_ref, grad_keys_ref, grad_values_ref,
                             grad_queries_ref, info_ref)
    grad_first_ref[...] = (grad_first + grad_first_in_ref[...]).astype(BF16)


def attend_back(heads, head_dim, grad_branch, first_ref, qkv_ref, att_ref, log_ref, w_ref,
                w_out_ref, kept_ref, sent_ref, d_bias_ref, acc_ref, keys_t_ref, keys_ref, values_ref,
                grad_keys_ref, grad_values_ref, grad_queries_ref, info_ref):
    is_long = info_ref[1]
    step = pl.program_id(0)
    steps = pl.num_programs(0)
    blocks = qkv_ref.shape[0] // QUERY_ROWS
    block = blocks - 1 - step
    width = heads * head_dim
    scale = 1.0 / math.sqrt(head_dim)

    @pl.when(step == 0)
    def _():
        key_rows = qkv_ref[:, width : 2 * width]
        keys_ref[...] = key_rows
        values_ref[...] = qkv_ref[:, 2 * width :]
        keys_t_ref[...] = key_rows.T
        grad_keys_ref[...] = jnp.zeros_like(grad_keys_ref)
        grad_values_ref[...] = jnp.zeros_like(grad_values_ref)
        d_bias_ref[...] = jnp.zeros_like(d_bias_ref)
        acc_ref[...] = jnp.zeros_like(acc_ref)

    start = pl.multiple_of(block * QUERY_ROWS, QUERY_ROWS)
    here = pl.ds(start, QUERY_ROWS)
    queries = qkv_ref[here, 0:width]
    logs = log_ref[...]
    grads = dot_nt(grad_branch, w_out_ref[...]).astype(BF16)

    def run(start_row, old_rows):
        grad_queries_ref[...] = attend_back_block(
            queries, grads, logs, keys_ref, keys_t_ref, values_ref, grad_keys_ref,
            grad_values_ref, start_row, old_rows, heads, head_dim, scale)

    @pl.when(jnp.logical_or(is_long == 0, block == 0))
    def _():
        run(start, 0)

    for position in range(1, blocks):

        @pl.when(jnp.logical_and(is_long == 1, block == position))
        def _(position=position):
            run(position * QUERY_ROWS, position * QUERY_ROWS)

    mixed = jnp.concatenate(
        [grad_queries_ref[...], grad_keys_ref[here, :] * scale, grad_values_ref[here, :]], axis=1
    ).astype(BF16)
    d_bias_ref[...] += jnp.sum(mixed.astype(F32), axis=0, keepdims=True)
    acc_ref[:, 0 : 3 * width] += dot_tn(first_ref[...], mixed)
    acc_ref[:, 3 * width :] += dot_tn(grad_branch, att_ref[...])

    @pl.when(step == steps - 1)
    def _():
        write_split(acc_ref, kept_ref, sent_ref, info_ref[5])

    return dot_nn(mixed, w_ref[...])


def last_norm_kernel(info_ref, x_ref, grad_a_ref, grad_b_ref, grad_residual_ref, gain_ref,
                     d_b_proj_ref, d_norm_two_ref, d_b_fc_ref, bias_own_ref, bias_other_ref,
                     grad_in_ref, near_ref, small_ref, sent_ref):
    step = pl.program_id(0)
    local = bias_own_ref.shape[1] // 3

    @pl.when(step == 0)
    def _():
        for target, row, bias_ref in ((small_ref, 0, bias_own_ref), (sent_ref, 1, bias_other_ref)):
            target[...] = jnp.zeros_like(target)
            target[0:1, :] = d_b_proj_ref[...]
            target[1:4, :] = d_norm_two_ref[0:3, :]
            target[6:7, :] = d_b_fc_ref[row : row + 1, :]
            target[7:8, 0 : 2 * local] = jnp.concatenate(
                [bias_ref[:, 0:local], bias_ref[:, 2 * local :]], axis=1
            )

    grad_first = grad_a_ref[...].astype(F32) + grad_b_ref[...].astype(F32)
    normed, inv_std = normalize(x_ref[...].astype(F32))
    grad_in = grad_residual_ref[...] + norm_back(grad_first, normed, inv_std, gain_ref[...])
    grad_low = grad_in.astype(BF16)
    grad_in_ref[...] = grad_low.astype(F32)

    @pl.when((step * x_ref.shape[0]) // info_ref[4] == info_ref[2])
    def _():
        near_ref[...] = grad_low

    gain_sum = jnp.sum(grad_first * normed, axis=0, keepdims=True)
    shift_sum = jnp.sum(grad_first, axis=0, keepdims=True)
    for target in (small_ref, sent_ref):
        target[4:5, :] += gain_sum
        target[5:6, :] += shift_sum


def block_value(residual_ref, mlp_a_ref, mlp_b_ref, bias_ref):
    total = residual_ref[...] + (mlp_a_ref[...].astype(F32) + mlp_b_ref[...].astype(F32))
    return (total + bias_ref[...]).astype(BF16)


def block_half_kernel(info_ref, residual_ref, mlp_a_ref, mlp_b_ref, bias_ref, out_ref):
    out_ref[...] = block_value(residual_ref, mlp_a_ref, mlp_b_ref, bias_ref)


def fill_kernel(info_ref, come_ref, whole_ref, out_ref):
    out_ref[...] = come_ref[...].astype(out_ref.dtype)


def row_spec(rows, width, shift=False):
    if shift:
        return pl.BlockSpec((rows, width), lambda step, info: (info[0] + step, 0))
    return pl.BlockSpec((rows, width), lambda step, info: (step, 0))


def back_spec(rows, width, blocks, shift=False):
    if shift:
        return pl.BlockSpec((rows, width), lambda step, info: (info[0] + blocks - 1 - step, 0))
    return pl.BlockSpec((rows, width), lambda step, info: (blocks - 1 - step, 0))


def whole(shape):
    return pl.BlockSpec(shape, lambda step, info: (0,) * len(shape))


def call(kernel, steps, in_specs, out_specs, out_shape, scratch, cost_us, aliases=None):
    return pl.pallas_call(
        kernel,
        grid_spec=pltpu.PrefetchScalarGridSpec(
            num_scalar_prefetch=1,
            grid=(steps,),
            in_specs=in_specs,
            out_specs=out_specs,
            scratch_shapes=scratch,
        ),
        out_shape=out_shape,
        input_output_aliases=aliases or {},
        compiler_params=pltpu.CompilerParams(
            dimension_semantics=("arbitrary",), vmem_limit_bytes=VMEM_BYTES
        ),
        cost_estimate=pl.CostEstimate(
            flops=int(cost_us * 1e9), transcendentals=0, bytes_accessed=int(cost_us * 3e6)
        ),
    )


def struct(shape, dtype):
    return jax.ShapeDtypeStruct(shape, dtype)


def exchange(value, axis_name, size, bit):
    return lax.ppermute(value, axis_name, [(i, i ^ bit) for i in range(size)])


def after(value, earlier):
    return lax.optimization_barrier((value, earlier))[0]


def make_body(dp_size, tensor_size):
    def body(hidden_in, doc_ids, ln1_gain, ln1_bias, w_qkv, b_qv, w_out, b_out, ln2_gain, ln2_bias,
             w_fc, b_fc, w_proj, b_proj, grad_out):
        row_count, width = hidden_in.shape
        heads, head_dim = w_qkv.shape[2:]
        local = heads * head_dim
        hidden = w_fc.shape[1]
        rows = row_count // 2
        blocks = rows // QUERY_ROWS
        half = rows // 2
        place = lax.axis_index("tensor")
        bits = dp_size.bit_length() - 1
        position = lax.axis_index("dp")
        share = width // dp_size
        first_bit = next(bit for bit in range(bits) if (share << bit) % 16 == 0)
        second_bit = min(first_bit + 1, bits - 1)
        upper = place // 2
        core = place % 2
        is_long = (doc_ids[SHORT_LEN] == doc_ids[0]).astype(jnp.int32)
        info = jnp.stack(
            [upper * blocks, is_long, core, (1 - upper) * blocks, half,
             (position >> first_bit) & 1, (position >> second_bit) & 1]
        ).astype(jnp.int32)

        def core_swap(value):
            return exchange(value, "tensor", tensor_size, 1)

        def pair_swap(value):
            return exchange(value, "tensor", tensor_size, 2)

        qkv_own = w_qkv.transpose(1, 2, 3, 0).reshape(3 * local, width)
        out_own = w_out.reshape(local, width)
        bias_own = b_qv.reshape(2, local)
        small_other = pair_swap(
            jnp.concatenate([b_qv.reshape(1, 2 * local), b_fc.reshape(1, hidden)], axis=1)
        )

        def my_piece(matrix):
            rows_each = matrix.shape[0] // dp_size
            return lax.dynamic_slice_in_dim(matrix, position * rows_each, rows_each, axis=0)[None]

        def widen(kept, come, bit):
            mine = (position >> bit) & 1
            return tuple(
                jnp.where(mine == 0, jnp.stack([a, b], 1), jnp.stack([b, a], 1)).reshape(
                    (2 * a.shape[0],) + a.shape[1:]
                )
                for a, b in zip(kept, come)
            )

        def dp_swap(values, bit):
            return tuple(exchange(value, "dp", dp_size, 1 << bit) for value in values)

        parts = tuple(pair_swap(my_piece(matrix)) for matrix in (w_proj, w_fc[width // 2 :]))
        out_other = pair_swap(out_own)
        qkv_other = pair_swap(qkv_own)
        fc_top = pair_swap(w_fc[: width // 2])
        come = dp_swap(parts, bits - 1)
        come, hidden_in = lax.optimization_barrier((come, hidden_in))
        parts = widen(parts, come, bits - 1)
        come = dp_swap(parts, bits - 2)

        first_spec = row_spec(QUERY_ROWS, width)
        qkv_spec = row_spec(QUERY_ROWS, 3 * local)
        att_spec = row_spec(QUERY_ROWS, local)
        log_spec = pl.BlockSpec((8, QUERY_ROWS), lambda step, info: (0, step))
        attend_scratch = [pltpu.VMEM((rows, local), BF16), pltpu.VMEM((local, rows), BF16)]

        def forward_own(*refs):
            forward_own_kernel(heads, head_dim, *refs)

        def forward_other(*refs):
            forward_other_kernel(heads, head_dim, *refs)

        first_in, mix_own, att_own, log_own = call(
            forward_own,
            blocks,
            [row_spec(QUERY_ROWS, width, True), whole((width,)), whole((width,)),
             whole((3 * local, width)), whole((2, local))],
            [first_spec, qkv_spec, att_spec, log_spec],
            [struct((rows, width), BF16), struct((rows, 3 * local), BF16),
             struct((rows, local), BF16), struct((8, rows), F32)],
            attend_scratch,
            11,
        )(info, hidden_in, ln1_gain, ln1_bias, qkv_own, bias_own)
        come, small_other = after((come, small_other), first_in)
        parts = widen(parts, come, bits - 2)
        for bit in reversed(range(bits - 2)):
            come = dp_swap(parts, bit)
            if bit:
                first_in = after(first_in, come)
            parts = widen(parts, come, bit)
        proj_other = parts[0].reshape(hidden, width)
        fc_low = parts[1].reshape(width // 2, hidden)
        bias_other = small_other[:, : 2 * local].reshape(2, local)
        b_fc_both = jnp.concatenate([b_fc.reshape(1, hidden), small_other[:, 2 * local :]], axis=0)
        mix_other, att_other, log_other, branch = call(
            forward_other,
            blocks,
            [first_spec, whole((3 * local, width)), whole((2, local)), att_spec,
             whole((local, width)), whole((local, width))],
            [qkv_spec, att_spec, log_spec, first_spec],
            [struct((rows, 3 * local), BF16), struct((rows, local), BF16),
             struct((8, rows), F32), struct((rows, width), BF16)],
            attend_scratch,
            12,
        )(info, first_in, qkv_other, bias_other, att_own, out_own, out_other)
        branch_swapped = core_swap(branch)

        def split_shape(bit, lead=()):
            runs = dp_size >> bit
            return lead + (runs // 2, share << bit, width)

        fc_shape = split_shape(first_bit, (2,))
        proj_shape = split_shape(second_bit, (2,))
        att_shape = split_shape(first_bit)
        (residual, mlp, grad_second, fc_kept, fc_sent, proj_kept, proj_sent, d_b_fc,
         d_b_proj) = call(
            mlp_kernel,
            blocks,
            [row_spec(QUERY_ROWS, width, True), first_spec, first_spec, whole((width,)),
             whole((width,)), whole((width,)), row_spec(QUERY_ROWS, width, True),
             whole((width, hidden)), whole((width // 2, hidden)), whole((width // 2, hidden)),
             whole((hidden, width)), whole((hidden, width)), whole((2, hidden))],
            [first_spec, first_spec, first_spec] + [whole(fc_shape)] * 2 + [whole(proj_shape)] * 2
            + [whole((2, hidden)), whole((1, width))],
            [struct((rows, width), F32), struct((rows, width), BF16), struct((rows, width), BF16),
             struct(fc_shape, BF16), struct(fc_shape, BF16), struct(proj_shape, BF16),
             struct(proj_shape, BF16),
             struct((2, hidden), F32), struct((1, width), F32)],
            [pltpu.VMEM((width, hidden), F32)] + [pltpu.VMEM((width, rows), BF16)] * 2 + [pltpu.VMEM((rows, hidden), BF16)] * 4,
            28,
        )(info, hidden_in, branch, branch_swapped, b_out, ln2_gain,
          ln2_bias, grad_out, w_fc, fc_top, fc_low, w_proj, proj_other, b_fc_both)
        grad_swapped = core_swap(grad_second)
        mlp_swapped = core_swap(mlp)

        half_spec = pl.BlockSpec(
            (QUERY_ROWS, width), lambda step, info: (info[2] * (half // QUERY_ROWS) + step, 0)
        )
        block_half = call(
            block_half_kernel,
            half // QUERY_ROWS,
            [half_spec, half_spec, half_spec, whole((width,))],
            first_spec,
            struct((half, width), BF16),
            [],
            3,
        )(info, residual, mlp, mlp_swapped, b_proj)
        block_near = pair_swap(block_half)

        back_rows = back_spec(QUERY_ROWS, width, blocks)
        back_att = back_spec(QUERY_ROWS, local, blocks)
        back_log = pl.BlockSpec((8, QUERY_ROWS), lambda step, info: (0, blocks - 1 - step))
        back_scratch = [
            pltpu.VMEM((width, 4 * local), F32),
            pltpu.VMEM((local, rows), BF16),
            pltpu.VMEM((rows, local), BF16),
            pltpu.VMEM((rows, local), BF16),
            pltpu.VMEM((rows, local), F32),
            pltpu.VMEM((rows, local), F32),
            pltpu.VMEM((QUERY_ROWS, local), F32),
        ]

        def backward_other(*refs):
            backward_other_kernel(heads, head_dim, *refs)

        def backward_own(*refs):
            backward_own_kernel(heads, head_dim, *refs)

        (grad_residual, grad_branch, grad_first_other, far_kept, far_sent, d_bias_other,
         d_norm_two, block_out) = call(
            backward_other,
            blocks,
            [back_rows, back_rows, back_rows, back_spec(QUERY_ROWS, width, blocks, True),
             whole((width,)), back_rows, back_rows, whole((width,)), back_rows,
             whole((rows, 3 * local)), back_att, back_log, whole((3 * local, width)),
             whole((local, width))],
            [back_rows, back_rows, back_rows, whole(att_shape), whole(att_shape),
             whole((1, 3 * local)), whole((8, width)),
             back_spec(QUERY_ROWS, width, blocks, True)],
            [struct((rows, width), F32), struct((rows, width), BF16), struct((rows, width), F32),
             struct(att_shape, BF16), struct(att_shape, BF16), struct((1, 3 * local), F32),
             struct((8, width), F32), struct((row_count, width), BF16)],
            back_scratch,
            21,
        )(info, grad_second, grad_swapped, residual, grad_out, ln2_gain, mlp, mlp_swapped, b_proj,
          first_in,
          mix_other, att_other, log_other, qkv_other, out_other)
        grad_first, near_kept, near_sent, d_bias_own = call(
            backward_own,
            blocks,
            [back_rows, back_rows, back_rows, whole((rows, 3 * local)), back_att, back_log,
             whole((3 * local, width)), whole((local, width))],
            [back_rows, whole(att_shape), whole(att_shape), whole((1, 3 * local))],
            [struct((rows, width), BF16), struct(att_shape, BF16), struct(att_shape, BF16),
             struct((1, 3 * local), F32)],
            back_scratch,
            17,
        )(info, grad_branch, grad_first_other, first_in, mix_own, att_own, log_own, qkv_own,
          out_own)
        first_swapped = core_swap(grad_first)
        quarter = half // QUERY_ROWS
        small_spec = whole((8, width))
        grad_in, grad_half, small, small_sent = call(
            last_norm_kernel,
            blocks,
            [row_spec(QUERY_ROWS, width, True), first_spec, first_spec, first_spec,
             whole((width,)), whole((1, width)), small_spec, whole((2, hidden)),
             whole((1, 3 * local)), whole((1, 3 * local))],
            [row_spec(QUERY_ROWS, width, True),
             pl.BlockSpec((QUERY_ROWS, width), lambda step, info: (
                jnp.clip(step - quarter * info[2], 0, quarter - 1), 0)),
             small_spec, small_spec],
            [struct((row_count, width), F32), struct((half, width), BF16),
             struct((8, width), F32), struct((8, width), F32)],
            [],
            7,
        )(info, hidden_in, grad_first, first_swapped, grad_residual, ln1_gain, d_b_proj,
          d_norm_two, d_b_fc, d_bias_own, d_bias_other)
        small_come = pair_swap(small_sent)
        grad_near = pair_swap(grad_half)

        def fill(target, come, part):
            def index(step, info):
                first = jnp.where(part == 0, info[2], 1 - info[2]) * quarter
                return info[3] + first + step, 0

            return call(
                fill_kernel,
                quarter,
                [first_spec, pl.BlockSpec(memory_space=pl.ANY)],
                pl.BlockSpec((QUERY_ROWS, width), index),
                struct(target.shape, target.dtype),
                [],
                2,
                {2: 0},
            )(info, come, target)

        block_far = core_swap(block_near)
        block_near, block_far = after((block_near, block_far), grad_half)
        block_out = fill(fill(block_out, block_near, 0), block_far, 1)
        grad_far = core_swap(grad_near)
        grad_in = fill(fill(grad_in, grad_near, 0), grad_far, 1)

        def pick(value, axis, which):
            return lax.dynamic_index_in_dim(value, which, axis, keepdims=False)

        def parted(value, lead=()):
            return value.reshape(lead + (2,) * (bits - 1) + (share, width))

        def add(kept, received):
            return kept.astype(F32) + received.astype(F32)

        def others(bit):
            return [b for b in range(bits) if b != bit]

        def stages(value, left):
            for number, bit in enumerate(left):
                above = len([b for b in left[number:] if b > bit])
                mine = (position >> bit) & 1
                received = exchange(
                    pick(value, above, 1 - mine).astype(BF16), "dp", dp_size, 1 << bit
                )
                if number == 0:
                    received = after(received, grad_half)
                value = add(pick(value, above, mine), received)
            return value

        got_fc = exchange(fc_sent, "dp", dp_size, 1 << first_bit)
        got_proj = exchange(proj_sent, "dp", dp_size, 1 << second_bit)
        got_far = exchange(far_sent, "dp", dp_size, 1 << first_bit)
        got_fc, got_proj = after((got_fc, got_proj), grad_branch)
        half_fc = add(fc_kept, got_fc)
        half_proj = add(proj_kept, got_proj)
        come_fc = pair_swap(half_fc[1].astype(BF16))
        come_proj = pair_swap(half_proj[1].astype(BF16))
        got_near = exchange(near_sent, "dp", dp_size, 1 << first_bit)
        got_far = after(got_far, grad_first)
        come_far = pair_swap(add(far_kept, got_far).astype(BF16))
        come_fc, come_proj = after((come_fc, come_proj), grad_first)
        come_far, got_near = after((come_far, got_near), grad_half)
        fc_share = stages(parted(add(half_fc[0], come_fc)), others(first_bit))
        proj_share = stages(parted(add(half_proj[0], come_proj)), others(second_bit))
        att_half = parted(add(add(near_kept, got_near), come_far))
        att_share = stages(att_half, others(first_bit))
        small = small + small_come
        for bit in range(bits):
            small = small + exchange(small, "dp", dp_size, 1 << bit)
        shares = lax.dynamic_index_in_dim(
            small[0:6].reshape(6, dp_size, share), position, 1, keepdims=False
        )
        d_b_proj_share, d_gain_two, d_shift_two, d_b_out, d_gain_one, d_shift_one = (
            shares[i] for i in range(6)
        )
        fc_rows, fc_columns = b_fc.shape
        d_b_fc_share = lax.dynamic_slice_in_dim(
            small[6].reshape(fc_rows, fc_columns), position * (fc_columns // dp_size),
            fc_columns // dp_size, axis=1,
        )
        d_b_qv_share = lax.dynamic_slice_in_dim(
            small[7, : 2 * local].reshape(2, heads, head_dim), position * (head_dim // dp_size),
            head_dim // dp_size, axis=2,
        )
        att_turned = att_share.T
        d_w_qkv = att_turned[: 3 * local].reshape(3, heads, head_dim, share).transpose(3, 0, 1, 2)
        d_w_out = att_turned[3 * local :].reshape(heads, head_dim, share)
        return (block_out, grad_in, d_gain_one, d_shift_one, d_w_qkv, d_b_qv_share, d_w_out,
                d_b_out, d_gain_two, d_shift_two, fc_share, d_b_fc_share, proj_share.T,
                d_b_proj_share)

    return body


def solution(mesh):
    in_specs = (
        P("dp", None),
        P("dp"),
        P(),
        P(),
        P(None, None, "tensor", None),
        P(None, "tensor", None),
        P("tensor", None, None),
        P(),
        P(),
        P(),
        P(None, "tensor"),
        P("tensor", None),
        P("tensor", None),
        P(),
        P("dp", None),
    )
    out_specs = (
        P("dp", None),
        P("dp", None),
        P("dp"),
        P("dp"),
        P("dp", None, "tensor", None),
        P(None, "tensor", "dp"),
        P("tensor", None, "dp"),
        P("dp"),
        P("dp"),
        P("dp"),
        P("dp", "tensor"),
        P("tensor", "dp"),
        P("tensor", "dp"),
        P("dp"),
    )
    inner = make_body(mesh.shape["dp"], mesh.shape["tensor"])

    return jax.shard_map(inner, mesh=mesh, in_specs=in_specs, out_specs=out_specs, check_vma=False)
```

```python
import math

import jax
import jax.numpy as jnp
from jax import lax
from jax.experimental import pallas as pl
from jax.experimental.pallas import tpu as pltpu
from jax.sharding import PartitionSpec as P


EPSILON = 1e-05
MASKED = -1e30
QUERY_ROWS = 256
SHORT_LEN = 256
BF16 = jnp.bfloat16
F32 = jnp.float32
VMEM_BYTES = 60 * 1024 * 1024


def dot_nn(left, right):
    return lax.dot_general(left, right, (((1,), (0,)), ((), ())), preferred_element_type=F32)


def dot_nt(left, right):
    return lax.dot_general(left, right, (((1,), (1,)), ((), ())), preferred_element_type=F32)


def normalize(values):
    row_mean = jnp.mean(values, axis=-1, keepdims=True)
    centered = values - row_mean
    inv_std = lax.rsqrt(jnp.mean(centered * centered, axis=-1, keepdims=True) + EPSILON)
    return (centered * inv_std, inv_std)


def norm_back(grad_normed, normed, inv_std, gain_vec):
    scaled = grad_normed * gain_vec
    return inv_std * (
        scaled
        - jnp.mean(scaled, axis=-1, keepdims=True)
        - normed * jnp.mean(scaled * normed, axis=-1, keepdims=True)
    )


def head_lanes(values, head, head_dim):
    per_group = 128 // head_dim
    first = (head // per_group) * 128
    group = values[:, first : min(first + 128, values.shape[1])]
    if group.shape[1] == head_dim:
        return group
    lane = lax.broadcasted_iota(jnp.int32, group.shape, 1)
    inside = (lane // head_dim) == (head % per_group)
    return jnp.where(inside, group, jnp.zeros_like(group))


def group_lanes(head, head_dim, width):
    per_group = 128 // head_dim
    first = (head // per_group) * 128
    return slice(first, min(first + 128, width))


def allowed_diagonal():
    key_pos = lax.broadcasted_iota(jnp.int32, (QUERY_ROWS, QUERY_ROWS), 0)
    row_pos = lax.broadcasted_iota(jnp.int32, (QUERY_ROWS, QUERY_ROWS), 1)
    return key_pos <= row_pos


def attend_block(queries, keys_ref, values_t_ref, start, old_blocks, heads, head_dim):
    width = heads * head_dim
    query_parts = [head_lanes(queries, head, head_dim) for head in range(heads)]

    def scores_of(head, rows):
        return dot_nt(keys_ref[rows, group_lanes(head, head_dim, width)], query_parts[head])

    def weighted(head, rows, weights):
        values_t = values_t_ref[head * head_dim : (head + 1) * head_dim, rows]
        return dot_nn(values_t, weights.astype(BF16))

    here = pl.ds(start, QUERY_ROWS)
    allowed = allowed_diagonal()
    state = []
    for head in range(heads):
        scores = jnp.where(allowed, scores_of(head, here), MASKED)
        row_max = jnp.max(scores, axis=0, keepdims=True)
        weights = jnp.exp(scores - row_max)
        state.append((row_max, jnp.sum(weights, axis=0, keepdims=True),
                      weighted(head, here, weights)))

    def old_block(index, state):
        rows = pl.ds(pl.multiple_of(index * QUERY_ROWS, QUERY_ROWS), QUERY_ROWS)
        result = []
        for head, (row_max, total, summed) in enumerate(state):
            scores = scores_of(head, rows)
            new_max = jnp.maximum(row_max, jnp.max(scores, axis=0, keepdims=True))
            weights = jnp.exp(scores - new_max)
            shrink = jnp.exp(row_max - new_max)
            result.append((new_max, total * shrink + jnp.sum(weights, axis=0, keepdims=True),
                           summed * shrink + weighted(head, rows, weights)))
        return tuple(result)

    state = lax.fori_loop(0, old_blocks, old_block, tuple(state))
    attended = jnp.concatenate([summed / total for _, total, summed in state], axis=0).T
    return attended, [row_max + jnp.log(total) for row_max, total, _ in state]


def attend_body(
    heads, head_dim, block, first_in, w_ref, bias_ref, mix_refs, att_ref, log_ref, keys_ref,
    values_t_ref, is_long,
):
    width = heads * head_dim
    projected = dot_nt(first_in, w_ref[...])
    queries = (projected[:, :width] + bias_ref[0:1, :]).astype(BF16)
    key_rows = projected[:, width : 2 * width].astype(BF16)
    value_rows = (projected[:, 2 * width :] + bias_ref[1:2, :]).astype(BF16)
    query_ref, key_ref, value_ref, keys_t_ref = mix_refs
    query_ref[...] = queries
    key_ref[...] = key_rows
    value_ref[...] = value_rows
    keys_t_ref[...] = key_rows.T
    start = pl.multiple_of(block * QUERY_ROWS, QUERY_ROWS)
    keys_ref[pl.ds(start, QUERY_ROWS), :] = key_rows
    values_t_ref[:, pl.ds(start, QUERY_ROWS)] = value_rows.T
    scaled = queries * jnp.asarray(1.0 / math.sqrt(head_dim), BF16)

    attended, logs = attend_block(
        scaled, keys_ref, values_t_ref, start, block * is_long, heads, head_dim
    )
    att_ref[...] = attended.astype(BF16)
    log_ref[...] = jnp.concatenate(logs + [jnp.zeros((8 - heads, QUERY_ROWS), F32)], axis=0)


def forward_own_kernel(heads, head_dim, info_ref, x_ref, gain_ref, shift_ref, w_ref, bias_ref,
                       first_ref, first_t_ref, query_ref, key_ref, value_ref, keys_t_ref, att_ref,
                       log_ref, keys_ref, values_t_ref):
    normed, _ = normalize(x_ref[...].astype(F32))
    first_in = (normed * gain_ref[...] + shift_ref[...]).astype(BF16)
    first_ref[...] = first_in
    first_t_ref[...] = first_in.T
    attend_body(heads, head_dim, pl.program_id(0), first_in, w_ref, bias_ref,
                (query_ref, key_ref, value_ref, keys_t_ref), att_ref, log_ref, keys_ref,
                values_t_ref, info_ref[1])


def forward_other_kernel(heads, head_dim, info_ref, first_ref, w_ref, bias_ref, att_own_ref,
                         w_out_own_ref, w_out_ref, query_ref, key_ref, value_ref, keys_t_ref,
                         att_ref, log_ref, branch_ref, keys_ref, values_t_ref):
    attend_body(heads, head_dim, pl.program_id(0), first_ref[...], w_ref, bias_ref,
                (query_ref, key_ref, value_ref, keys_t_ref), att_ref, log_ref, keys_ref,
                values_t_ref, info_ref[1])
    branch = dot_nn(att_own_ref[...], w_out_own_ref[...]) + dot_nn(att_ref[...], w_out_ref[...])
    branch_ref[...] = branch.astype(BF16)


def write_split(source_ref, kept_ref, sent_ref, mine, part=None):
    run = kept_ref.shape[-2]
    count = kept_ref.shape[-3]
    for value in range(2):

        @pl.when(mine == value)
        def _(value=value):
            for index in range(2 * count):
                target = kept_ref if index % 2 == value else sent_ref
                piece = source_ref[index * run : (index + 1) * run, :].astype(BF16)
                if part is None:
                    target[index // 2] = piece
                else:
                    target[part, index // 2] = piece


def mlp_kernel(info_ref, x_ref, branch_a_ref, branch_b_ref, b_out_ref, gain_ref, shift_ref, go_ref,
               fc_own_ref, fc_top_ref, fc_low_ref, proj_own_ref, proj_other_ref, b_fc_ref,
               residual_ref, mlp_ref, grad_ref, fc_kept_ref, fc_sent_ref, proj_kept_ref,
               proj_sent_ref, d_b_fc_ref, d_b_proj_ref,
               in_t_ref, go_t_ref, pre_own_ref, pre_other_ref, act_own_ref, act_other_ref):
    step = pl.program_id(0)
    rows = x_ref.shape[0]

    @pl.when(step == 0)
    def _():
        d_b_fc_ref[...] = jnp.zeros_like(d_b_fc_ref)
        d_b_proj_ref[...] = jnp.zeros_like(d_b_proj_ref)

    residual = x_ref[...].astype(F32) + (
        branch_a_ref[...].astype(F32) + branch_b_ref[...].astype(F32) + b_out_ref[...]
    )
    residual_ref[...] = residual
    normed, _ = normalize(residual)
    second_in = (normed * gain_ref[...] + shift_ref[...]).astype(BF16)
    grad_out = go_ref[...]
    here = pl.ds(pl.multiple_of(step * rows, rows), rows)
    in_t_ref[:, here] = second_in.T
    go_t_ref[:, here] = grad_out.T

    d_b_proj_ref[...] += jnp.sum(grad_out.astype(F32), axis=0, keepdims=True)
    mlp = None
    grad_second = None
    grad_acts = [dot_nt(grad_out, ref[...]) for ref in (proj_own_ref, proj_other_ref)]
    parts = (
        ((fc_own_ref,), proj_own_ref, pre_own_ref, act_own_ref),
        ((fc_top_ref, fc_low_ref), proj_other_ref, pre_other_ref, act_other_ref),
    )
    slope = math.sqrt(2.0 / math.pi)
    for part, (fc_refs, proj_ref, pre_ref, act_ref) in enumerate(parts):
        pre_act = b_fc_ref[part : part + 1, :]
        first = 0
        for fc_ref in fc_refs:
            last = first + fc_ref.shape[0]
            pre_act = pre_act + dot_nn(second_in[:, first:last], fc_ref[...])
            first = last
        square = pre_act * pre_act
        bent = jnp.tanh(pre_act * (slope + (0.044715 * slope) * square))
        half = 0.5 + 0.5 * bent
        act_low = (pre_act * half).astype(BF16)
        act_ref[here, :] = act_low
        part_out = dot_nn(act_low, proj_ref[...])
        grad_act = grad_acts[part]
        rise = pre_act * (2.0 * slope + (6.0 * 0.044715 * slope) * square)
        derivative = half + half * ((1.0 - half) * rise)
        grad_pre = (grad_act * derivative).astype(BF16)
        pre_ref[here, :] = grad_pre
        d_b_fc_ref[part : part + 1, :] += jnp.sum(grad_pre.astype(F32), axis=0, keepdims=True)
        part_grad = jnp.concatenate([dot_nt(grad_pre, fc_ref[...]) for fc_ref in fc_refs], axis=1)
        mlp = part_out if mlp is None else mlp + part_out
        grad_second = part_grad if grad_second is None else grad_second + part_grad
    mlp_ref[...] = mlp.astype(BF16)
    grad_ref[...] = grad_second.astype(BF16)

    @pl.when(step == pl.num_programs(0) - 1)
    def _():
        for part, (act_ref, pre_ref) in enumerate(
            ((act_own_ref, pre_own_ref), (act_other_ref, pre_other_ref))
        ):
            write_split(dot_nn(in_t_ref[...], pre_ref[...]).astype(BF16), fc_kept_ref,
                        fc_sent_ref, info_ref[5], part)
            write_split(dot_nn(go_t_ref[...], act_ref[...]).astype(BF16), proj_kept_ref,
                        proj_sent_ref, info_ref[6], part)


def attend_back_block(queries, grads, attended, logs, keys_ref, keys_t_ref, values_ref,
                      grad_keys_ref, grad_values_ref, start, old_blocks, heads, head_dim, scale):
    width = heads * head_dim
    query_parts = [head_lanes(queries, head, head_dim) for head in range(heads)]
    scaled_parts = [query * jnp.asarray(scale, BF16) for query in query_parts]
    grad_parts = [head_lanes(grads, head, head_dim) for head in range(heads)]
    product = grads.astype(F32) * attended.astype(F32)
    high = product.astype(BF16)
    low = (product - high.astype(F32)).astype(BF16)
    member = (
        lax.broadcasted_iota(jnp.int32, (8, width), 1) // head_dim
        == lax.broadcasted_iota(jnp.int32, (8, width), 0)
    )
    member = jnp.where(member, 1.0, 0.0).astype(BF16)
    deltas = dot_nt(member, high) + dot_nt(member, low)

    def through(rows, allowed):
        results = []
        for head in range(heads):
            lanes = group_lanes(head, head_dim, width)
            scores = dot_nt(keys_ref[rows, lanes], scaled_parts[head])
            weights = jnp.exp(scores - logs[head : head + 1, :])
            if allowed is not None:
                weights = jnp.where(allowed, weights, 0.0)
            grad_weights = dot_nt(values_ref[rows, lanes], grad_parts[head])
            grad_scores = (weights * (grad_weights - deltas[head : head + 1, :])).astype(BF16)
            grad_keys_ref[rows, lanes] += dot_nn(grad_scores, query_parts[head])
            grad_values_ref[rows, lanes] += dot_nn(weights.astype(BF16), grad_parts[head])
            keys_t = keys_t_ref[head * head_dim : (head + 1) * head_dim, rows]
            results.append(dot_nn(keys_t, grad_scores))
        return tuple(results)

    def old_block(index, sums):
        rows = pl.ds(pl.multiple_of(index * QUERY_ROWS, QUERY_ROWS), QUERY_ROWS)
        return tuple(old + new for old, new in zip(sums, through(rows, None)))

    sums = through(pl.ds(start, QUERY_ROWS), allowed_diagonal())
    sums = lax.fori_loop(0, old_blocks, old_block, sums)
    return jnp.concatenate(sums, axis=0).T * scale


def backward_other_kernel(heads, head_dim, info_ref, grad_a_ref, grad_b_ref, residual_ref, go_ref,
                          gain_ref, mlp_a_ref, mlp_b_ref, b_proj_ref, query_ref, key_ref, value_ref,
                          keys_t_ref, att_ref, log_ref, w_ref, w_out_ref, first_t_hbm,
                          grad_residual_ref, grad_branch_ref, grad_branch_t_ref, grad_first_ref,
                          kept_ref, sent_ref, d_bias_ref, d_norm_ref, block_ref,
                          first_t_ref, mixed_ref, grad_keys_ref, grad_values_ref, copy_sem):
    step = pl.program_id(0)
    copies = (pltpu.make_async_copy(first_t_hbm, first_t_ref, copy_sem.at[0]),)

    @pl.when(step == 0)
    def _():
        copies[0].start()
        d_norm_ref[...] = jnp.zeros_like(d_norm_ref)
        grad_keys_ref[...] = jnp.zeros_like(grad_keys_ref)
        grad_values_ref[...] = jnp.zeros_like(grad_values_ref)
        d_bias_ref[...] = jnp.zeros_like(d_bias_ref)

    rows = grad_a_ref.shape[0]
    block = pl.num_programs(0) - 1 - step
    here = pl.ds(pl.multiple_of(block * rows, rows), rows)
    grad_second = grad_a_ref[...].astype(F32) + grad_b_ref[...].astype(F32)
    normed, inv_std = normalize(residual_ref[...])
    grad_residual = go_ref[...].astype(F32) + norm_back(grad_second, normed, inv_std, gain_ref[...])
    grad_residual_ref[...] = grad_residual
    block_ref[...] = block_value(residual_ref, mlp_a_ref, mlp_b_ref, b_proj_ref)
    grad_branch = grad_residual.astype(BF16)
    grad_branch_ref[...] = grad_branch
    grad_branch_t_ref[:, here] = grad_branch.T
    d_norm_ref[0:1, :] += jnp.sum(grad_second * normed, axis=0, keepdims=True)
    d_norm_ref[1:2, :] += jnp.sum(grad_second, axis=0, keepdims=True)
    d_norm_ref[2:3, :] += jnp.sum(grad_branch.astype(F32), axis=0, keepdims=True)
    grad_first_ref[...] = attend_back(
        heads, head_dim, grad_branch, query_ref, key_ref, value_ref, keys_t_ref, att_ref, log_ref,
        w_ref, w_out_ref, d_bias_ref, mixed_ref, grad_keys_ref, grad_values_ref, info_ref[1])
    weight_grads(copies, first_t_ref, grad_branch_t_ref, mixed_ref, att_ref,
                 kept_ref, sent_ref, info_ref[5])


def backward_own_kernel(heads, head_dim, info_ref, grad_branch_ref, grad_first_in_ref, query_ref,
                        key_ref, value_ref, keys_t_ref, att_ref, log_ref, w_ref, w_out_ref,
                        first_t_hbm, grad_branch_t_hbm, grad_first_ref, kept_ref, sent_ref,
                        d_bias_ref, first_t_ref, grad_branch_t_ref, mixed_ref, grad_keys_ref,
                        grad_values_ref, copy_sem):
    copies = (
        pltpu.make_async_copy(first_t_hbm, first_t_ref, copy_sem.at[0]),
        pltpu.make_async_copy(grad_branch_t_hbm, grad_branch_t_ref, copy_sem.at[1]),
    )

    @pl.when(pl.program_id(0) == 0)
    def _():
        for copy in copies:
            copy.start()
        grad_keys_ref[...] = jnp.zeros_like(grad_keys_ref)
        grad_values_ref[...] = jnp.zeros_like(grad_values_ref)
        d_bias_ref[...] = jnp.zeros_like(d_bias_ref)

    grad_first = attend_back(
        heads, head_dim, grad_branch_ref[...], query_ref, key_ref, value_ref, keys_t_ref, att_ref,
        log_ref, w_ref, w_out_ref, d_bias_ref, mixed_ref, grad_keys_ref, grad_values_ref,
        info_ref[1])
    grad_first_ref[...] = (grad_first + grad_first_in_ref[...]).astype(BF16)
    weight_grads(copies, first_t_ref, grad_branch_t_ref, mixed_ref, att_ref,
                 kept_ref, sent_ref, info_ref[5])


def attend_back(heads, head_dim, grad_branch, query_ref, key_ref, value_ref, keys_t_ref, att_ref,
                log_ref, w_ref, w_out_ref, d_bias_ref, mixed_ref, grad_keys_ref, grad_values_ref,
                is_long):
    blocks = key_ref.shape[0] // QUERY_ROWS
    block = blocks - 1 - pl.program_id(0)
    scale = 1.0 / math.sqrt(head_dim)
    start = pl.multiple_of(block * QUERY_ROWS, QUERY_ROWS)
    here = pl.ds(start, QUERY_ROWS)
    grads = dot_nt(grad_branch, w_out_ref[...]).astype(BF16)
    grad_queries = attend_back_block(
        query_ref[...], grads, att_ref[here, :], log_ref[...], key_ref, keys_t_ref, value_ref,
        grad_keys_ref, grad_values_ref, start, block * is_long, heads, head_dim, scale)
    mixed = jnp.concatenate(
        [grad_queries.astype(BF16), (grad_keys_ref[here, :] * scale).astype(BF16),
         grad_values_ref[here, :].astype(BF16)], axis=1
    )
    mixed_ref[here, :] = mixed
    d_bias_ref[...] += jnp.sum(mixed.astype(F32), axis=0, keepdims=True)
    return dot_nn(mixed, w_ref[...])


def weight_grads(copies, first_t_ref, grad_branch_t_ref, mixed_ref, att_ref, kept_ref,
                 sent_ref, mine):
    @pl.when(pl.program_id(0) == pl.num_programs(0) - 1)
    def _():
        for copy in copies:
            copy.wait()
        total = jnp.concatenate(
            [dot_nn(first_t_ref[...], mixed_ref[...]).astype(BF16),
             dot_nn(grad_branch_t_ref[...], att_ref[...]).astype(BF16)], axis=1
        )
        write_split(total, kept_ref, sent_ref, mine)


def last_norm_kernel(info_ref, x_ref, grad_a_ref, grad_b_ref, grad_residual_ref, gain_ref,
                     d_b_proj_ref, d_norm_two_ref, d_b_fc_ref, bias_own_ref, bias_other_ref,
                     grad_in_ref, near_ref, small_ref, sent_ref):
    step = pl.program_id(0)
    local = bias_own_ref.shape[1] // 3

    @pl.when(step == 0)
    def _():
        for target, row, bias_ref in ((small_ref, 0, bias_own_ref), (sent_ref, 1, bias_other_ref)):
            target[...] = jnp.zeros_like(target)
            target[0:1, :] = d_b_proj_ref[...]
            target[1:4, :] = d_norm_two_ref[0:3, :]
            target[6:7, :] = d_b_fc_ref[row : row + 1, :]
            target[7:8, 0 : 2 * local] = jnp.concatenate(
                [bias_ref[:, 0:local], bias_ref[:, 2 * local :]], axis=1
            )

    grad_first = grad_a_ref[...].astype(F32) + grad_b_ref[...].astype(F32)
    normed, inv_std = normalize(x_ref[...].astype(F32))
    grad_in = grad_residual_ref[...] + norm_back(grad_first, normed, inv_std, gain_ref[...])
    grad_low = grad_in.astype(BF16)
    grad_in_ref[...] = grad_low.astype(F32)

    @pl.when((step * x_ref.shape[0]) // info_ref[4] == info_ref[2])
    def _():
        near_ref[...] = grad_low

    gain_sum = jnp.sum(grad_first * normed, axis=0, keepdims=True)
    shift_sum = jnp.sum(grad_first, axis=0, keepdims=True)
    for target in (small_ref, sent_ref):
        target[4:5, :] += gain_sum
        target[5:6, :] += shift_sum


def block_value(residual_ref, mlp_a_ref, mlp_b_ref, bias_ref):
    total = residual_ref[...] + (mlp_a_ref[...].astype(F32) + mlp_b_ref[...].astype(F32))
    return (total + bias_ref[...]).astype(BF16)


def block_half_kernel(info_ref, residual_ref, mlp_a_ref, mlp_b_ref, bias_ref, out_ref):
    out_ref[...] = block_value(residual_ref, mlp_a_ref, mlp_b_ref, bias_ref)


def fill_both_kernel(info_ref, near_ref, far_ref, whole_ref, out_ref):
    from_near = (pl.program_id(0) * near_ref.shape[0]) // info_ref[4] == info_ref[2]
    out_ref[...] = jnp.where(from_near, near_ref[...], far_ref[...]).astype(out_ref.dtype)


def row_spec(rows, width, shift=False):
    if shift:
        return pl.BlockSpec((rows, width), lambda step, info: (info[0] + step, 0))
    return pl.BlockSpec((rows, width), lambda step, info: (step, 0))


def back_spec(rows, width, blocks, shift=False):
    if shift:
        return pl.BlockSpec((rows, width), lambda step, info: (info[0] + blocks - 1 - step, 0))
    return pl.BlockSpec((rows, width), lambda step, info: (blocks - 1 - step, 0))


def whole(shape):
    return pl.BlockSpec(shape, lambda step, info: (0,) * len(shape))


def call(kernel, steps, in_specs, out_specs, out_shape, scratch, cost_us, aliases=None):
    return pl.pallas_call(
        kernel,
        grid_spec=pltpu.PrefetchScalarGridSpec(
            num_scalar_prefetch=1,
            grid=(steps,),
            in_specs=in_specs,
            out_specs=out_specs,
            scratch_shapes=scratch,
        ),
        out_shape=out_shape,
        input_output_aliases=aliases or {},
        compiler_params=pltpu.CompilerParams(
            dimension_semantics=("arbitrary",), vmem_limit_bytes=VMEM_BYTES
        ),
        cost_estimate=pl.CostEstimate(
            flops=int(cost_us * 1e9), transcendentals=0, bytes_accessed=int(cost_us * 3e6)
        ),
    )


def struct(shape, dtype):
    return jax.ShapeDtypeStruct(shape, dtype)


def exchange(value, axis_name, size, bit):
    return lax.ppermute(value, axis_name, [(i, i ^ bit) for i in range(size)])


def after(value, earlier):
    return lax.optimization_barrier((value, earlier))[0]


def make_body(dp_size, tensor_size):
    def body(hidden_in, doc_ids, ln1_gain, ln1_bias, w_qkv, b_qv, w_out, b_out, ln2_gain, ln2_bias,
             w_fc, b_fc, w_proj, b_proj, grad_out):
        row_count, width = hidden_in.shape
        heads, head_dim = w_qkv.shape[2:]
        local = heads * head_dim
        hidden = w_fc.shape[1]
        rows = row_count // 2
        blocks = rows // QUERY_ROWS
        half = rows // 2
        place = lax.axis_index("tensor")
        bits = dp_size.bit_length() - 1
        position = lax.axis_index("dp")
        share = width // dp_size
        first_bit = next(bit for bit in range(bits) if (share << bit) % 16 == 0)
        second_bit = min(first_bit + 1, bits - 1)
        upper = place // 2
        core = place % 2
        is_long = (doc_ids[SHORT_LEN] == doc_ids[0]).astype(jnp.int32)
        info = jnp.stack(
            [upper * blocks, is_long, core, (1 - upper) * blocks, half,
             (position >> first_bit) & 1, (position >> second_bit) & 1]
        ).astype(jnp.int32)

        def core_swap(value):
            return exchange(value, "tensor", tensor_size, 1)

        def pair_swap(value):
            return exchange(value, "tensor", tensor_size, 2)

        qkv_own = w_qkv.transpose(1, 2, 3, 0).reshape(3 * local, width)
        out_own = w_out.reshape(local, width)
        bias_own = b_qv.reshape(2, local)
        small_other = pair_swap(
            jnp.concatenate([b_qv.reshape(1, 2 * local), b_fc.reshape(1, hidden)], axis=1)
        )

        def my_piece(matrix):
            rows_each = matrix.shape[0] // dp_size
            return lax.dynamic_slice_in_dim(matrix, position * rows_each, rows_each, axis=0)[None]

        def widen(kept, come, bit):
            mine = (position >> bit) & 1
            return tuple(
                jnp.where(mine == 0, jnp.stack([a, b], 1), jnp.stack([b, a], 1)).reshape(
                    (2 * a.shape[0],) + a.shape[1:]
                )
                for a, b in zip(kept, come)
            )

        def dp_swap(values, bit):
            return tuple(exchange(value, "dp", dp_size, 1 << bit) for value in values)

        parts = tuple(
            pair_swap(my_piece(matrix)) for matrix in (w_proj, w_fc[width // 2 :])
        )
        out_other = pair_swap(out_own)
        qkv_other = pair_swap(qkv_own)
        fc_top = pair_swap(w_fc[: width // 2])
        come = dp_swap(parts, bits - 1)
        come, hidden_in = lax.optimization_barrier((come, hidden_in))
        parts = widen(parts, come, bits - 1)
        come = dp_swap(parts, bits - 2)

        first_spec = row_spec(QUERY_ROWS, width)
        turned_spec = pl.BlockSpec((local, QUERY_ROWS), lambda step, info: (0, step))
        att_spec = row_spec(QUERY_ROWS, local)
        log_spec = pl.BlockSpec((8, QUERY_ROWS), lambda step, info: (0, step))
        mix_specs = [att_spec] * 3 + [turned_spec]
        mix_structs = [struct((rows, local), BF16)] * 3 + [struct((local, rows), BF16)]
        attend_scratch = [pltpu.VMEM((rows, local), BF16), pltpu.VMEM((local, rows), BF16)]

        def forward_own(*refs):
            forward_own_kernel(heads, head_dim, *refs)

        def forward_other(*refs):
            forward_other_kernel(heads, head_dim, *refs)

        first_in, first_t, *mix_own, att_own, log_own = call(
            forward_own,
            blocks,
            [row_spec(QUERY_ROWS, width, True), whole((width,)), whole((width,)),
             whole((3 * local, width)), whole((2, local))],
            [first_spec, pl.BlockSpec((width, QUERY_ROWS), lambda step, info: (0, step))]
            + mix_specs + [att_spec, log_spec],
            [struct((rows, width), BF16), struct((width, rows), BF16)] + mix_structs
            + [struct((rows, local), BF16), struct((8, rows), F32)],
            attend_scratch,
            11,
        )(info, hidden_in, ln1_gain, ln1_bias, qkv_own, bias_own)
        come, small_other = after((come, small_other), first_in)
        parts = widen(parts, come, bits - 2)
        for bit in reversed(range(bits - 2)):
            come = dp_swap(parts, bit)
            if bit:
                first_in = after(first_in, come)
            parts = widen(parts, come, bit)
        proj_other = parts[0].reshape(hidden, width)
        fc_low = parts[1].reshape(width // 2, hidden)
        bias_other = small_other[:, : 2 * local].reshape(2, local)
        b_fc_both = jnp.concatenate([b_fc.reshape(1, hidden), small_other[:, 2 * local :]], axis=0)
        *mix_other, att_other, log_other, branch = call(
            forward_other,
            blocks,
            [first_spec, whole((3 * local, width)), whole((2, local)), att_spec,
             whole((local, width)), whole((local, width))],
            mix_specs + [att_spec, log_spec, first_spec],
            mix_structs + [struct((rows, local), BF16), struct((8, rows), F32),
                           struct((rows, width), BF16)],
            attend_scratch,
            12,
        )(info, first_in, qkv_other, bias_other, att_own, out_own, out_other)
        branch_swapped = core_swap(branch)

        def split_shape(bit, lead=()):
            runs = dp_size >> bit
            return lead + (runs // 2, share << bit, width)

        fc_shape = split_shape(first_bit, (2,))
        proj_shape = split_shape(second_bit, (2,))
        att_shape = split_shape(first_bit)
        (residual, mlp, grad_second, fc_kept, fc_sent, proj_kept, proj_sent, d_b_fc,
         d_b_proj) = call(
            mlp_kernel,
            blocks,
            [row_spec(QUERY_ROWS, width, True), first_spec, first_spec, whole((width,)),
             whole((width,)), whole((width,)), row_spec(QUERY_ROWS, width, True),
             whole((width, hidden)), whole((width // 2, hidden)), whole((width // 2, hidden)),
             whole((hidden, width)), whole((hidden, width)), whole((2, hidden))],
            [first_spec, first_spec, first_spec] + [whole(fc_shape)] * 2 + [whole(proj_shape)] * 2
            + [whole((2, hidden)), whole((1, width))],
            [struct((rows, width), F32), struct((rows, width), BF16), struct((rows, width), BF16),
             struct(fc_shape, BF16), struct(fc_shape, BF16), struct(proj_shape, BF16),
             struct(proj_shape, BF16),
             struct((2, hidden), F32), struct((1, width), F32)],
            [pltpu.VMEM((width, rows), BF16)] * 2 + [pltpu.VMEM((rows, hidden), BF16)] * 4,
            28,
        )(info, hidden_in, branch, branch_swapped, b_out, ln2_gain,
          ln2_bias, grad_out, w_fc, fc_top, fc_low, w_proj, proj_other, b_fc_both)
        grad_swapped = core_swap(grad_second)
        mlp_swapped = core_swap(mlp)

        half_spec = pl.BlockSpec(
            (QUERY_ROWS, width), lambda step, info: (info[2] * (half // QUERY_ROWS) + step, 0)
        )
        block_half = call(
            block_half_kernel,
            half // QUERY_ROWS,
            [half_spec, half_spec, half_spec, whole((width,))],
            first_spec,
            struct((half, width), BF16),
            [],
            3,
        )(info, residual, mlp, mlp_swapped, b_proj)
        block_near = pair_swap(block_half)

        back_rows = back_spec(QUERY_ROWS, width, blocks)
        back_att = back_spec(QUERY_ROWS, local, blocks)
        back_log = pl.BlockSpec((8, QUERY_ROWS), lambda step, info: (0, blocks - 1 - step))
        back_scratch = [
            pltpu.VMEM((rows, 3 * local), BF16),
            pltpu.VMEM((rows, local), F32),
            pltpu.VMEM((rows, local), F32),
            pltpu.SemaphoreType.DMA((2,)),
        ]
        turned_scratch = pltpu.VMEM((width, rows), BF16)
        back_mix = [back_att, whole((rows, local)), whole((rows, local)), whole((local, rows)),
                    whole((rows, local)), back_log, whole((3 * local, width)),
                    whole((local, width))]
        in_place = pl.BlockSpec(memory_space=pl.ANY)

        def backward_other(*refs):
            backward_other_kernel(heads, head_dim, *refs)

        def backward_own(*refs):
            backward_own_kernel(heads, head_dim, *refs)

        (grad_residual, grad_branch, grad_branch_t, grad_first_other, far_kept, far_sent, d_bias_other,
         d_norm_two, block_out) = call(
            backward_other,
            blocks,
            [back_rows, back_rows, back_rows, back_spec(QUERY_ROWS, width, blocks, True),
             whole((width,)), back_rows, back_rows, whole((width,))] + back_mix + [in_place],
            [back_rows, back_rows, whole((width, rows)), back_rows, whole(att_shape), whole(att_shape),
             whole((1, 3 * local)), whole((8, width)),
             back_spec(QUERY_ROWS, width, blocks, True)],
            [struct((rows, width), F32), struct((rows, width), BF16),
             struct((width, rows), BF16), struct((rows, width), F32),
             struct(att_shape, BF16), struct(att_shape, BF16), struct((1, 3 * local), F32),
             struct((8, width), F32), struct((row_count, width), BF16)],
            [turned_scratch] + back_scratch,
            21,
        )(info, grad_second, grad_swapped, residual, grad_out, ln2_gain, mlp, mlp_swapped, b_proj,
          *mix_other, att_other, log_other, qkv_other, out_other, first_t)
        grad_first, near_kept, near_sent, d_bias_own = call(
            backward_own,
            blocks,
            [back_rows, back_rows] + back_mix + [in_place, in_place],
            [back_rows, whole(att_shape), whole(att_shape), whole((1, 3 * local))],
            [struct((rows, width), BF16), struct(att_shape, BF16), struct(att_shape, BF16),
             struct((1, 3 * local), F32)],
            [turned_scratch, turned_scratch] + back_scratch,
            17,
        )(info, grad_branch, grad_first_other, *mix_own, att_own, log_own, qkv_own, out_own,
          first_t, grad_branch_t)
        first_swapped = core_swap(grad_first)
        quarter = half // QUERY_ROWS
        small_spec = whole((8, width))
        grad_in, grad_half, small, small_sent = call(
            last_norm_kernel,
            blocks,
            [row_spec(QUERY_ROWS, width, True), first_spec, first_spec, first_spec,
             whole((width,)), whole((1, width)), small_spec, whole((2, hidden)),
             whole((1, 3 * local)), whole((1, 3 * local))],
            [row_spec(QUERY_ROWS, width, True),
             pl.BlockSpec((QUERY_ROWS, width), lambda step, info: (
                jnp.clip(step - quarter * info[2], 0, quarter - 1), 0)),
             small_spec, small_spec],
            [struct((row_count, width), F32), struct((half, width), BF16),
             struct((8, width), F32), struct((8, width), F32)],
            [],
            7,
        )(info, hidden_in, grad_first, first_swapped, grad_residual, ln1_gain, d_b_proj,
          d_norm_two, d_b_fc, d_bias_own, d_bias_other)
        small_come = pair_swap(small_sent)
        grad_near = pair_swap(grad_half)

        def quarter_spec(part):
            def index(step, info):
                first = jnp.where(part == 0, info[2], 1 - info[2]) * quarter
                return jnp.clip(step - first, 0, quarter - 1), 0

            return pl.BlockSpec((QUERY_ROWS, width), index)

        def fill_both(target, near, far):
            return call(
                fill_both_kernel,
                blocks,
                [quarter_spec(0), quarter_spec(1), pl.BlockSpec(memory_space=pl.ANY)],
                pl.BlockSpec((QUERY_ROWS, width), lambda step, info: (info[3] + step, 0)),
                struct(target.shape, target.dtype),
                [],
                3,
                {3: 0},
            )(info, near, far, target)

        block_far = core_swap(block_near)
        block_near, block_far = after((block_near, block_far), grad_half)
        block_out = fill_both(block_out, block_near, block_far)
        grad_far = core_swap(grad_near)
        grad_in = fill_both(grad_in, grad_near, grad_far)

        def pick(value, axis, which):
            return lax.dynamic_index_in_dim(value, which, axis, keepdims=False)

        def parted(value, lead=()):
            return value.reshape(lead + (2,) * (bits - 1) + (share, width))

        def add(kept, received):
            return kept.astype(F32) + received.astype(F32)

        def others(bit):
            return [b for b in range(bits) if b != bit]

        def stages(value, left):
            for number, bit in enumerate(left):
                above = len([b for b in left[number:] if b > bit])
                mine = (position >> bit) & 1
                received = exchange(
                    pick(value, above, 1 - mine).astype(BF16), "dp", dp_size, 1 << bit
                )
                if number == 0:
                    received = after(received, grad_half)
                value = add(pick(value, above, mine), received)
            return value

        got_fc = exchange(fc_sent, "dp", dp_size, 1 << first_bit)
        got_proj = exchange(proj_sent, "dp", dp_size, 1 << second_bit)
        got_far = exchange(far_sent, "dp", dp_size, 1 << first_bit)
        got_fc, got_proj = after((got_fc, got_proj), grad_branch)
        half_fc = add(fc_kept, got_fc)
        half_proj = add(proj_kept, got_proj)
        come_fc = pair_swap(half_fc[1].astype(BF16))
        come_proj = pair_swap(half_proj[1].astype(BF16))
        got_near = exchange(near_sent, "dp", dp_size, 1 << first_bit)
        got_far = after(got_far, grad_first)
        come_far = pair_swap(add(far_kept, got_far).astype(BF16))
        come_fc = after(come_fc, grad_first)
        come_proj, come_far, got_near = after((come_proj, come_far, got_near), grad_half)
        fc_share = stages(parted(add(half_fc[0], come_fc)), others(first_bit))
        proj_share = stages(parted(add(half_proj[0], come_proj)), others(second_bit))
        att_half = parted(add(add(near_kept, got_near), come_far))
        att_share = stages(att_half, others(first_bit))
        small = small + small_come
        for bit in range(bits):
            small_come = exchange(small, "dp", dp_size, 1 << bit)
            small = small + small_come
        shares = lax.dynamic_index_in_dim(
            small[0:6].reshape(6, dp_size, share), position, 1, keepdims=False
        )
        d_b_proj_share, d_gain_two, d_shift_two, d_b_out, d_gain_one, d_shift_one = (
            shares[i] for i in range(6)
        )
        fc_rows, fc_columns = b_fc.shape
        d_b_fc_share = lax.dynamic_slice_in_dim(
            small[6].reshape(fc_rows, fc_columns), position * (fc_columns // dp_size),
            fc_columns // dp_size, axis=1,
        )
        d_b_qv_share = lax.dynamic_slice_in_dim(
            small[7, : 2 * local].reshape(2, heads, head_dim), position * (head_dim // dp_size),
            head_dim // dp_size, axis=2,
        )
        att_turned = att_share.T
        d_w_qkv = att_turned[: 3 * local].reshape(3, heads, head_dim, share).transpose(3, 0, 1, 2)
        d_w_out = att_turned[3 * local :].reshape(heads, head_dim, share)
        return (block_out, grad_in, d_gain_one, d_shift_one, d_w_qkv, d_b_qv_share, d_w_out,
                d_b_out, d_gain_two, d_shift_two, fc_share, d_b_fc_share, proj_share.T,
                d_b_proj_share)

    return body


def solution(mesh):
    in_specs = (
        P("dp", None),
        P("dp"),
        P(),
        P(),
        P(None, None, "tensor", None),
        P(None, "tensor", None),
        P("tensor", None, None),
        P(),
        P(),
        P(),
        P(None, "tensor"),
        P("tensor", None),
        P("tensor", None),
        P(),
        P("dp", None),
    )
    out_specs = (
        P("dp", None),
        P("dp", None),
        P("dp"),
        P("dp"),
        P("dp", None, "tensor", None),
        P(None, "tensor", "dp"),
        P("tensor", None, "dp"),
        P("dp"),
        P("dp"),
        P("dp"),
        P("dp", "tensor"),
        P("tensor", "dp"),
        P("tensor", "dp"),
        P("dp"),
    )
    inner = make_body(mesh.shape["dp"], mesh.shape["tensor"])

    return jax.shard_map(inner, mesh=mesh, in_specs=in_specs, out_specs=out_specs, check_vma=False)
```

```python
import math

import jax
import jax.numpy as jnp
from jax import lax
from jax.experimental import pallas as pl
from jax.experimental.pallas import tpu as pltpu
from jax.sharding import PartitionSpec as P


EPSILON = 1e-05
MASKED = -1e30
QUERY_ROWS = 256
SHORT_LEN = 256
BF16 = jnp.bfloat16
F32 = jnp.float32
VMEM_BYTES = 60 * 1024 * 1024
DP = "dp"
TENSOR = "tensor"


def dot_nn(left, right):
    return lax.dot_general(left, right, (((1,), (0,)), ((), ())), preferred_element_type=F32)


def dot_nt(left, right):
    return lax.dot_general(left, right, (((1,), (1,)), ((), ())), preferred_element_type=F32)


def normalize(values):
    row_mean = jnp.mean(values, axis=-1, keepdims=True)
    centered = values - row_mean
    inv_std = lax.rsqrt(jnp.mean(centered * centered, axis=-1, keepdims=True) + EPSILON)
    return (centered * inv_std, inv_std)


def norm_back(grad_normed, normed, inv_std, gain_vec):
    scaled = grad_normed * gain_vec
    return inv_std * (
        scaled
        - jnp.mean(scaled, axis=-1, keepdims=True)
        - normed * jnp.mean(scaled * normed, axis=-1, keepdims=True)
    )


def head_lanes(values, head, head_dim):
    per_group = 128 // head_dim
    first = (head // per_group) * 128
    group = values[:, first : min(first + 128, values.shape[1])]
    if group.shape[1] == head_dim:
        return group
    lane = lax.broadcasted_iota(jnp.int32, group.shape, 1)
    inside = (lane // head_dim) == (head % per_group)
    return jnp.where(inside, group, jnp.zeros_like(group))


def group_lanes(head, head_dim, width):
    per_group = 128 // head_dim
    first = (head // per_group) * 128
    return slice(first, min(first + 128, width))


def allowed_diagonal():
    key_pos = lax.broadcasted_iota(jnp.int32, (QUERY_ROWS, QUERY_ROWS), 0)
    row_pos = lax.broadcasted_iota(jnp.int32, (QUERY_ROWS, QUERY_ROWS), 1)
    return key_pos <= row_pos


def attend_block(queries, keys_ref, values_t_ref, start, old_blocks, heads, head_dim):
    width = heads * head_dim
    query_parts = [head_lanes(queries, head, head_dim) for head in range(heads)]

    def scores_of(head, rows):
        return dot_nt(keys_ref[rows, group_lanes(head, head_dim, width)], query_parts[head])

    def weighted(head, rows, weights):
        values_t = values_t_ref[head * head_dim : (head + 1) * head_dim, rows]
        return dot_nn(values_t, weights.astype(BF16))

    here = pl.ds(start, QUERY_ROWS)
    allowed = allowed_diagonal()
    state = []
    for head in range(heads):
        scores = jnp.where(allowed, scores_of(head, here), MASKED)
        row_max = jnp.max(scores, axis=0, keepdims=True)
        weights = jnp.exp(scores - row_max)
        state.append((row_max, jnp.sum(weights, axis=0, keepdims=True),
                      weighted(head, here, weights)))

    def old_block(index, state):
        rows = pl.ds(pl.multiple_of(index * QUERY_ROWS, QUERY_ROWS), QUERY_ROWS)
        result = []
        for head, (row_max, total, summed) in enumerate(state):
            scores = scores_of(head, rows)
            new_max = jnp.maximum(row_max, jnp.max(scores, axis=0, keepdims=True))
            weights = jnp.exp(scores - new_max)
            shrink = jnp.exp(row_max - new_max)
            result.append((new_max, total * shrink + jnp.sum(weights, axis=0, keepdims=True),
                           summed * shrink + weighted(head, rows, weights)))
        return tuple(result)

    state = lax.fori_loop(0, old_blocks, old_block, tuple(state))
    attended = jnp.concatenate([summed / total for _, total, summed in state], axis=0).T
    return attended, [row_max + jnp.log(total) for row_max, total, _ in state]


def attend_body(
    heads, head_dim, block, first_in, w_ref, bias_ref, mix_refs, att_ref, log_ref, keys_ref,
    values_t_ref, is_long,
):
    width = heads * head_dim
    projected = dot_nt(first_in, w_ref[...])
    queries = (projected[:, :width] + bias_ref[0:1, :]).astype(BF16)
    key_rows = projected[:, width : 2 * width].astype(BF16)
    value_rows = (projected[:, 2 * width :] + bias_ref[1:2, :]).astype(BF16)
    query_ref, key_ref, value_ref, keys_t_ref = mix_refs
    query_ref[...] = queries
    key_ref[...] = key_rows
    value_ref[...] = value_rows
    keys_t_ref[...] = key_rows.T
    start = pl.multiple_of(block * QUERY_ROWS, QUERY_ROWS)
    keys_ref[pl.ds(start, QUERY_ROWS), :] = key_rows
    values_t_ref[:, pl.ds(start, QUERY_ROWS)] = value_rows.T
    scaled = queries * jnp.asarray(1.0 / math.sqrt(head_dim), BF16)

    attended, logs = attend_block(
        scaled, keys_ref, values_t_ref, start, block * is_long, heads, head_dim
    )
    att_ref[...] = attended.astype(BF16)
    log_ref[...] = jnp.concatenate(logs + [jnp.zeros((8 - heads, QUERY_ROWS), F32)], axis=0)


def forward_own_kernel(heads, head_dim, info_ref, x_ref, gain_ref, shift_ref, w_ref, bias_ref,
                       first_ref, first_t_ref, query_ref, key_ref, value_ref, keys_t_ref, att_ref,
                       log_ref, keys_ref, values_t_ref):
    normed, _ = normalize(x_ref[...].astype(F32))
    first_in = (normed * gain_ref[...] + shift_ref[...]).astype(BF16)
    first_ref[...] = first_in
    first_t_ref[...] = first_in.T
    attend_body(heads, head_dim, pl.program_id(0), first_in, w_ref, bias_ref,
                (query_ref, key_ref, value_ref, keys_t_ref), att_ref, log_ref, keys_ref,
                values_t_ref, info_ref[1])


def forward_other_kernel(heads, head_dim, info_ref, first_ref, w_ref, bias_ref, att_own_ref,
                         w_out_own_ref, w_out_ref, query_ref, key_ref, value_ref, keys_t_ref,
                         att_ref, log_ref, branch_ref, keys_ref, values_t_ref):
    attend_body(heads, head_dim, pl.program_id(0), first_ref[...], w_ref, bias_ref,
                (query_ref, key_ref, value_ref, keys_t_ref), att_ref, log_ref, keys_ref,
                values_t_ref, info_ref[1])
    branch = dot_nn(att_own_ref[...], w_out_own_ref[...]) + dot_nn(att_ref[...], w_out_ref[...])
    branch_ref[...] = branch.astype(BF16)


def write_split(source_ref, kept_ref, sent_ref, mine, part=None):
    run = kept_ref.shape[-2]
    count = kept_ref.shape[-3]
    for value in range(2):

        @pl.when(mine == value)
        def _(value=value):
            for index in range(2 * count):
                target = kept_ref if index % 2 == value else sent_ref
                piece = source_ref[index * run : (index + 1) * run, :].astype(BF16)
                if part is None:
                    target[index // 2] = piece
                else:
                    target[part, index // 2] = piece


def mlp_kernel(info_ref, x_ref, branch_a_ref, branch_b_ref, b_out_ref, gain_ref, shift_ref, go_ref,
               fc_own_ref, fc_top_ref, fc_low_ref, proj_own_ref, proj_other_ref, b_fc_ref,
               residual_ref, mlp_ref, grad_ref, fc_kept_ref, fc_sent_ref, proj_kept_ref,
               proj_sent_ref, d_b_fc_ref, d_b_proj_ref,
               in_t_ref, go_t_ref, pre_own_ref, pre_other_ref, act_own_ref, act_other_ref):
    step = pl.program_id(0)
    rows = x_ref.shape[0]

    @pl.when(step == 0)
    def _():
        d_b_fc_ref[...] = jnp.zeros_like(d_b_fc_ref)
        d_b_proj_ref[...] = jnp.zeros_like(d_b_proj_ref)

    residual = x_ref[...].astype(F32) + (
        branch_a_ref[...].astype(F32) + branch_b_ref[...].astype(F32) + b_out_ref[...]
    )
    residual_ref[...] = residual
    normed, _ = normalize(residual)
    second_in = (normed * gain_ref[...] + shift_ref[...]).astype(BF16)
    grad_out = go_ref[...]
    here = pl.ds(pl.multiple_of(step * rows, rows), rows)
    in_t_ref[:, here] = second_in.T
    go_t_ref[:, here] = grad_out.T

    d_b_proj_ref[...] += jnp.sum(grad_out.astype(F32), axis=0, keepdims=True)
    mlp = None
    grad_second = None
    grad_acts = [dot_nt(grad_out, ref[...]) for ref in (proj_own_ref, proj_other_ref)]
    parts = (
        ((fc_own_ref,), proj_own_ref, pre_own_ref, act_own_ref),
        ((fc_top_ref, fc_low_ref), proj_other_ref, pre_other_ref, act_other_ref),
    )
    slope = math.sqrt(2.0 / math.pi)
    for part, (fc_refs, proj_ref, pre_ref, act_ref) in enumerate(parts):
        pre_act = b_fc_ref[part : part + 1, :]
        first = 0
        for fc_ref in fc_refs:
            last = first + fc_ref.shape[0]
            pre_act = pre_act + dot_nn(second_in[:, first:last], fc_ref[...])
            first = last
        square = pre_act * pre_act
        bent = jnp.tanh(pre_act * (slope + (0.044715 * slope) * square))
        half = 0.5 + 0.5 * bent
        act_low = (pre_act * half).astype(BF16)
        act_ref[here, :] = act_low
        part_out = dot_nn(act_low, proj_ref[...])
        grad_act = grad_acts[part]
        rise = pre_act * (2.0 * slope + (6.0 * 0.044715 * slope) * square)
        derivative = half + half * ((1.0 - half) * rise)
        grad_pre = (grad_act * derivative).astype(BF16)
        pre_ref[here, :] = grad_pre
        d_b_fc_ref[part : part + 1, :] += jnp.sum(grad_pre.astype(F32), axis=0, keepdims=True)
        part_grad = jnp.concatenate([dot_nt(grad_pre, fc_ref[...]) for fc_ref in fc_refs], axis=1)
        mlp = part_out if mlp is None else mlp + part_out
        grad_second = part_grad if grad_second is None else grad_second + part_grad
    mlp_ref[...] = mlp.astype(BF16)
    grad_ref[...] = grad_second.astype(BF16)

    @pl.when(step == pl.num_programs(0) - 1)
    def _():
        for part, (act_ref, pre_ref) in enumerate(
            ((act_own_ref, pre_own_ref), (act_other_ref, pre_other_ref))
        ):
            write_split(dot_nn(in_t_ref[...], pre_ref[...]).astype(BF16), fc_kept_ref,
                        fc_sent_ref, info_ref[5], part)
            write_split(dot_nn(go_t_ref[...], act_ref[...]).astype(BF16), proj_kept_ref,
                        proj_sent_ref, info_ref[6], part)


def attend_back_block(queries, grads, attended, logs, keys_ref, keys_t_ref, values_ref,
                      grad_keys_ref, grad_values_ref, start, old_blocks, heads, head_dim, scale):
    width = heads * head_dim
    query_parts = [head_lanes(queries, head, head_dim) for head in range(heads)]
    scaled_parts = [query * jnp.asarray(scale, BF16) for query in query_parts]
    grad_parts = [head_lanes(grads, head, head_dim) for head in range(heads)]
    product = grads.astype(F32) * attended.astype(F32)
    high = product.astype(BF16)
    low = (product - high.astype(F32)).astype(BF16)
    member = (
        lax.broadcasted_iota(jnp.int32, (8, width), 1) // head_dim
        == lax.broadcasted_iota(jnp.int32, (8, width), 0)
    )
    member = jnp.where(member, 1.0, 0.0).astype(BF16)
    deltas = dot_nt(member, high) + dot_nt(member, low)

    def through(rows, allowed):
        results = []
        for head in range(heads):
            lanes = group_lanes(head, head_dim, width)
            scores = dot_nt(keys_ref[rows, lanes], scaled_parts[head])
            weights = jnp.exp(scores - logs[head : head + 1, :])
            if allowed is not None:
                weights = jnp.where(allowed, weights, 0.0)
            grad_weights = dot_nt(values_ref[rows, lanes], grad_parts[head])
            grad_scores = (weights * (grad_weights - deltas[head : head + 1, :])).astype(BF16)
            grad_keys_ref[rows, lanes] += dot_nn(grad_scores, query_parts[head])
            grad_values_ref[rows, lanes] += dot_nn(weights.astype(BF16), grad_parts[head])
            keys_t = keys_t_ref[head * head_dim : (head + 1) * head_dim, rows]
            results.append(dot_nn(keys_t, grad_scores))
        return tuple(results)

    def old_block(index, sums):
        rows = pl.ds(pl.multiple_of(index * QUERY_ROWS, QUERY_ROWS), QUERY_ROWS)
        return tuple(old + new for old, new in zip(sums, through(rows, None)))

    sums = through(pl.ds(start, QUERY_ROWS), allowed_diagonal())
    sums = lax.fori_loop(0, old_blocks, old_block, sums)
    return jnp.concatenate(sums, axis=0).T * scale


def backward_other_kernel(heads, head_dim, info_ref, grad_a_ref, grad_b_ref, residual_ref, go_ref,
                          gain_ref, mlp_a_ref, mlp_b_ref, b_proj_ref, query_ref, key_ref, value_ref,
                          keys_t_ref, att_ref, log_ref, w_ref, w_out_ref, first_t_hbm,
                          grad_residual_ref, grad_branch_ref, grad_branch_t_ref, grad_first_ref,
                          kept_ref, sent_ref, d_bias_ref, d_norm_ref, block_ref,
                          first_t_ref, mixed_ref, grad_keys_ref, grad_values_ref, copy_sem):
    step = pl.program_id(0)
    copies = (pltpu.make_async_copy(first_t_hbm, first_t_ref, copy_sem.at[0]),)

    @pl.when(step == 0)
    def _():
        copies[0].start()
        d_norm_ref[...] = jnp.zeros_like(d_norm_ref)
        grad_keys_ref[...] = jnp.zeros_like(grad_keys_ref)
        grad_values_ref[...] = jnp.zeros_like(grad_values_ref)
        d_bias_ref[...] = jnp.zeros_like(d_bias_ref)

    rows = grad_a_ref.shape[0]
    block = pl.num_programs(0) - 1 - step
    here = pl.ds(pl.multiple_of(block * rows, rows), rows)
    grad_second = grad_a_ref[...].astype(F32) + grad_b_ref[...].astype(F32)
    normed, inv_std = normalize(residual_ref[...])
    grad_residual = go_ref[...].astype(F32) + norm_back(grad_second, normed, inv_std, gain_ref[...])
    grad_residual_ref[...] = grad_residual
    block_ref[...] = block_value(residual_ref, mlp_a_ref, mlp_b_ref, b_proj_ref)
    grad_branch = grad_residual.astype(BF16)
    grad_branch_ref[...] = grad_branch
    grad_branch_t_ref[:, here] = grad_branch.T
    d_norm_ref[0:1, :] += jnp.sum(grad_second * normed, axis=0, keepdims=True)
    d_norm_ref[1:2, :] += jnp.sum(grad_second, axis=0, keepdims=True)
    d_norm_ref[2:3, :] += jnp.sum(grad_branch.astype(F32), axis=0, keepdims=True)
    grad_first_ref[...] = attend_back(
        heads, head_dim, grad_branch, query_ref, key_ref, value_ref, keys_t_ref, att_ref, log_ref,
        w_ref, w_out_ref, d_bias_ref, mixed_ref, grad_keys_ref, grad_values_ref, info_ref[1])
    weight_grads(copies, first_t_ref, grad_branch_t_ref, mixed_ref, att_ref,
                 kept_ref, sent_ref, info_ref[5])


def backward_own_kernel(heads, head_dim, info_ref, grad_branch_ref, grad_first_in_ref, query_ref,
                        key_ref, value_ref, keys_t_ref, att_ref, log_ref, w_ref, w_out_ref,
                        first_t_hbm, grad_branch_t_hbm, grad_first_ref, kept_ref, sent_ref,
                        d_bias_ref, first_t_ref, grad_branch_t_ref, mixed_ref, grad_keys_ref,
                        grad_values_ref, copy_sem):
    copies = (
        pltpu.make_async_copy(first_t_hbm, first_t_ref, copy_sem.at[0]),
        pltpu.make_async_copy(grad_branch_t_hbm, grad_branch_t_ref, copy_sem.at[1]),
    )

    @pl.when(pl.program_id(0) == 0)
    def _():
        for copy in copies:
            copy.start()
        grad_keys_ref[...] = jnp.zeros_like(grad_keys_ref)
        grad_values_ref[...] = jnp.zeros_like(grad_values_ref)
        d_bias_ref[...] = jnp.zeros_like(d_bias_ref)

    grad_first = attend_back(
        heads, head_dim, grad_branch_ref[...], query_ref, key_ref, value_ref, keys_t_ref, att_ref,
        log_ref, w_ref, w_out_ref, d_bias_ref, mixed_ref, grad_keys_ref, grad_values_ref,
        info_ref[1])
    grad_first_ref[...] = (grad_first + grad_first_in_ref[...]).astype(BF16)
    weight_grads(copies, first_t_ref, grad_branch_t_ref, mixed_ref, att_ref,
                 kept_ref, sent_ref, info_ref[5])


def attend_back(heads, head_dim, grad_branch, query_ref, key_ref, value_ref, keys_t_ref, att_ref,
                log_ref, w_ref, w_out_ref, d_bias_ref, mixed_ref, grad_keys_ref, grad_values_ref,
                is_long):
    blocks = key_ref.shape[0] // QUERY_ROWS
    block = blocks - 1 - pl.program_id(0)
    scale = 1.0 / math.sqrt(head_dim)
    start = pl.multiple_of(block * QUERY_ROWS, QUERY_ROWS)
    here = pl.ds(start, QUERY_ROWS)
    grads = dot_nt(grad_branch, w_out_ref[...]).astype(BF16)
    grad_queries = attend_back_block(
        query_ref[...], grads, att_ref[here, :], log_ref[...], key_ref, keys_t_ref, value_ref,
        grad_keys_ref, grad_values_ref, start, block * is_long, heads, head_dim, scale)
    mixed = jnp.concatenate(
        [grad_queries.astype(BF16), (grad_keys_ref[here, :] * scale).astype(BF16),
         grad_values_ref[here, :].astype(BF16)], axis=1
    )
    mixed_ref[here, :] = mixed
    d_bias_ref[...] += jnp.sum(mixed.astype(F32), axis=0, keepdims=True)
    return dot_nn(mixed, w_ref[...])


def weight_grads(copies, first_t_ref, grad_branch_t_ref, mixed_ref, att_ref, kept_ref,
                 sent_ref, mine):
    @pl.when(pl.program_id(0) == pl.num_programs(0) - 1)
    def _():
        for copy in copies:
            copy.wait()
        total = jnp.concatenate(
            [dot_nn(first_t_ref[...], mixed_ref[...]).astype(BF16),
             dot_nn(grad_branch_t_ref[...], att_ref[...]).astype(BF16)], axis=1
        )
        write_split(total, kept_ref, sent_ref, mine)


def last_norm_kernel(info_ref, x_ref, grad_a_ref, grad_b_ref, grad_residual_ref, gain_ref,
                     d_b_proj_ref, d_norm_two_ref, d_b_fc_ref, bias_own_ref, bias_other_ref,
                     grad_in_ref, near_ref, small_ref, sent_ref):
    step = pl.program_id(0)
    local = bias_own_ref.shape[1] // 3

    @pl.when(step == 0)
    def _():
        for target, row, bias_ref in ((small_ref, 0, bias_own_ref), (sent_ref, 1, bias_other_ref)):
            target[...] = jnp.zeros_like(target)
            target[0:1, :] = d_b_proj_ref[...]
            target[1:4, :] = d_norm_two_ref[0:3, :]
            target[6:7, :] = d_b_fc_ref[row : row + 1, :]
            target[7:8, 0 : 2 * local] = jnp.concatenate(
                [bias_ref[:, 0:local], bias_ref[:, 2 * local :]], axis=1
            )

    grad_first = grad_a_ref[...].astype(F32) + grad_b_ref[...].astype(F32)
    normed, inv_std = normalize(x_ref[...].astype(F32))
    grad_in = grad_residual_ref[...] + norm_back(grad_first, normed, inv_std, gain_ref[...])
    grad_low = grad_in.astype(BF16)
    grad_in_ref[...] = grad_low.astype(F32)

    @pl.when((step * x_ref.shape[0]) // info_ref[4] == info_ref[2])
    def _():
        near_ref[...] = grad_low

    gain_sum = jnp.sum(grad_first * normed, axis=0, keepdims=True)
    shift_sum = jnp.sum(grad_first, axis=0, keepdims=True)
    for target in (small_ref, sent_ref):
        target[4:5, :] += gain_sum
        target[5:6, :] += shift_sum


def block_value(residual_ref, mlp_a_ref, mlp_b_ref, bias_ref):
    total = residual_ref[...] + (mlp_a_ref[...].astype(F32) + mlp_b_ref[...].astype(F32))
    return (total + bias_ref[...]).astype(BF16)


def block_half_kernel(info_ref, residual_ref, mlp_a_ref, mlp_b_ref, bias_ref, out_ref):
    out_ref[...] = block_value(residual_ref, mlp_a_ref, mlp_b_ref, bias_ref)


def fill_kernel(info_ref, come_ref, whole_ref, out_ref):
    out_ref[...] = come_ref[...].astype(out_ref.dtype)


def fill_both_kernel(info_ref, near_ref, far_ref, whole_ref, out_ref):
    from_near = (pl.program_id(0) * near_ref.shape[0]) // info_ref[4] == info_ref[2]
    out_ref[...] = jnp.where(from_near, near_ref[...], far_ref[...]).astype(out_ref.dtype)


def row_spec(rows, width, shift=False):
    if shift:
        return pl.BlockSpec((rows, width), lambda step, info: (info[0] + step, 0))
    return pl.BlockSpec((rows, width), lambda step, info: (step, 0))


def back_spec(rows, width, blocks, shift=False):
    if shift:
        return pl.BlockSpec((rows, width), lambda step, info: (info[0] + blocks - 1 - step, 0))
    return pl.BlockSpec((rows, width), lambda step, info: (blocks - 1 - step, 0))


def whole(shape):
    return pl.BlockSpec(shape, lambda step, info: (0,) * len(shape))


def call(kernel, steps, in_specs, out_specs, out_shape, scratch, cost_us, aliases=None):
    return pl.pallas_call(
        kernel,
        grid_spec=pltpu.PrefetchScalarGridSpec(
            num_scalar_prefetch=1,
            grid=(steps,),
            in_specs=in_specs,
            out_specs=out_specs,
            scratch_shapes=scratch,
        ),
        out_shape=out_shape,
        input_output_aliases=aliases or {},
        compiler_params=pltpu.CompilerParams(
            dimension_semantics=("arbitrary",), vmem_limit_bytes=VMEM_BYTES
        ),
        cost_estimate=pl.CostEstimate(
            flops=int(cost_us * 1e9), transcendentals=0, bytes_accessed=int(cost_us * 3e6)
        ),
    )


def struct(shape, dtype):
    return jax.ShapeDtypeStruct(shape, dtype)


def exchange(value, axis_name, size, bit):
    return lax.ppermute(value, axis_name, [(i, i ^ bit) for i in range(size)])


def after(value, earlier):
    return lax.optimization_barrier((value, earlier))[0]


def make_body(dp_size, tensor_size):
    def body(hidden_in, doc_ids, ln1_gain, ln1_bias, w_qkv, b_qv, w_out, b_out, ln2_gain, ln2_bias,
             w_fc, b_fc, w_proj, b_proj, grad_out):
        row_count, width = hidden_in.shape
        heads, head_dim = w_qkv.shape[2:]
        local = heads * head_dim
        hidden = w_fc.shape[1]
        rows = row_count // 2
        blocks = rows // QUERY_ROWS
        half = rows // 2
        place = lax.axis_index(TENSOR)
        bits = dp_size.bit_length() - 1
        position = lax.axis_index(DP)
        share = width // dp_size
        first_bit = next(bit for bit in range(bits) if (share << bit) % 16 == 0)
        second_bit = min(first_bit + 1, bits - 1)
        upper = place // 2
        core = place % 2
        is_long = (doc_ids[SHORT_LEN] == doc_ids[0]).astype(jnp.int32)
        info = jnp.stack(
            [upper * blocks, is_long, core, (1 - upper) * blocks, half,
             (position >> first_bit) & 1, (position >> second_bit) & 1]
        ).astype(jnp.int32)

        def core_swap(value):
            return exchange(value, TENSOR, tensor_size, 1)

        def pair_swap(value):
            return exchange(value, TENSOR, tensor_size, 2)

        qkv_own = w_qkv.transpose(1, 2, 3, 0).reshape(3 * local, width)
        out_own = w_out.reshape(local, width)
        bias_own = b_qv.reshape(2, local)
        small_other = pair_swap(
            jnp.concatenate([b_qv.reshape(1, 2 * local), b_fc.reshape(1, hidden)], axis=1)
        )

        def my_piece(matrix):
            rows_each = matrix.shape[0] // dp_size
            return lax.dynamic_slice_in_dim(matrix, position * rows_each, rows_each, axis=0)[None]

        def widen(kept, come, bit):
            mine = (position >> bit) & 1
            return tuple(
                jnp.where(mine == 0, jnp.stack([a, b], 1), jnp.stack([b, a], 1)).reshape(
                    (2 * a.shape[0],) + a.shape[1:]
                )
                for a, b in zip(kept, come)
            )

        def dp_swap(values, bit):
            return tuple(exchange(value, DP, dp_size, 1 << bit) for value in values)

        parts = tuple(
            pair_swap(my_piece(matrix)) for matrix in (w_proj, w_fc[width // 2 :])
        )
        out_other = pair_swap(out_own)
        qkv_other = pair_swap(qkv_own)
        fc_top = pair_swap(w_fc[: width // 2])
        come = dp_swap(parts, bits - 1)
        come, hidden_in = lax.optimization_barrier((come, hidden_in))
        parts = widen(parts, come, bits - 1)
        come = dp_swap(parts, bits - 2)

        first_spec = row_spec(QUERY_ROWS, width)
        turned_spec = pl.BlockSpec((local, QUERY_ROWS), lambda step, info: (0, step))
        att_spec = row_spec(QUERY_ROWS, local)
        log_spec = pl.BlockSpec((8, QUERY_ROWS), lambda step, info: (0, step))
        mix_specs = [att_spec] * 3 + [turned_spec]
        mix_structs = [struct((rows, local), BF16)] * 3 + [struct((local, rows), BF16)]
        attend_scratch = [pltpu.VMEM((rows, local), BF16), pltpu.VMEM((local, rows), BF16)]

        def forward_own(*refs):
            forward_own_kernel(heads, head_dim, *refs)

        def forward_other(*refs):
            forward_other_kernel(heads, head_dim, *refs)

        first_in, first_t, *mix_own, att_own, log_own = call(
            forward_own,
            blocks,
            [row_spec(QUERY_ROWS, width, True), whole((width,)), whole((width,)),
             whole((3 * local, width)), whole((2, local))],
            [first_spec, pl.BlockSpec((width, QUERY_ROWS), lambda step, info: (0, step))]
            + mix_specs + [att_spec, log_spec],
            [struct((rows, width), BF16), struct((width, rows), BF16)] + mix_structs
            + [struct((rows, local), BF16), struct((8, rows), F32)],
            attend_scratch,
            11,
        )(info, hidden_in, ln1_gain, ln1_bias, qkv_own, bias_own)
        come, small_other = after((come, small_other), first_in)
        parts = widen(parts, come, bits - 2)
        for bit in reversed(range(bits - 2)):
            come = dp_swap(parts, bit)
            if bit:
                first_in = after(first_in, come)
            parts = widen(parts, come, bit)
        proj_other = parts[0].reshape(hidden, width)
        fc_low = parts[1].reshape(width // 2, hidden)
        bias_other = small_other[:, : 2 * local].reshape(2, local)
        b_fc_both = jnp.concatenate([b_fc.reshape(1, hidden), small_other[:, 2 * local :]], axis=0)
        *mix_other, att_other, log_other, branch = call(
            forward_other,
            blocks,
            [first_spec, whole((3 * local, width)), whole((2, local)), att_spec,
             whole((local, width)), whole((local, width))],
            mix_specs + [att_spec, log_spec, first_spec],
            mix_structs + [struct((rows, local), BF16), struct((8, rows), F32),
                           struct((rows, width), BF16)],
            attend_scratch,
            12,
        )(info, first_in, qkv_other, bias_other, att_own, out_own, out_other)
        branch_swapped = core_swap(branch)

        def split_shape(bit, lead=()):
            runs = dp_size >> bit
            return lead + (runs // 2, share << bit, width)

        fc_shape = split_shape(first_bit, (2,))
        proj_shape = split_shape(second_bit, (2,))
        att_shape = split_shape(first_bit)
        (residual, mlp, grad_second, fc_kept, fc_sent, proj_kept, proj_sent, d_b_fc,
         d_b_proj) = call(
            mlp_kernel,
            blocks,
            [row_spec(QUERY_ROWS, width, True), first_spec, first_spec, whole((width,)),
             whole((width,)), whole((width,)), row_spec(QUERY_ROWS, width, True),
             whole((width, hidden)), whole((width // 2, hidden)), whole((width // 2, hidden)),
             whole((hidden, width)), whole((hidden, width)), whole((2, hidden))],
            [first_spec, first_spec, first_spec] + [whole(fc_shape)] * 2 + [whole(proj_shape)] * 2
            + [whole((2, hidden)), whole((1, width))],
            [struct((rows, width), F32), struct((rows, width), BF16), struct((rows, width), BF16),
             struct(fc_shape, BF16), struct(fc_shape, BF16), struct(proj_shape, BF16),
             struct(proj_shape, BF16),
             struct((2, hidden), F32), struct((1, width), F32)],
            [pltpu.VMEM((width, rows), BF16)] * 2 + [pltpu.VMEM((rows, hidden), BF16)] * 4,
            28,
        )(info, hidden_in, branch, branch_swapped, b_out, ln2_gain,
          ln2_bias, grad_out, w_fc, fc_top, fc_low, w_proj, proj_other, b_fc_both)
        grad_swapped = core_swap(grad_second)
        mlp_swapped = core_swap(mlp)

        half_spec = pl.BlockSpec(
            (QUERY_ROWS, width), lambda step, info: (info[2] * (half // QUERY_ROWS) + step, 0)
        )
        block_half = call(
            block_half_kernel,
            half // QUERY_ROWS,
            [half_spec, half_spec, half_spec, whole((width,))],
            first_spec,
            struct((half, width), BF16),
            [],
            3,
        )(info, residual, mlp, mlp_swapped, b_proj)
        block_near = pair_swap(block_half)

        back_rows = back_spec(QUERY_ROWS, width, blocks)
        back_att = back_spec(QUERY_ROWS, local, blocks)
        back_log = pl.BlockSpec((8, QUERY_ROWS), lambda step, info: (0, blocks - 1 - step))
        back_scratch = [
            pltpu.VMEM((rows, 3 * local), BF16),
            pltpu.VMEM((rows, local), F32),
            pltpu.VMEM((rows, local), F32),
            pltpu.SemaphoreType.DMA((2,)),
        ]
        turned_scratch = pltpu.VMEM((width, rows), BF16)
        back_mix = [back_att, whole((rows, local)), whole((rows, local)), whole((local, rows)),
                    whole((rows, local)), back_log, whole((3 * local, width)),
                    whole((local, width))]
        in_place = pl.BlockSpec(memory_space=pl.ANY)

        def backward_other(*refs):
            backward_other_kernel(heads, head_dim, *refs)

        def backward_own(*refs):
            backward_own_kernel(heads, head_dim, *refs)

        (grad_residual, grad_branch, grad_branch_t, grad_first_other, far_kept, far_sent, d_bias_other,
         d_norm_two, block_out) = call(
            backward_other,
            blocks,
            [back_rows, back_rows, back_rows, back_spec(QUERY_ROWS, width, blocks, True),
             whole((width,)), back_rows, back_rows, whole((width,))] + back_mix + [in_place],
            [back_rows, back_rows, whole((width, rows)), back_rows, whole(att_shape), whole(att_shape),
             whole((1, 3 * local)), whole((8, width)),
             back_spec(QUERY_ROWS, width, blocks, True)],
            [struct((rows, width), F32), struct((rows, width), BF16),
             struct((width, rows), BF16), struct((rows, width), F32),
             struct(att_shape, BF16), struct(att_shape, BF16), struct((1, 3 * local), F32),
             struct((8, width), F32), struct((row_count, width), BF16)],
            [turned_scratch] + back_scratch,
            21,
        )(info, grad_second, grad_swapped, residual, grad_out, ln2_gain, mlp, mlp_swapped, b_proj,
          *mix_other, att_other, log_other, qkv_other, out_other, first_t)
        grad_first, near_kept, near_sent, d_bias_own = call(
            backward_own,
            blocks,
            [back_rows, back_rows] + back_mix + [in_place, in_place],
            [back_rows, whole(att_shape), whole(att_shape), whole((1, 3 * local))],
            [struct((rows, width), BF16), struct(att_shape, BF16), struct(att_shape, BF16),
             struct((1, 3 * local), F32)],
            [turned_scratch, turned_scratch] + back_scratch,
            17,
        )(info, grad_branch, grad_first_other, *mix_own, att_own, log_own, qkv_own, out_own,
          first_t, grad_branch_t)
        first_swapped = core_swap(grad_first)
        quarter = half // QUERY_ROWS
        small_spec = whole((8, width))
        grad_in, grad_half, small, small_sent = call(
            last_norm_kernel,
            blocks,
            [row_spec(QUERY_ROWS, width, True), first_spec, first_spec, first_spec,
             whole((width,)), whole((1, width)), small_spec, whole((2, hidden)),
             whole((1, 3 * local)), whole((1, 3 * local))],
            [row_spec(QUERY_ROWS, width, True),
             pl.BlockSpec((QUERY_ROWS, width), lambda step, info: (
                jnp.clip(step - quarter * info[2], 0, quarter - 1), 0)),
             small_spec, small_spec],
            [struct((row_count, width), F32), struct((half, width), BF16),
             struct((8, width), F32), struct((8, width), F32)],
            [],
            7,
        )(info, hidden_in, grad_first, first_swapped, grad_residual, ln1_gain, d_b_proj,
          d_norm_two, d_b_fc, d_bias_own, d_bias_other)
        small_come = pair_swap(small_sent)
        grad_near = pair_swap(grad_half)

        def quarter_spec(part):
            def index(step, info):
                first = jnp.where(part == 0, info[2], 1 - info[2]) * quarter
                return jnp.clip(step - first, 0, quarter - 1), 0

            return pl.BlockSpec((QUERY_ROWS, width), index)

        def fill_both(target, near, far):
            return call(
                fill_both_kernel,
                blocks,
                [quarter_spec(0), quarter_spec(1), pl.BlockSpec(memory_space=pl.ANY)],
                pl.BlockSpec((QUERY_ROWS, width), lambda step, info: (info[3] + step, 0)),
                struct(target.shape, target.dtype),
                [],
                3,
                {3: 0},
            )(info, near, far, target)

        block_far = core_swap(block_near)
        block_near, block_far = after((block_near, block_far), grad_half)
        block_out = fill_both(block_out, block_near, block_far)
        grad_far = core_swap(grad_near)

        def fill(target, come, part):
            def index(step, info):
                first = jnp.where(part == 0, info[2], 1 - info[2]) * quarter
                return info[3] + first + step, 0

            return call(
                fill_kernel,
                quarter,
                [first_spec, pl.BlockSpec(memory_space=pl.ANY)],
                pl.BlockSpec((QUERY_ROWS, width), index),
                struct(target.shape, target.dtype),
                [],
                2,
                {2: 0},
            )(info, come, target)

        grad_in = fill(grad_in, grad_near, 0)
        grad_in = fill(grad_in, grad_far, 1)

        def pick(value, axis, which):
            return lax.dynamic_index_in_dim(value, which, axis, keepdims=False)

        def parted(value, lead=()):
            return value.reshape(lead + (2,) * (bits - 1) + (share, width))

        def add(kept, received):
            return kept.astype(F32) + received.astype(F32)

        def others(bit):
            return [b for b in range(bits) if b != bit]

        def stages(value, left):
            for number, bit in enumerate(left):
                above = len([b for b in left[number:] if b > bit])
                mine = (position >> bit) & 1
                received = exchange(
                    pick(value, above, 1 - mine).astype(BF16), DP, dp_size, 1 << bit
                )
                if number == 0:
                    received = after(received, grad_half)
                value = add(pick(value, above, mine), received)
            return value

        got_fc = exchange(fc_sent, DP, dp_size, 1 << first_bit)
        got_proj = exchange(proj_sent, DP, dp_size, 1 << second_bit)
        got_far = exchange(far_sent, DP, dp_size, 1 << first_bit)
        got_fc, got_proj = after((got_fc, got_proj), grad_branch)
        half_fc = add(fc_kept[1], got_fc[1])
        half_proj = add(proj_kept[1], got_proj[1])
        come_fc = pair_swap(half_fc.astype(BF16))
        come_proj = pair_swap(half_proj.astype(BF16))
        got_near = exchange(near_sent, DP, dp_size, 1 << first_bit)
        got_far = after(got_far, grad_first)
        come_far = pair_swap(add(far_kept, got_far).astype(BF16))
        come_fc, got_fc = after((come_fc, got_fc), grad_first)
        come_proj, got_proj, come_far, got_near = after(
            (come_proj, got_proj, come_far, got_near), grad_half
        )
        fc_share = stages(parted(add(add(fc_kept[0], got_fc[0]), come_fc)), others(first_bit))
        proj_share = stages(parted(add(add(proj_kept[0], got_proj[0]), come_proj)), others(second_bit))
        att_half = parted(add(add(near_kept, got_near), come_far))
        att_share = stages(att_half, others(first_bit))
        small = small + small_come
        for bit in range(bits):
            small_come = exchange(small, DP, dp_size, 1 << bit)
            small = small + small_come
        shares = lax.dynamic_index_in_dim(
            small[0:6].reshape(6, dp_size, share), position, 1, keepdims=False
        )
        d_b_proj_share, d_gain_two, d_shift_two, d_b_out, d_gain_one, d_shift_one = (
            shares[i] for i in range(6)
        )
        fc_rows, fc_columns = b_fc.shape
        d_b_fc_share = lax.dynamic_slice_in_dim(
            small[6].reshape(fc_rows, fc_columns), position * (fc_columns // dp_size),
            fc_columns // dp_size, axis=1,
        )
        d_b_qv_share = lax.dynamic_slice_in_dim(
            small[7, : 2 * local].reshape(2, heads, head_dim), position * (head_dim // dp_size),
            head_dim // dp_size, axis=2,
        )
        att_turned = att_share.T
        d_w_qkv = att_turned[: 3 * local].reshape(3, heads, head_dim, share).transpose(3, 0, 1, 2)
        d_w_out = att_turned[3 * local :].reshape(heads, head_dim, share)
        return (block_out, grad_in, d_gain_one, d_shift_one, d_w_qkv, d_b_qv_share, d_w_out,
                d_b_out, d_gain_two, d_shift_two, fc_share, d_b_fc_share, proj_share.T,
                d_b_proj_share)

    return body


def solution(mesh):
    in_specs = (
        P(DP, None),
        P(DP),
        P(),
        P(),
        P(None, None, TENSOR, None),
        P(None, TENSOR, None),
        P(TENSOR, None, None),
        P(),
        P(),
        P(),
        P(None, TENSOR),
        P(TENSOR, None),
        P(TENSOR, None),
        P(),
        P(DP, None),
    )
    out_specs = (
        P(DP, None),
        P(DP, None),
        P(DP),
        P(DP),
        P(DP, None, TENSOR, None),
        P(None, TENSOR, DP),
        P(TENSOR, None, DP),
        P(DP),
        P(DP),
        P(DP),
        P(DP, TENSOR),
        P(TENSOR, DP),
        P(TENSOR, DP),
        P(DP),
    )
    inner = make_body(mesh.shape[DP], mesh.shape[TENSOR])

    return jax.shard_map(inner, mesh=mesh, in_specs=in_specs, out_specs=out_specs, check_vma=False)
```

```python
import math

import jax
import jax.numpy as jnp
from jax import lax
from jax.experimental import pallas as pl
from jax.experimental.pallas import tpu as pltpu
from jax.sharding import PartitionSpec as P


EPSILON = 1e-05
MASKED = -1e30
QUERY_ROWS = 256
SHORT_LEN = 256
BF16 = jnp.bfloat16
F32 = jnp.float32
VMEM_BYTES = 60 * 1024 * 1024
DP = "dp"
TENSOR = "tensor"


def dot_nn(left, right):
    return lax.dot_general(left, right, (((1,), (0,)), ((), ())), preferred_element_type=F32)


def dot_nt(left, right):
    return lax.dot_general(left, right, (((1,), (1,)), ((), ())), preferred_element_type=F32)


def normalize(values):
    row_mean = jnp.mean(values, axis=-1, keepdims=True)
    centered = values - row_mean
    inv_std = lax.rsqrt(jnp.mean(centered * centered, axis=-1, keepdims=True) + EPSILON)
    return (centered * inv_std, inv_std)


def norm_back(grad_normed, normed, inv_std, gain_vec):
    scaled = grad_normed * gain_vec
    return inv_std * (
        scaled
        - jnp.mean(scaled, axis=-1, keepdims=True)
        - normed * jnp.mean(scaled * normed, axis=-1, keepdims=True)
    )


def head_lanes(values, head, head_dim):
    per_group = 128 // head_dim
    first = (head // per_group) * 128
    group = values[:, first : min(first + 128, values.shape[1])]
    if group.shape[1] == head_dim:
        return group
    lane = lax.broadcasted_iota(jnp.int32, group.shape, 1)
    inside = (lane // head_dim) == (head % per_group)
    return jnp.where(inside, group, jnp.zeros_like(group))


def group_lanes(head, head_dim, width):
    per_group = 128 // head_dim
    first = (head // per_group) * 128
    return slice(first, min(first + 128, width))


def allowed_diagonal():
    key_pos = lax.broadcasted_iota(jnp.int32, (QUERY_ROWS, QUERY_ROWS), 0)
    row_pos = lax.broadcasted_iota(jnp.int32, (QUERY_ROWS, QUERY_ROWS), 1)
    return key_pos <= row_pos


def attend_block(queries, keys_ref, values_t_ref, start, old_blocks, heads, head_dim):
    width = heads * head_dim
    query_parts = [head_lanes(queries, head, head_dim) for head in range(heads)]

    def scores_of(head, rows):
        return dot_nt(keys_ref[rows, group_lanes(head, head_dim, width)], query_parts[head])

    def weighted(head, rows, weights):
        values_t = values_t_ref[head * head_dim : (head + 1) * head_dim, rows]
        return dot_nn(values_t, weights.astype(BF16))

    here = pl.ds(start, QUERY_ROWS)
    allowed = allowed_diagonal()
    state = []
    for head in range(heads):
        scores = jnp.where(allowed, scores_of(head, here), MASKED)
        row_max = jnp.max(scores, axis=0, keepdims=True)
        weights = jnp.exp(scores - row_max)
        state.append((row_max, jnp.sum(weights, axis=0, keepdims=True),
                      weighted(head, here, weights)))

    def old_block(index, state):
        rows = pl.ds(pl.multiple_of(index * QUERY_ROWS, QUERY_ROWS), QUERY_ROWS)
        result = []
        for head, (row_max, total, summed) in enumerate(state):
            scores = scores_of(head, rows)
            new_max = jnp.maximum(row_max, jnp.max(scores, axis=0, keepdims=True))
            weights = jnp.exp(scores - new_max)
            shrink = jnp.exp(row_max - new_max)
            result.append((new_max, total * shrink + jnp.sum(weights, axis=0, keepdims=True),
                           summed * shrink + weighted(head, rows, weights)))
        return tuple(result)

    state = lax.fori_loop(0, old_blocks, old_block, tuple(state))
    attended = jnp.concatenate([summed / total for _, total, summed in state], axis=0).T
    return attended, [row_max + jnp.log(total) for row_max, total, _ in state]


def attend_rows(queries, keys_ref, values_t_ref, start, old_rows, heads, head_dim):
    width = heads * head_dim
    allowed = allowed_diagonal()
    here = pl.ds(start, QUERY_ROWS)
    attended_t = []
    logs = []
    for head in range(heads):
        query = head_lanes(queries, head, head_dim)
        lanes = group_lanes(head, head_dim, width)
        rows = slice(head * head_dim, (head + 1) * head_dim)
        near = jnp.where(allowed, dot_nt(keys_ref[here, lanes], query), MASKED)
        row_max = jnp.max(near, axis=0, keepdims=True)
        if old_rows:
            far = dot_nt(keys_ref[0:old_rows, lanes], query)
            row_max = jnp.maximum(row_max, jnp.max(far, axis=0, keepdims=True))
        near = jnp.exp(near - row_max)
        total = jnp.sum(near, axis=0, keepdims=True)
        summed = dot_nn(values_t_ref[rows, here], near.astype(BF16))
        if old_rows:
            far = jnp.exp(far - row_max)
            total = total + jnp.sum(far, axis=0, keepdims=True)
            summed = summed + dot_nn(values_t_ref[rows, 0:old_rows], far.astype(BF16))
        attended_t.append(summed / total)
        logs.append(row_max + jnp.log(total))
    return jnp.concatenate(attended_t, axis=0).T, logs


def attend_body(
    heads, head_dim, block, first_in, w_ref, bias_ref, mix_refs, att_ref, log_ref, keys_ref,
    values_t_ref, is_long, unrolled,
):
    width = heads * head_dim
    projected = dot_nt(first_in, w_ref[...])
    queries = (projected[:, :width] + bias_ref[0:1, :]).astype(BF16)
    key_rows = projected[:, width : 2 * width].astype(BF16)
    value_rows = (projected[:, 2 * width :] + bias_ref[1:2, :]).astype(BF16)
    query_ref, key_ref, value_ref, keys_t_ref = mix_refs
    query_ref[...] = queries
    key_ref[...] = key_rows
    value_ref[...] = value_rows
    keys_t_ref[...] = key_rows.T
    start = pl.multiple_of(block * QUERY_ROWS, QUERY_ROWS)
    keys_ref[pl.ds(start, QUERY_ROWS), :] = key_rows
    values_t_ref[:, pl.ds(start, QUERY_ROWS)] = value_rows.T
    scaled = queries * jnp.asarray(1.0 / math.sqrt(head_dim), BF16)


    def finish(attended, logs):
        att_ref[...] = attended.astype(BF16)
        log_ref[...] = jnp.concatenate(logs + [jnp.zeros((8 - heads, QUERY_ROWS), F32)], axis=0)

    if not unrolled:
        finish(*attend_block(
            scaled, keys_ref, values_t_ref, start, block * is_long, heads, head_dim
        ))
        return

    @pl.when(block * is_long == 0)
    def _():
        finish(*attend_rows(scaled, keys_ref, values_t_ref, start, 0, heads, head_dim))

    for position in range(1, keys_ref.shape[0] // QUERY_ROWS):

        @pl.when(block * is_long == position)
        def _(first=position * QUERY_ROWS):
            finish(*attend_rows(scaled, keys_ref, values_t_ref, first, first, heads, head_dim))


def forward_own_kernel(heads, head_dim, info_ref, x_ref, gain_ref, shift_ref, w_ref, bias_ref,
                       first_ref, first_t_ref, query_ref, key_ref, value_ref, keys_t_ref, att_ref,
                       log_ref, keys_ref, values_t_ref):
    normed, _ = normalize(x_ref[...].astype(F32))
    first_in = (normed * gain_ref[...] + shift_ref[...]).astype(BF16)
    first_ref[...] = first_in
    first_t_ref[...] = first_in.T
    attend_body(heads, head_dim, pl.program_id(0), first_in, w_ref, bias_ref,
                (query_ref, key_ref, value_ref, keys_t_ref), att_ref, log_ref, keys_ref,
                values_t_ref, info_ref[1], True)


def forward_other_kernel(heads, head_dim, info_ref, first_ref, w_ref, bias_ref, att_own_ref,
                         w_out_own_ref, w_out_ref, query_ref, key_ref, value_ref, keys_t_ref,
                         att_ref, log_ref, branch_ref, keys_ref, values_t_ref):
    attend_body(heads, head_dim, pl.program_id(0), first_ref[...], w_ref, bias_ref,
                (query_ref, key_ref, value_ref, keys_t_ref), att_ref, log_ref, keys_ref,
                values_t_ref, info_ref[1], True)
    branch = dot_nn(att_own_ref[...], w_out_own_ref[...]) + dot_nn(att_ref[...], w_out_ref[...])
    branch_ref[...] = branch.astype(BF16)


def write_split(source_ref, kept_ref, sent_ref, mine, part=None):
    run = kept_ref.shape[-2]
    count = kept_ref.shape[-3]
    for value in range(2):

        @pl.when(mine == value)
        def _(value=value):
            for index in range(2 * count):
                target = kept_ref if index % 2 == value else sent_ref
                piece = source_ref[index * run : (index + 1) * run, :].astype(BF16)
                if part is None:
                    target[index // 2] = piece
                else:
                    target[part, index // 2] = piece


def mlp_kernel(info_ref, x_ref, branch_a_ref, branch_b_ref, b_out_ref, gain_ref, shift_ref, go_ref,
               fc_own_ref, fc_top_ref, fc_low_ref, proj_own_ref, proj_other_ref, b_fc_ref,
               residual_ref, mlp_ref, grad_ref, fc_kept_ref, fc_sent_ref, proj_kept_ref,
               proj_sent_ref, d_b_fc_ref, d_b_proj_ref,
               in_t_ref, go_t_ref, pre_own_ref, pre_other_ref, act_own_ref, act_other_ref):
    step = pl.program_id(0)
    rows = x_ref.shape[0]

    @pl.when(step == 0)
    def _():
        d_b_fc_ref[...] = jnp.zeros_like(d_b_fc_ref)
        d_b_proj_ref[...] = jnp.zeros_like(d_b_proj_ref)

    residual = x_ref[...].astype(F32) + (
        branch_a_ref[...].astype(F32) + branch_b_ref[...].astype(F32) + b_out_ref[...]
    )
    residual_ref[...] = residual
    normed, _ = normalize(residual)
    second_in = (normed * gain_ref[...] + shift_ref[...]).astype(BF16)
    grad_out = go_ref[...]
    here = pl.ds(pl.multiple_of(step * rows, rows), rows)
    in_t_ref[:, here] = second_in.T
    go_t_ref[:, here] = grad_out.T

    d_b_proj_ref[...] += jnp.sum(grad_out.astype(F32), axis=0, keepdims=True)
    mlp = None
    grad_second = None
    grad_acts = [dot_nt(grad_out, ref[...]) for ref in (proj_own_ref, proj_other_ref)]
    parts = (
        ((fc_own_ref,), proj_own_ref, pre_own_ref, act_own_ref),
        ((fc_top_ref, fc_low_ref), proj_other_ref, pre_other_ref, act_other_ref),
    )
    slope = math.sqrt(2.0 / math.pi)
    for part, (fc_refs, proj_ref, pre_ref, act_ref) in enumerate(parts):
        pre_act = b_fc_ref[part : part + 1, :]
        first = 0
        for fc_ref in fc_refs:
            last = first + fc_ref.shape[0]
            pre_act = pre_act + dot_nn(second_in[:, first:last], fc_ref[...])
            first = last
        square = pre_act * pre_act
        bent = jnp.tanh(pre_act * (slope + (0.044715 * slope) * square))
        half = 0.5 + 0.5 * bent
        act_low = (pre_act * half).astype(BF16)
        act_ref[here, :] = act_low
        part_out = dot_nn(act_low, proj_ref[...])
        grad_act = grad_acts[part]
        rise = pre_act * (2.0 * slope + (6.0 * 0.044715 * slope) * square)
        derivative = half + half * ((1.0 - half) * rise)
        grad_pre = (grad_act * derivative).astype(BF16)
        pre_ref[here, :] = grad_pre
        d_b_fc_ref[part : part + 1, :] += jnp.sum(grad_pre.astype(F32), axis=0, keepdims=True)
        part_grad = jnp.concatenate([dot_nt(grad_pre, fc_ref[...]) for fc_ref in fc_refs], axis=1)
        mlp = part_out if mlp is None else mlp + part_out
        grad_second = part_grad if grad_second is None else grad_second + part_grad
    mlp_ref[...] = mlp.astype(BF16)
    grad_ref[...] = grad_second.astype(BF16)

    @pl.when(step == pl.num_programs(0) - 1)
    def _():
        for part, (act_ref, pre_ref) in enumerate(
            ((act_own_ref, pre_own_ref), (act_other_ref, pre_other_ref))
        ):
            write_split(dot_nn(in_t_ref[...], pre_ref[...]).astype(BF16), fc_kept_ref,
                        fc_sent_ref, info_ref[5], part)
            write_split(dot_nn(go_t_ref[...], act_ref[...]).astype(BF16), proj_kept_ref,
                        proj_sent_ref, info_ref[6], part)


def attend_back_block(queries, grads, attended, logs, keys_ref, keys_t_ref, values_ref,
                      grad_keys_ref, grad_values_ref, start, old_blocks, heads, head_dim, scale):
    width = heads * head_dim
    query_parts = [head_lanes(queries, head, head_dim) for head in range(heads)]
    scaled_parts = [query * jnp.asarray(scale, BF16) for query in query_parts]
    grad_parts = [head_lanes(grads, head, head_dim) for head in range(heads)]
    product = grads.astype(F32) * attended.astype(F32)
    high = product.astype(BF16)
    low = (product - high.astype(F32)).astype(BF16)
    member = (
        lax.broadcasted_iota(jnp.int32, (8, width), 1) // head_dim
        == lax.broadcasted_iota(jnp.int32, (8, width), 0)
    )
    member = jnp.where(member, 1.0, 0.0).astype(BF16)
    deltas = dot_nt(member, high) + dot_nt(member, low)

    def through(rows, allowed):
        results = []
        for head in range(heads):
            lanes = group_lanes(head, head_dim, width)
            scores = dot_nt(keys_ref[rows, lanes], scaled_parts[head])
            weights = jnp.exp(scores - logs[head : head + 1, :])
            if allowed is not None:
                weights = jnp.where(allowed, weights, 0.0)
            grad_weights = dot_nt(values_ref[rows, lanes], grad_parts[head])
            grad_scores = (weights * (grad_weights - deltas[head : head + 1, :])).astype(BF16)
            grad_keys_ref[rows, lanes] += dot_nn(grad_scores, query_parts[head])
            grad_values_ref[rows, lanes] += dot_nn(weights.astype(BF16), grad_parts[head])
            keys_t = keys_t_ref[head * head_dim : (head + 1) * head_dim, rows]
            results.append(dot_nn(keys_t, grad_scores))
        return tuple(results)

    def old_block(index, sums):
        rows = pl.ds(pl.multiple_of(index * QUERY_ROWS, QUERY_ROWS), QUERY_ROWS)
        return tuple(old + new for old, new in zip(sums, through(rows, None)))

    sums = through(pl.ds(start, QUERY_ROWS), allowed_diagonal())
    sums = lax.fori_loop(0, old_blocks, old_block, sums)
    return jnp.concatenate(sums, axis=0).T * scale


def backward_other_kernel(heads, head_dim, info_ref, grad_a_ref, grad_b_ref, residual_ref, go_ref,
                          gain_ref, mlp_a_ref, mlp_b_ref, b_proj_ref, query_ref, key_ref, value_ref,
                          keys_t_ref, att_ref, log_ref, w_ref, w_out_ref, first_t_hbm,
                          grad_residual_ref, grad_branch_ref, grad_branch_t_ref, grad_first_ref,
                          kept_ref, sent_ref, d_bias_ref, d_norm_ref, block_ref,
                          first_t_ref, mixed_ref, grad_keys_ref, grad_values_ref, copy_sem):
    step = pl.program_id(0)
    copies = (pltpu.make_async_copy(first_t_hbm, first_t_ref, copy_sem.at[0]),)

    @pl.when(step == 0)
    def _():
        copies[0].start()
        d_norm_ref[...] = jnp.zeros_like(d_norm_ref)
        grad_keys_ref[...] = jnp.zeros_like(grad_keys_ref)
        grad_values_ref[...] = jnp.zeros_like(grad_values_ref)
        d_bias_ref[...] = jnp.zeros_like(d_bias_ref)

    rows = grad_a_ref.shape[0]
    block = pl.num_programs(0) - 1 - step
    here = pl.ds(pl.multiple_of(block * rows, rows), rows)
    grad_second = grad_a_ref[...].astype(F32) + grad_b_ref[...].astype(F32)
    normed, inv_std = normalize(residual_ref[...])
    grad_residual = go_ref[...].astype(F32) + norm_back(grad_second, normed, inv_std, gain_ref[...])
    grad_residual_ref[...] = grad_residual
    block_ref[...] = block_value(residual_ref, mlp_a_ref, mlp_b_ref, b_proj_ref)
    grad_branch = grad_residual.astype(BF16)
    grad_branch_ref[...] = grad_branch
    grad_branch_t_ref[:, here] = grad_branch.T
    d_norm_ref[0:1, :] += jnp.sum(grad_second * normed, axis=0, keepdims=True)
    d_norm_ref[1:2, :] += jnp.sum(grad_second, axis=0, keepdims=True)
    d_norm_ref[2:3, :] += jnp.sum(grad_branch.astype(F32), axis=0, keepdims=True)
    grad_first_ref[...] = attend_back(
        heads, head_dim, grad_branch, query_ref, key_ref, value_ref, keys_t_ref, att_ref, log_ref,
        w_ref, w_out_ref, d_bias_ref, mixed_ref, grad_keys_ref, grad_values_ref, info_ref[1])
    weight_grads(copies, first_t_ref, grad_branch_t_ref, mixed_ref, att_ref,
                 kept_ref, sent_ref, info_ref[5])


def backward_own_kernel(heads, head_dim, info_ref, grad_branch_ref, grad_first_in_ref, query_ref,
                        key_ref, value_ref, keys_t_ref, att_ref, log_ref, w_ref, w_out_ref,
                        first_t_hbm, grad_branch_t_hbm, grad_first_ref, kept_ref, sent_ref,
                        d_bias_ref, first_t_ref, grad_branch_t_ref, mixed_ref, grad_keys_ref,
                        grad_values_ref, copy_sem):
    copies = (
        pltpu.make_async_copy(first_t_hbm, first_t_ref, copy_sem.at[0]),
        pltpu.make_async_copy(grad_branch_t_hbm, grad_branch_t_ref, copy_sem.at[1]),
    )

    @pl.when(pl.program_id(0) == 0)
    def _():
        for copy in copies:
            copy.start()
        grad_keys_ref[...] = jnp.zeros_like(grad_keys_ref)
        grad_values_ref[...] = jnp.zeros_like(grad_values_ref)
        d_bias_ref[...] = jnp.zeros_like(d_bias_ref)

    grad_first = attend_back(
        heads, head_dim, grad_branch_ref[...], query_ref, key_ref, value_ref, keys_t_ref, att_ref,
        log_ref, w_ref, w_out_ref, d_bias_ref, mixed_ref, grad_keys_ref, grad_values_ref,
        info_ref[1])
    grad_first_ref[...] = (grad_first + grad_first_in_ref[...]).astype(BF16)
    weight_grads(copies, first_t_ref, grad_branch_t_ref, mixed_ref, att_ref,
                 kept_ref, sent_ref, info_ref[5])


def attend_back(heads, head_dim, grad_branch, query_ref, key_ref, value_ref, keys_t_ref, att_ref,
                log_ref, w_ref, w_out_ref, d_bias_ref, mixed_ref, grad_keys_ref, grad_values_ref,
                is_long):
    blocks = key_ref.shape[0] // QUERY_ROWS
    block = blocks - 1 - pl.program_id(0)
    scale = 1.0 / math.sqrt(head_dim)
    start = pl.multiple_of(block * QUERY_ROWS, QUERY_ROWS)
    here = pl.ds(start, QUERY_ROWS)
    grads = dot_nt(grad_branch, w_out_ref[...]).astype(BF16)
    grad_queries = attend_back_block(
        query_ref[...], grads, att_ref[here, :], log_ref[...], key_ref, keys_t_ref, value_ref,
        grad_keys_ref, grad_values_ref, start, block * is_long, heads, head_dim, scale)
    mixed = jnp.concatenate(
        [grad_queries.astype(BF16), (grad_keys_ref[here, :] * scale).astype(BF16),
         grad_values_ref[here, :].astype(BF16)], axis=1
    )
    mixed_ref[here, :] = mixed
    d_bias_ref[...] += jnp.sum(mixed.astype(F32), axis=0, keepdims=True)
    return dot_nn(mixed, w_ref[...])


def weight_grads(copies, first_t_ref, grad_branch_t_ref, mixed_ref, att_ref, kept_ref,
                 sent_ref, mine):
    @pl.when(pl.program_id(0) == pl.num_programs(0) - 1)
    def _():
        for copy in copies:
            copy.wait()
        total = jnp.concatenate(
            [dot_nn(first_t_ref[...], mixed_ref[...]).astype(BF16),
             dot_nn(grad_branch_t_ref[...], att_ref[...]).astype(BF16)], axis=1
        )
        write_split(total, kept_ref, sent_ref, mine)


def last_norm_kernel(info_ref, x_ref, grad_a_ref, grad_b_ref, grad_residual_ref, gain_ref,
                     d_b_proj_ref, d_norm_two_ref, d_b_fc_ref, bias_own_ref, bias_other_ref,
                     grad_in_ref, near_ref, small_ref, sent_ref):
    step = pl.program_id(0)
    local = bias_own_ref.shape[1] // 3

    @pl.when(step == 0)
    def _():
        for target, row, bias_ref in ((small_ref, 0, bias_own_ref), (sent_ref, 1, bias_other_ref)):
            target[...] = jnp.zeros_like(target)
            target[0:1, :] = d_b_proj_ref[...]
            target[1:4, :] = d_norm_two_ref[0:3, :]
            target[6:7, :] = d_b_fc_ref[row : row + 1, :]
            target[7:8, 0 : 2 * local] = jnp.concatenate(
                [bias_ref[:, 0:local], bias_ref[:, 2 * local :]], axis=1
            )

    grad_first = grad_a_ref[...].astype(F32) + grad_b_ref[...].astype(F32)
    normed, inv_std = normalize(x_ref[...].astype(F32))
    grad_in = grad_residual_ref[...] + norm_back(grad_first, normed, inv_std, gain_ref[...])
    grad_low = grad_in.astype(BF16)
    grad_in_ref[...] = grad_low.astype(F32)

    @pl.when((step * x_ref.shape[0]) // info_ref[4] == info_ref[2])
    def _():
        near_ref[...] = grad_low

    gain_sum = jnp.sum(grad_first * normed, axis=0, keepdims=True)
    shift_sum = jnp.sum(grad_first, axis=0, keepdims=True)
    for target in (small_ref, sent_ref):
        target[4:5, :] += gain_sum
        target[5:6, :] += shift_sum


def block_value(residual_ref, mlp_a_ref, mlp_b_ref, bias_ref):
    total = residual_ref[...] + (mlp_a_ref[...].astype(F32) + mlp_b_ref[...].astype(F32))
    return (total + bias_ref[...]).astype(BF16)


def block_half_kernel(info_ref, residual_ref, mlp_a_ref, mlp_b_ref, bias_ref, out_ref):
    out_ref[...] = block_value(residual_ref, mlp_a_ref, mlp_b_ref, bias_ref)


def fill_kernel(info_ref, come_ref, whole_ref, out_ref):
    out_ref[...] = come_ref[...].astype(out_ref.dtype)


def fill_both_kernel(info_ref, near_ref, far_ref, whole_ref, out_ref):
    from_near = (pl.program_id(0) * near_ref.shape[0]) // info_ref[4] == info_ref[2]
    out_ref[...] = jnp.where(from_near, near_ref[...], far_ref[...]).astype(out_ref.dtype)


def row_spec(rows, width, shift=False):
    if shift:
        return pl.BlockSpec((rows, width), lambda step, info: (info[0] + step, 0))
    return pl.BlockSpec((rows, width), lambda step, info: (step, 0))


def back_spec(rows, width, blocks, shift=False):
    if shift:
        return pl.BlockSpec((rows, width), lambda step, info: (info[0] + blocks - 1 - step, 0))
    return pl.BlockSpec((rows, width), lambda step, info: (blocks - 1 - step, 0))


def whole(shape):
    return pl.BlockSpec(shape, lambda step, info: (0,) * len(shape))


def call(kernel, steps, in_specs, out_specs, out_shape, scratch, cost_us, aliases=None):
    return pl.pallas_call(
        kernel,
        grid_spec=pltpu.PrefetchScalarGridSpec(
            num_scalar_prefetch=1,
            grid=(steps,),
            in_specs=in_specs,
            out_specs=out_specs,
            scratch_shapes=scratch,
        ),
        out_shape=out_shape,
        input_output_aliases=aliases or {},
        compiler_params=pltpu.CompilerParams(
            dimension_semantics=("arbitrary",), vmem_limit_bytes=VMEM_BYTES
        ),
        cost_estimate=pl.CostEstimate(
            flops=int(cost_us * 1e9), transcendentals=0, bytes_accessed=int(cost_us * 3e6)
        ),
    )


def struct(shape, dtype):
    return jax.ShapeDtypeStruct(shape, dtype)


def exchange(value, axis_name, size, bit):
    return lax.ppermute(value, axis_name, [(i, i ^ bit) for i in range(size)])


def after(value, earlier):
    return lax.optimization_barrier((value, earlier))[0]


def make_body(dp_size, tensor_size):
    def body(hidden_in, doc_ids, ln1_gain, ln1_bias, w_qkv, b_qv, w_out, b_out, ln2_gain, ln2_bias,
             w_fc, b_fc, w_proj, b_proj, grad_out):
        row_count, width = hidden_in.shape
        heads, head_dim = w_qkv.shape[2:]
        local = heads * head_dim
        hidden = w_fc.shape[1]
        rows = row_count // 2
        blocks = rows // QUERY_ROWS
        half = rows // 2
        place = lax.axis_index(TENSOR)
        bits = dp_size.bit_length() - 1
        position = lax.axis_index(DP)
        share = width // dp_size
        first_bit = next(bit for bit in range(bits) if (share << bit) % 16 == 0)
        second_bit = min(first_bit + 1, bits - 1)
        upper = place // 2
        core = place % 2
        is_long = (doc_ids[SHORT_LEN] == doc_ids[0]).astype(jnp.int32)
        info = jnp.stack(
            [upper * blocks, is_long, core, (1 - upper) * blocks, half,
             (position >> first_bit) & 1, (position >> second_bit) & 1]
        ).astype(jnp.int32)

        def core_swap(value):
            return exchange(value, TENSOR, tensor_size, 1)

        def pair_swap(value):
            return exchange(value, TENSOR, tensor_size, 2)

        qkv_own = w_qkv.transpose(1, 2, 3, 0).reshape(3 * local, width)
        out_own = w_out.reshape(local, width)
        bias_own = b_qv.reshape(2, local)
        small_other = pair_swap(
            jnp.concatenate([b_qv.reshape(1, 2 * local), b_fc.reshape(1, hidden)], axis=1)
        )

        def my_piece(matrix):
            rows_each = matrix.shape[0] // dp_size
            return lax.dynamic_slice_in_dim(matrix, position * rows_each, rows_each, axis=0)[None]

        def widen(kept, come, bit):
            mine = (position >> bit) & 1
            return tuple(
                jnp.where(mine == 0, jnp.stack([a, b], 1), jnp.stack([b, a], 1)).reshape(
                    (2 * a.shape[0],) + a.shape[1:]
                )
                for a, b in zip(kept, come)
            )

        def dp_swap(values, bit):
            return tuple(exchange(value, DP, dp_size, 1 << bit) for value in values)

        parts = tuple(
            pair_swap(my_piece(matrix)) for matrix in (w_proj, w_fc[width // 2 :])
        )
        out_other = pair_swap(out_own)
        qkv_other = pair_swap(qkv_own)
        fc_top = pair_swap(w_fc[: width // 2])
        come = dp_swap(parts, bits - 1)
        come, hidden_in = lax.optimization_barrier((come, hidden_in))
        parts = widen(parts, come, bits - 1)
        come = dp_swap(parts, bits - 2)

        first_spec = row_spec(QUERY_ROWS, width)
        turned_spec = pl.BlockSpec((local, QUERY_ROWS), lambda step, info: (0, step))
        att_spec = row_spec(QUERY_ROWS, local)
        log_spec = pl.BlockSpec((8, QUERY_ROWS), lambda step, info: (0, step))
        mix_specs = [att_spec] * 3 + [turned_spec]
        mix_structs = [struct((rows, local), BF16)] * 3 + [struct((local, rows), BF16)]
        attend_scratch = [pltpu.VMEM((rows, local), BF16), pltpu.VMEM((local, rows), BF16)]

        def forward_own(*refs):
            forward_own_kernel(heads, head_dim, *refs)

        def forward_other(*refs):
            forward_other_kernel(heads, head_dim, *refs)

        first_in, first_t, *mix_own, att_own, log_own = call(
            forward_own,
            blocks,
            [row_spec(QUERY_ROWS, width, True), whole((width,)), whole((width,)),
             whole((3 * local, width)), whole((2, local))],
            [first_spec, pl.BlockSpec((width, QUERY_ROWS), lambda step, info: (0, step))]
            + mix_specs + [att_spec, log_spec],
            [struct((rows, width), BF16), struct((width, rows), BF16)] + mix_structs
            + [struct((rows, local), BF16), struct((8, rows), F32)],
            attend_scratch,
            11,
        )(info, hidden_in, ln1_gain, ln1_bias, qkv_own, bias_own)
        come, small_other = after((come, small_other), first_in)
        parts = widen(parts, come, bits - 2)
        for bit in reversed(range(bits - 2)):
            come = dp_swap(parts, bit)
            if bit:
                first_in = after(first_in, come)
            parts = widen(parts, come, bit)
        proj_other = parts[0].reshape(hidden, width)
        fc_low = parts[1].reshape(width // 2, hidden)
        bias_other = small_other[:, : 2 * local].reshape(2, local)
        b_fc_both = jnp.concatenate([b_fc.reshape(1, hidden), small_other[:, 2 * local :]], axis=0)
        *mix_other, att_other, log_other, branch = call(
            forward_other,
            blocks,
            [first_spec, whole((3 * local, width)), whole((2, local)), att_spec,
             whole((local, width)), whole((local, width))],
            mix_specs + [att_spec, log_spec, first_spec],
            mix_structs + [struct((rows, local), BF16), struct((8, rows), F32),
                           struct((rows, width), BF16)],
            attend_scratch,
            12,
        )(info, first_in, qkv_other, bias_other, att_own, out_own, out_other)
        branch_swapped = core_swap(branch)

        def split_shape(bit, lead=()):
            runs = dp_size >> bit
            return lead + (runs // 2, share << bit, width)

        fc_shape = split_shape(first_bit, (2,))
        proj_shape = split_shape(second_bit, (2,))
        att_shape = split_shape(first_bit)
        (residual, mlp, grad_second, fc_kept, fc_sent, proj_kept, proj_sent, d_b_fc,
         d_b_proj) = call(
            mlp_kernel,
            blocks,
            [row_spec(QUERY_ROWS, width, True), first_spec, first_spec, whole((width,)),
             whole((width,)), whole((width,)), row_spec(QUERY_ROWS, width, True),
             whole((width, hidden)), whole((width // 2, hidden)), whole((width // 2, hidden)),
             whole((hidden, width)), whole((hidden, width)), whole((2, hidden))],
            [first_spec, first_spec, first_spec] + [whole(fc_shape)] * 2 + [whole(proj_shape)] * 2
            + [whole((2, hidden)), whole((1, width))],
            [struct((rows, width), F32), struct((rows, width), BF16), struct((rows, width), BF16),
             struct(fc_shape, BF16), struct(fc_shape, BF16), struct(proj_shape, BF16),
             struct(proj_shape, BF16),
             struct((2, hidden), F32), struct((1, width), F32)],
            [pltpu.VMEM((width, rows), BF16)] * 2 + [pltpu.VMEM((rows, hidden), BF16)] * 4,
            28,
        )(info, hidden_in, branch, branch_swapped, b_out, ln2_gain,
          ln2_bias, grad_out, w_fc, fc_top, fc_low, w_proj, proj_other, b_fc_both)
        grad_swapped = core_swap(grad_second)
        mlp_swapped = core_swap(mlp)

        half_spec = pl.BlockSpec(
            (QUERY_ROWS, width), lambda step, info: (info[2] * (half // QUERY_ROWS) + step, 0)
        )
        block_half = call(
            block_half_kernel,
            half // QUERY_ROWS,
            [half_spec, half_spec, half_spec, whole((width,))],
            first_spec,
            struct((half, width), BF16),
            [],
            3,
        )(info, residual, mlp, mlp_swapped, b_proj)
        block_near = pair_swap(block_half)

        back_rows = back_spec(QUERY_ROWS, width, blocks)
        back_att = back_spec(QUERY_ROWS, local, blocks)
        back_log = pl.BlockSpec((8, QUERY_ROWS), lambda step, info: (0, blocks - 1 - step))
        back_scratch = [
            pltpu.VMEM((rows, 3 * local), BF16),
            pltpu.VMEM((rows, local), F32),
            pltpu.VMEM((rows, local), F32),
            pltpu.SemaphoreType.DMA((2,)),
        ]
        turned_scratch = pltpu.VMEM((width, rows), BF16)
        back_mix = [back_att, whole((rows, local)), whole((rows, local)), whole((local, rows)),
                    whole((rows, local)), back_log, whole((3 * local, width)),
                    whole((local, width))]
        in_place = pl.BlockSpec(memory_space=pl.ANY)

        def backward_other(*refs):
            backward_other_kernel(heads, head_dim, *refs)

        def backward_own(*refs):
            backward_own_kernel(heads, head_dim, *refs)

        (grad_residual, grad_branch, grad_branch_t, grad_first_other, far_kept, far_sent, d_bias_other,
         d_norm_two, block_out) = call(
            backward_other,
            blocks,
            [back_rows, back_rows, back_rows, back_spec(QUERY_ROWS, width, blocks, True),
             whole((width,)), back_rows, back_rows, whole((width,))] + back_mix + [in_place],
            [back_rows, back_rows, whole((width, rows)), back_rows, whole(att_shape), whole(att_shape),
             whole((1, 3 * local)), whole((8, width)),
             back_spec(QUERY_ROWS, width, blocks, True)],
            [struct((rows, width), F32), struct((rows, width), BF16),
             struct((width, rows), BF16), struct((rows, width), F32),
             struct(att_shape, BF16), struct(att_shape, BF16), struct((1, 3 * local), F32),
             struct((8, width), F32), struct((row_count, width), BF16)],
            [turned_scratch] + back_scratch,
            21,
        )(info, grad_second, grad_swapped, residual, grad_out, ln2_gain, mlp, mlp_swapped, b_proj,
          *mix_other, att_other, log_other, qkv_other, out_other, first_t)
        grad_first, near_kept, near_sent, d_bias_own = call(
            backward_own,
            blocks,
            [back_rows, back_rows] + back_mix + [in_place, in_place],
            [back_rows, whole(att_shape), whole(att_shape), whole((1, 3 * local))],
            [struct((rows, width), BF16), struct(att_shape, BF16), struct(att_shape, BF16),
             struct((1, 3 * local), F32)],
            [turned_scratch, turned_scratch] + back_scratch,
            17,
        )(info, grad_branch, grad_first_other, *mix_own, att_own, log_own, qkv_own, out_own,
          first_t, grad_branch_t)
        first_swapped = core_swap(grad_first)
        quarter = half // QUERY_ROWS
        small_spec = whole((8, width))
        grad_in, grad_half, small, small_sent = call(
            last_norm_kernel,
            blocks,
            [row_spec(QUERY_ROWS, width, True), first_spec, first_spec, first_spec,
             whole((width,)), whole((1, width)), small_spec, whole((2, hidden)),
             whole((1, 3 * local)), whole((1, 3 * local))],
            [row_spec(QUERY_ROWS, width, True),
             pl.BlockSpec((QUERY_ROWS, width), lambda step, info: (
                jnp.clip(step - quarter * info[2], 0, quarter - 1), 0)),
             small_spec, small_spec],
            [struct((row_count, width), F32), struct((half, width), BF16),
             struct((8, width), F32), struct((8, width), F32)],
            [],
            7,
        )(info, hidden_in, grad_first, first_swapped, grad_residual, ln1_gain, d_b_proj,
          d_norm_two, d_b_fc, d_bias_own, d_bias_other)
        small_come = pair_swap(small_sent)
        grad_near = pair_swap(grad_half)

        def quarter_spec(part):
            def index(step, info):
                first = jnp.where(part == 0, info[2], 1 - info[2]) * quarter
                return jnp.clip(step - first, 0, quarter - 1), 0

            return pl.BlockSpec((QUERY_ROWS, width), index)

        def fill_both(target, near, far):
            return call(
                fill_both_kernel,
                blocks,
                [quarter_spec(0), quarter_spec(1), pl.BlockSpec(memory_space=pl.ANY)],
                pl.BlockSpec((QUERY_ROWS, width), lambda step, info: (info[3] + step, 0)),
                struct(target.shape, target.dtype),
                [],
                3,
                {3: 0},
            )(info, near, far, target)

        block_far = core_swap(block_near)
        block_near, block_far = after((block_near, block_far), grad_half)
        block_out = fill_both(block_out, block_near, block_far)
        grad_far = core_swap(grad_near)

        def fill(target, come, part):
            def index(step, info):
                first = jnp.where(part == 0, info[2], 1 - info[2]) * quarter
                return info[3] + first + step, 0

            return call(
                fill_kernel,
                quarter,
                [first_spec, pl.BlockSpec(memory_space=pl.ANY)],
                pl.BlockSpec((QUERY_ROWS, width), index),
                struct(target.shape, target.dtype),
                [],
                2,
                {2: 0},
            )(info, come, target)

        grad_in = fill(grad_in, grad_near, 0)
        grad_in = fill(grad_in, grad_far, 1)

        def pick(value, axis, which):
            return lax.dynamic_index_in_dim(value, which, axis, keepdims=False)

        def parted(value, lead=()):
            return value.reshape(lead + (2,) * (bits - 1) + (share, width))

        def add(kept, received):
            return kept.astype(F32) + received.astype(F32)

        def others(bit):
            return [b for b in range(bits) if b != bit]

        def stages(value, left):
            for number, bit in enumerate(left):
                above = len([b for b in left[number:] if b > bit])
                mine = (position >> bit) & 1
                received = exchange(
                    pick(value, above, 1 - mine).astype(BF16), DP, dp_size, 1 << bit
                )
                if number == 0:
                    received = after(received, grad_half)
                value = add(pick(value, above, mine), received)
            return value

        got_fc = exchange(fc_sent, DP, dp_size, 1 << first_bit)
        got_proj = exchange(proj_sent, DP, dp_size, 1 << second_bit)
        got_far = exchange(far_sent, DP, dp_size, 1 << first_bit)
        got_fc, got_proj = after((got_fc, got_proj), grad_branch)
        half_fc = add(fc_kept[1], got_fc[1])
        half_proj = add(proj_kept[1], got_proj[1])
        come_fc = pair_swap(half_fc.astype(BF16))
        come_proj = pair_swap(half_proj.astype(BF16))
        got_near = exchange(near_sent, DP, dp_size, 1 << first_bit)
        got_far = after(got_far, grad_first)
        come_far = pair_swap(add(far_kept, got_far).astype(BF16))
        come_fc, got_fc = after((come_fc, got_fc), grad_first)
        come_proj, got_proj, come_far, got_near = after(
            (come_proj, got_proj, come_far, got_near), grad_half
        )
        fc_share = stages(parted(add(add(fc_kept[0], got_fc[0]), come_fc)), others(first_bit))
        proj_share = stages(parted(add(add(proj_kept[0], got_proj[0]), come_proj)), others(second_bit))
        att_half = parted(add(add(near_kept, got_near), come_far))
        att_share = stages(att_half, others(first_bit))
        small = small + small_come
        for bit in range(bits):
            small_come = exchange(small, DP, dp_size, 1 << bit)
            small = small + small_come
        shares = lax.dynamic_index_in_dim(
            small[0:6].reshape(6, dp_size, share), position, 1, keepdims=False
        )
        d_b_proj_share, d_gain_two, d_shift_two, d_b_out, d_gain_one, d_shift_one = (
            shares[i] for i in range(6)
        )
        fc_rows, fc_columns = b_fc.shape
        d_b_fc_share = lax.dynamic_slice_in_dim(
            small[6].reshape(fc_rows, fc_columns), position * (fc_columns // dp_size),
            fc_columns // dp_size, axis=1,
        )
        d_b_qv_share = lax.dynamic_slice_in_dim(
            small[7, : 2 * local].reshape(2, heads, head_dim), position * (head_dim // dp_size),
            head_dim // dp_size, axis=2,
        )
        att_turned = att_share.T
        d_w_qkv = att_turned[: 3 * local].reshape(3, heads, head_dim, share).transpose(3, 0, 1, 2)
        d_w_out = att_turned[3 * local :].reshape(heads, head_dim, share)
        return (block_out, grad_in, d_gain_one, d_shift_one, d_w_qkv, d_b_qv_share, d_w_out,
                d_b_out, d_gain_two, d_shift_two, fc_share, d_b_fc_share, proj_share.T,
                d_b_proj_share)

    return body


def solution(mesh):
    in_specs = (
        P(DP, None),
        P(DP),
        P(),
        P(),
        P(None, None, TENSOR, None),
        P(None, TENSOR, None),
        P(TENSOR, None, None),
        P(),
        P(),
        P(),
        P(None, TENSOR),
        P(TENSOR, None),
        P(TENSOR, None),
        P(),
        P(DP, None),
    )
    out_specs = (
        P(DP, None),
        P(DP, None),
        P(DP),
        P(DP),
        P(DP, None, TENSOR, None),
        P(None, TENSOR, DP),
        P(TENSOR, None, DP),
        P(DP),
        P(DP),
        P(DP),
        P(DP, TENSOR),
        P(TENSOR, DP),
        P(TENSOR, DP),
        P(DP),
    )
    inner = make_body(mesh.shape[DP], mesh.shape[TENSOR])

    return jax.shard_map(inner, mesh=mesh, in_specs=in_specs, out_specs=out_specs, check_vma=False)
```
